32 devices in a mesh: slot: 4 (over y, x), seq: 2 (over core), blk: 4 (over z).
Axes of the slice: x: 2, y: 2, z: 4, core: 2. Of those that a mesh axis runs over, the one named last changes fastest.
Arguments:
- tokens: bfloat16 [4, 1024, 2048], P('slot', ('blk', 'seq')), may hold values from -6 to 6
- out_grad: bfloat16 [4, 1024, 2048], P('slot', ('blk', 'seq')), may hold values from -6 to 6
- lengths: int32 [4], P('slot'), may hold values from 256 to 1024, as said below
- attn_gain: bfloat16 [2048], P(('slot', 'blk')), may hold values from 0.099609375 to 1.8984375
- w_query: bfloat16 [2048, 2048], P(('slot', 'blk'), 'seq'), may hold values from -0.125 to 0.125
- w_key: bfloat16 [2048, 2048], P(('slot', 'blk'), 'seq'), may hold values from -0.125 to 0.125
- w_value: bfloat16 [2048, 2048], P(('slot', 'blk'), 'seq'), may hold values from -0.125 to 0.125
- output_weight: bfloat16 [2048, 2048], P(('slot', 'blk'), 'seq'), may hold values from -1 to 1
- mlp_gain: bfloat16 [2048], P(('slot', 'blk')), may hold values from 0.099609375 to 1.8984375
- gate_weight: bfloat16 [2048, 8192], P(('slot', 'blk'), 'seq'), may hold values from -0.125 to 0.125
- up_weight: bfloat16 [2048, 8192], P(('slot', 'blk'), 'seq'), may hold values from -0.125 to 0.125
- down_weight: bfloat16 [2048, 8192], P(('slot', 'blk'), 'seq'), may hold values from -0.0625 to 0.0625
Outputs:
- layer_out: bfloat16 [4, 1024, 2048], P('slot', ('blk', 'seq'))
- grad_tokens: float32 [4, 1024, 2048], P('slot', ('blk', 'seq'))
- grad_attn_gain: float32 [2048], P(('slot', 'blk'))
- grad_w_query: float32 [2048, 2048], P(('slot', 'blk'), 'seq')
- grad_w_key: float32 [2048, 2048], P(('slot', 'blk'), 'seq')
- grad_w_value: float32 [2048, 2048], P(('slot', 'blk'), 'seq')
- grad_w_output: float32 [2048, 2048], P(('slot', 'blk'), 'seq')
- grad_mlp_gain: float32 [2048], P(('slot', 'blk'))
- grad_w_gate: float32 [2048, 8192], P(('slot', 'blk'), 'seq')
- grad_w_up: float32 [2048, 8192], P(('slot', 'blk'), 'seq')
- grad_w_down: float32 [2048, 8192], P(('slot', 'blk'), 'seq')
The draws below stay inside these ranges and needn't reach their ends.
Inputs may be any that keep to these rules, and one draw needn't show every extreme that they name: `lengths`: the valid tokens of a slot are its first ones; at least one slot is full.
All inputs are finite; a program needn't handle non-finite values.
Results may differ from the reference program's by a relative error of at most 0.025.
Values may be sent and summed in bfloat16 or wider, within the bound.
No kernel may reach another device: no remote copies, remote signals or barrier semaphores. Data moves between devices by JAX's collectives and lax.ppermute only.
A program may use at most 192 MiB of HBM per device.

```python
import jax
import jax.numpy as jnp
from jax import lax

D = 2048
HEADS = 32
HEAD_DIM = 64
FF = 8192
SLOTS = 4
SLOT_LEN = 1024


def draw_lengths(key, part):
    first_key, second_key = jax.random.split(key)
    drawn = jax.random.randint(first_key, (SLOTS,), SLOT_LEN // 4, SLOT_LEN + 1)
    full_slot = jax.random.randint(second_key, (), 0, SLOTS)
    return jnp.where(jnp.arange(SLOTS) == full_slot, SLOT_LEN, drawn).astype(jnp.int32)


def level_of(key, dims, shards, least, largest):
    def one(axis_at, blocks):
        steps = jax.random.uniform(jax.random.fold_in(jax.random.fold_in(key, 6), axis_at), (blocks,), jnp.float32, least / len(shards), largest / len(shards))
        return jnp.repeat(jnp.exp(steps), dims[axis_at] // blocks).reshape((-1,) + (1,) * (len(dims) - axis_at - 1))

    level = one(*shards[0])
    for cut in shards[1:]:
        level = level * one(*cut)
    return level


def scatter_about(rng, shape, width, bound, shards=(), kind=jnp.bfloat16):
    entries = jax.random.normal(rng, shape, jnp.float32) * width
    if len(shards) > 0:
        entries = level_of(rng, shape, shards, -0.22, 0.18) * entries
    return jnp.clip(entries, min=-bound, max=bound).astype(kind)


def setup_inputs(seed: int = 0) -> dict:
    streams_of = jax.random.split(jax.random.key(seed), 13)
    return {
        "tokens": scatter_about(streams_of[0], (SLOTS, SLOT_LEN, D), 1.0, 6.0, ((0, 4), (1, 8))),
        "out_grad": scatter_about(streams_of[1], (SLOTS, SLOT_LEN, D), 1.0, 6.0, ((0, 4), (1, 8))),
        "lengths": draw_lengths(jax.random.fold_in(streams_of[12], 71), 0),
        "attn_gain": jnp.clip(1.0 + 0.18 * jax.random.normal(streams_of[3], (D,), jnp.float32), 0.099609375, 1.8984375).astype(jnp.bfloat16),
        "w_query": scatter_about(streams_of[4], (D, D), D ** -0.5, 0.125, ((0, 16), (1, 2))),
        "w_key": scatter_about(streams_of[5], (D, D), D ** -0.5, 0.125, ((0, 16), (1, 2))),
        "w_value": scatter_about(streams_of[6], (D, D), D ** -0.5, 0.125, ((0, 16), (1, 2))),
        "output_weight": scatter_about(streams_of[7], (D, D), (D // 64) ** -0.5, 1.0, ((0, 16), (1, 2))),
        "mlp_gain": jnp.clip(1.0 + 0.18 * jax.random.normal(streams_of[8], (D,), jnp.float32), 0.099609375, 1.8984375).astype(jnp.bfloat16),
        "gate_weight": scatter_about(streams_of[9], (D, FF), D ** -0.5, 0.125, ((0, 16), (1, 2))),
        "up_weight": scatter_about(streams_of[10], (D, FF), D ** -0.5, 0.125, ((0, 16), (1, 2))),
        "down_weight": scatter_about(streams_of[11], (D, FF), FF ** -0.5, 0.0625, ((0, 16), (1, 2))),
    }


EPSILON = 1e-05
ROPE_BASE = 130000.0

@jax.custom_vjp
def low(v):
    return lax.optimization_barrier(v.astype(jnp.bfloat16)).astype(jnp.float32)

@jax.custom_vjp
def reduced_backward(v):
    return v

def low_keep(v):
    return (low(v), None)

def low_pass(kept, grad):
    return (grad,)

def back_keep(v):
    return (v, None)

def back_low(kept, grad):
    return (low(grad),)
low.defvjp(low_keep, low_pass)
reduced_backward.defvjp(back_keep, back_low)

def rope_tables(positions, head_size):
    half_size = head_size // 2
    frequency = ROPE_BASE ** (-jnp.arange(half_size, dtype=jnp.float32) * 2.0 / head_size)
    angles = positions.astype(jnp.float32)[:, None] * frequency[None, :]
    return (jnp.cos(angles), jnp.sin(angles))

def rotate(vectors, cosine, sine_tab):
    half_size = vectors.shape[-1] // 2
    first_half = vectors[..., :half_size]
    second_half = vectors[..., half_size:]
    cos_wide = cosine[:, None, :]
    sin_wide = sine_tab[:, None, :]
    return jnp.concatenate([first_half * cos_wide - second_half * sin_wide, second_half * cos_wide + first_half * sin_wide], axis=-1)

def rms_norm(input_rows_packed, gain_row):
    return input_rows_packed * lax.rsqrt(lax.optimization_barrier(jnp.mean(input_rows_packed * input_rows_packed, axis=-1, keepdims=True)) + EPSILON) * gain_row

def head_attention(queries, key_rows, val_rows, length):
    seq_len = queries.shape[0]
    positions = jnp.arange(seq_len, dtype=jnp.int32)
    allowed = (positions[None, :] <= positions[:, None]) & (positions[None, :] < length)
    scores = jnp.dot(queries, key_rows.T, precision=lax.Precision.HIGHEST) * HEAD_DIM ** (-0.5)
    scores = reduced_backward(jnp.where(allowed, scores, -1e+30))
    row_max = lax.optimization_barrier(jnp.max(scores, axis=1, keepdims=True))
    exponent = jnp.exp(scores - row_max)
    softmax_w = exponent / lax.optimization_barrier(jnp.sum(exponent, axis=1, keepdims=True))
    return jnp.dot(low(softmax_w), val_rows, precision=lax.Precision.HIGHEST)

def layer_forward(input_rows_packed, attn_gain, w_query, w_key, w_value, output_weight, mlp_gain, gate_weight, up_weight, down_weight, lengths):
    slots, seq_len, model_width = input_rows_packed.shape
    highest_precision = lax.Precision.HIGHEST
    cosine, sine_tab = rope_tables(jnp.arange(seq_len, dtype=jnp.int32), HEAD_DIM)
    hidden_after_attention = low(rms_norm(input_rows_packed, attn_gain))

    def project(weight_tensor):
        return jnp.einsum('fnr,rq->fnq', hidden_after_attention, weight_tensor, precision=highest_precision)
    head_shape = (slots, seq_len, HEADS, HEAD_DIM)
    queries = low(reduced_backward(rotate(reduced_backward(project(w_query)).reshape(head_shape), cosine, sine_tab)))
    key_rows = low(reduced_backward(rotate(reduced_backward(project(w_key)).reshape(head_shape), cosine, sine_tab)))
    val_rows = low(reduced_backward(project(w_value))).reshape(head_shape)

    def by_heads(array):
        return jnp.transpose(array, (0, 2, 1, 3)).reshape(slots * HEADS, seq_len, HEAD_DIM)
    head_lengths = jnp.repeat(lengths, HEADS)
    checked = jax.checkpoint(head_attention)
    attention_mixed = lax.map(lambda items: checked(items[0], items[1], items[2], items[3]), (by_heads(queries), by_heads(key_rows), by_heads(val_rows), head_lengths))
    attention_mixed = jnp.transpose(attention_mixed.reshape(slots, HEADS, seq_len, HEAD_DIM), (0, 2, 1, 3)).reshape(slots, seq_len, model_width)
    attention_mixed = low(reduced_backward(attention_mixed))
    residual_stream = input_rows_packed + reduced_backward(jnp.einsum('xko,to->xkt', attention_mixed, output_weight, precision=highest_precision))
    hidden_after_feedforward = low(rms_norm(residual_stream, mlp_gain))
    gate_logits = reduced_backward(jnp.einsum('gew,wj->gej', hidden_after_feedforward, gate_weight, precision=highest_precision))
    up_logits = reduced_backward(jnp.einsum('gew,wj->gej', hidden_after_feedforward, up_weight, precision=highest_precision))
    swiglu_product = low(gate_logits * jax.nn.sigmoid(gate_logits) * up_logits)
    feedforward_output = reduced_backward(jnp.einsum('jie,ce->jic', swiglu_product, down_weight, precision=highest_precision))
    live_rows = (jnp.arange(seq_len, dtype=jnp.int32)[None, :] < lengths[:, None])[:, :, None]
    return jnp.where(live_rows, residual_stream + feedforward_output, 0.0)

def reference(tokens, out_grad, lengths, attn_gain, w_query, w_key, w_value, output_weight, mlp_gain, gate_weight, up_weight, down_weight):

    def forward(input_rows_packed, gain_a, weight_q, weight_k, weight_v, weight_o, gain_m, weight_g, weight_u, weight_d):
        return layer_forward(input_rows_packed, gain_a, weight_q, weight_k, weight_v, weight_o, gain_m, weight_g, weight_u, weight_d, lengths)
    floats = [array.astype(jnp.float32) for array in (tokens, attn_gain, w_query, w_key, w_value, output_weight, mlp_gain, gate_weight, up_weight, down_weight)]
    result, pullback = jax.vjp(forward, floats[0], floats[1], floats[2], floats[3], floats[4], floats[5], floats[6], floats[7], floats[8], floats[9])
    grads = pullback(out_grad.astype(jnp.float32))
    return (result.astype(jnp.bfloat16), grads[0], grads[1], grads[2], grads[3], grads[4], grads[5], grads[6], grads[7], grads[8], grads[9])
```

```python
from functools import partial

import jax
import jax.numpy as jnp
from jax import lax
from jax.experimental import pallas as pl
from jax.experimental.pallas import tpu as pltpu
from jax.sharding import PartitionSpec as P

HEADS = 32
HEAD_DIM = 64
EPSILON = 1e-05
ROPE_BASE = 130000.0
LOW = jnp.bfloat16
WIDE = jnp.float32


def turn(value, axis, by):
    count = lax.axis_size(axis)
    return lax.ppermute(value, axis, [(i, (i + by) % count) for i in range(count)])


def swap(value, axis, mask):
    count = lax.axis_size(axis)
    return lax.ppermute(value, axis, [(i, i ^ mask) for i in range(count)])


def after(value, *others):
    return lax.optimization_barrier((value, *others))[0]


def matmul(left, right):
    return jnp.dot(left, right, preferred_element_type=WIDE)


def over_rows(left, right):
    return lax.dot_general(left, right, (((0,), (0,)), ((), ())), preferred_element_type=WIDE)


def over_cols(left, right):
    return lax.dot_general(left, right, (((1,), (1,)), ((), ())), preferred_element_type=WIDE)


def slot_order(array):
    rank = lax.axis_index("slot")
    count = lax.axis_size("slot")
    parts = jnp.split(array, count, axis=-1)
    bit = 1
    while bit < count:
        flip = (rank & bit) != 0
        parts = [jnp.where(flip, parts[i ^ bit], parts[i]) for i in range(count)]
        bit *= 2
    return jnp.concatenate(parts, axis=-1)


def seq_gather(rows):
    count = lax.axis_size("seq")
    held = [rows]
    bit = 1
    while bit < count:
        held = held + [swap(part, "seq", bit) for part in held]
        bit *= 2
    return held


def seq_reduce(parts):
    bit = lax.axis_size("seq") // 2
    while bit >= 1:
        sent = [swap(part.astype(LOW), "seq", bit) for part in parts[bit:]]
        parts = [a.astype(WIDE) + b.astype(WIDE) for a, b in zip(parts[:bit], sent)]
        bit //= 2
    return parts[0]


def gather_rows(rows):
    moving = rows
    blocks = seq_gather(moving)
    for _ in range(lax.axis_size("blk") - 1):
        moving = turn(moving, "blk", 1)
        blocks = blocks + seq_gather(moving)
    return jnp.concatenate(blocks, axis=0)


def scatter_rows(terms):
    blks, seqs = lax.axis_size("blk"), lax.axis_size("seq")
    size = terms.shape[0] // (blks * seqs)

    def block(k):
        first = k * seqs
        return seq_reduce([terms[(first + m) * size : (first + m + 1) * size] for m in range(seqs)])

    moving = block(1 % blks)
    for step in range(1, blks):
        here = block((1 + step) % blks)
        moving = turn(moving.astype(LOW), "blk", 1).astype(WIDE) + here
    return moving


def columns_of(array, owner, parts):
    width = array.shape[1] // parts
    return lax.dynamic_slice(array, (0, owner * width), (array.shape[0], width))


def blk_weights(arrays):
    blks, rank = lax.axis_size("blk"), lax.axis_index("blk")

    def piece(owner):
        return jnp.concatenate([columns_of(a, owner, blks) for a in arrays], axis=1)

    own = piece(rank)
    rows = own.shape[0]
    full = jnp.zeros((blks * rows, own.shape[1]), own.dtype)
    full = lax.dynamic_update_slice(full, own, (rank * rows, 0))
    for k in range(1, blks):
        got = turn(piece((rank + k) % blks), "blk", k)
        full = lax.dynamic_update_slice(full, got, ((rank - k) % blks * rows, 0))
    return full


def slot_weights(own, first):
    near = [swap(own, "slot", 1), swap(own, "slot", 2)]
    far = swap(near[first - 1], "slot", 3 - first)
    return jnp.concatenate([own, near[0], near[1], far], axis=0)


def slot_sum(terms, first):
    far = swap(terms[3].astype(LOW), "slot", first)
    second = 3 - first
    relay = (terms[second].astype(WIDE) + far.astype(WIDE)).astype(LOW)
    one = swap(relay, "slot", second)
    two = swap(terms[first].astype(LOW), "slot", first)
    return terms[0].astype(WIDE) + one.astype(WIDE) + two.astype(WIDE)


def blk_grads(summed, widths):
    blks, rank = lax.axis_size("blk"), lax.axis_index("blk")
    rows = summed.shape[0] // blks
    low = summed.astype(LOW)

    def piece(owner):
        return lax.dynamic_slice(low, (owner * rows, 0), (rows, low.shape[1]))

    got = [(rank, piece(rank))]
    for k in range(1, blks):
        got.append(((rank - k) % blks, turn(piece((rank + k) % blks), "blk", k)))
    outs, at = [], 0
    for width in widths:
        out = jnp.zeros((rows, blks * width), WIDE)
        for owner, part in got:
            out = lax.dynamic_update_slice(out, part[:, at : at + width].astype(WIDE), (0, owner * width))
        outs.append(out)
        at += width
    return outs


def norm_rows(rows, gain_row):
    inverse = lax.rsqrt(jnp.mean(rows * rows, axis=-1, keepdims=True) + EPSILON)
    return rows * inverse * gain_row, inverse


def norm_back(rows, inverse, gain_row, upstream):
    scaled = upstream * gain_row
    normed = rows * inverse
    grad_in = inverse * (scaled - normed * jnp.mean(scaled * normed, axis=-1, keepdims=True))
    return grad_in, jnp.sum(upstream * normed, axis=0)


def row_positions(index, blk_rank, seq_rank, blks, seqs, size):
    sub = index // size
    k, m = sub // seqs, sub % seqs
    return ((blk_rank - k + blks) % blks * seqs + (seq_rank ^ m)) * size + index % size


def partner(vectors, lanes):
    half = HEAD_DIM // 2
    width = vectors.shape[1]
    if width % 128 == 0:
        ahead = pltpu.roll(vectors, width - half, 1)
        behind = pltpu.roll(vectors, half, 1)
        return jnp.where(lanes % HEAD_DIM < half, ahead, behind)
    parts = []
    for head in range(width // HEAD_DIM):
        first = head * HEAD_DIM
        parts += [vectors[:, first + half : first + HEAD_DIM], vectors[:, first : first + half]]
    return jnp.concatenate(parts, axis=1)


def attend_kernel(dims, place_ref, qkv_ref, kv_ref, cos_ref, sin_ref, allcos_ref, allsin_ref, q_ref, k_ref, v_ref, out_ref, lse_ref):
    heads, width, rows, total, blks, seqs, size, scale = dims
    step = pl.program_id(0)
    lanes = lax.broadcasted_iota(jnp.int32, (1, width), 1)

    @pl.when(step == 0)
    def _():
        pre = kv_ref[:, width : 2 * width]
        k_ref[...] = (pre * allcos_ref[...] + partner(pre, lanes) * allsin_ref[...]).astype(LOW)
        v_ref[...] = kv_ref[:, 2 * width :].astype(LOW)

    pre = qkv_ref[:, :width]
    queries = (pre * cos_ref[...] + partner(pre, lanes) * sin_ref[...]).astype(LOW)
    q_ref[...] = queries
    blk_rank, seq_rank, length = place_ref[0], place_ref[1], place_ref[2]
    q_index = step * rows + lax.broadcasted_iota(jnp.int32, (rows, 1), 0)
    k_index = lax.broadcasted_iota(jnp.int32, (1, total), 1)
    q_pos = row_positions(q_index, blk_rank, seq_rank, blks, seqs, size)
    k_pos = row_positions(k_index, blk_rank, seq_rank, blks, seqs, size)
    k_pos = jnp.where(k_pos < length, k_pos, jnp.int32(1 << 30))
    allowed = k_pos <= q_pos
    lse_lanes = lax.broadcasted_iota(jnp.int32, (1, 128), 1)

    def one_head(head, carried):
        out, lse = carried
        mine = lanes // HEAD_DIM == head
        picked = jnp.where(mine, queries.astype(WIDE) * scale, 0.0).astype(LOW)
        scores = over_cols(picked, k_ref[...])
        scores = jnp.where(allowed, scores, -1e30)
        top = jnp.max(scores, axis=1, keepdims=True)
        weights = jnp.exp(scores - top)
        total_weight = jnp.sum(weights, axis=1, keepdims=True)
        mixed = matmul(weights.astype(LOW), v_ref[...]) / total_weight
        out = jnp.where(mine, mixed, out)
        lse = jnp.where(lse_lanes == head, top + jnp.log(total_weight), lse)
        return out, lse

    out, lse = lax.fori_loop(
        0, heads, one_head, (jnp.zeros((rows, width), WIDE), jnp.zeros((rows, 128), WIDE))
    )
    out_ref[...] = out.astype(LOW)
    lse_ref[...] = lse


def attend_back_kernel(
    dims, place_ref, q_ref, k_ref, v_ref, out_ref, cot_ref, lse_ref, cos_ref, sin_ref, allcos_ref, allsin_ref, grad_ref, gk_acc, gv_acc
):
    heads, width, rows, total, blks, seqs, size, scale = dims
    step = pl.program_id(0)
    lanes = lax.broadcasted_iota(jnp.int32, (1, width), 1)

    @pl.when(step == 0)
    def _():
        gk_acc[...] = jnp.zeros_like(gk_acc)
        gv_acc[...] = jnp.zeros_like(gv_acc)

    queries = q_ref[...]
    blk_rank, seq_rank, length = place_ref[0], place_ref[1], place_ref[2]
    q_index = step * rows + lax.broadcasted_iota(jnp.int32, (rows, 1), 0)
    k_index = lax.broadcasted_iota(jnp.int32, (1, total), 1)
    q_pos = row_positions(q_index, blk_rank, seq_rank, blks, seqs, size)
    k_pos = row_positions(k_index, blk_rank, seq_rank, blks, seqs, size)
    k_pos = jnp.where(k_pos < length, k_pos, jnp.int32(1 << 30))
    allowed = k_pos <= q_pos
    lse_lanes = lax.broadcasted_iota(jnp.int32, (1, 128), 1)
    cot = cot_ref[...].astype(WIDE)
    dots = cot * out_ref[...].astype(WIDE)

    def one_head(head, grad_q):
        mine = lanes // HEAD_DIM == head
        picked = jnp.where(mine, queries.astype(WIDE) * scale, 0.0).astype(LOW)
        cot_head = jnp.where(mine, cot, 0.0).astype(LOW)
        row_dot = jnp.sum(jnp.where(mine, dots, 0.0), axis=1, keepdims=True)
        lse = jnp.sum(jnp.where(lse_lanes == head, lse_ref[...], 0.0), axis=1, keepdims=True)
        scores = over_cols(picked, k_ref[...])
        probs = jnp.exp(jnp.where(allowed, scores, -1e30) - lse)
        gv_acc[...] += over_rows(probs.astype(LOW), cot_head)
        grad_probs = over_cols(cot_head, v_ref[...])
        grad_scores = (probs * (grad_probs - row_dot)).astype(LOW)
        gk_acc[...] += over_rows(grad_scores, picked)
        return jnp.where(mine, matmul(grad_scores, k_ref[...]) * scale, grad_q)

    grad_q = lax.fori_loop(0, heads, one_head, jnp.zeros((rows, width), WIDE))
    low = grad_q.astype(LOW).astype(WIDE)
    turned = low * cos_ref[...] - partner(low, lanes) * sin_ref[...]
    here = pl.ds(pl.multiple_of(step * rows, rows), rows)
    grad_ref[here, :width] = turned.astype(LOW)

    @pl.when(step == pl.num_programs(0) - 1)
    def _():
        low_k = gk_acc[...].astype(LOW).astype(WIDE)
        turned_k = low_k * allcos_ref[...] - partner(low_k, lanes) * allsin_ref[...]
        grad_ref[:, width : 2 * width] = turned_k.astype(LOW)
        grad_ref[:, 2 * width :] = gv_acc[...].astype(LOW)


def attention_dims(total, width, size, rows):
    return (
        width // HEAD_DIM, width, rows, total, lax.axis_size("blk"), lax.axis_size("seq"), size, HEAD_DIM**-0.5,
    )


def attend(qkv, place, cos, sin, size):
    total, width = qkv.shape[0], qkv.shape[1] // 3
    rows = min(256, total)
    dims = attention_dims(total, width, size, rows)
    by_rows = lambda wide: pl.BlockSpec((rows, wide), lambda i, place: (i, 0))
    whole = lambda wide: pl.BlockSpec((total, wide), lambda i, place: (0, 0))
    return pl.pallas_call(
        partial(attend_kernel, dims),
        grid_spec=pltpu.PrefetchScalarGridSpec(
            num_scalar_prefetch=1,
            grid=(total // rows,),
            in_specs=[
                by_rows(3 * width), whole(3 * width), by_rows(width), by_rows(width), whole(width), whole(width),
            ],
            out_specs=[by_rows(width), whole(width), whole(width), by_rows(width), by_rows(128)],
        ),
        out_shape=[
            jax.ShapeDtypeStruct((total, width), LOW),
            jax.ShapeDtypeStruct((total, width), LOW),
            jax.ShapeDtypeStruct((total, width), LOW),
            jax.ShapeDtypeStruct((total, width), LOW),
            jax.ShapeDtypeStruct((total, 128), WIDE),
        ],
        compiler_params=pltpu.CompilerParams(vmem_limit_bytes=48 << 20),
        cost_estimate=pl.CostEstimate(
            flops=4 * total * total * width * dims[0], bytes_accessed=total * width * 30,
            transcendentals=total * total * dims[0],
        ),
        name="attend",
    )(place, qkv, qkv, cos, sin, cos, sin)


def attend_back(queries, key_rows, val_rows, attended, cot, lse, place, cos, sin, size):
    total, width = queries.shape
    rows = min(256, total)
    dims = attention_dims(total, width, size, rows)
    by_rows = lambda wide: pl.BlockSpec((rows, wide), lambda i, place: (i, 0))
    whole = lambda wide: pl.BlockSpec((total, wide), lambda i, place: (0, 0))
    return pl.pallas_call(
        partial(attend_back_kernel, dims),
        grid_spec=pltpu.PrefetchScalarGridSpec(
            num_scalar_prefetch=1,
            grid=(total // rows,),
            in_specs=[
                by_rows(width), whole(width), whole(width), by_rows(width), by_rows(width), by_rows(128),
                by_rows(width), by_rows(width), whole(width), whole(width),
            ],
            out_specs=whole(3 * width),
            scratch_shapes=[pltpu.VMEM((total, width), WIDE), pltpu.VMEM((total, width), WIDE)],
        ),
        out_shape=jax.ShapeDtypeStruct((total, 3 * width), LOW),
        compiler_params=pltpu.CompilerParams(vmem_limit_bytes=48 << 20),
        cost_estimate=pl.CostEstimate(
            flops=10 * total * total * width * dims[0], bytes_accessed=total * width * 30,
            transcendentals=total * total * dims[0],
        ),
        name="attend_back",
    )(place, queries, key_rows, val_rows, attended, cot, lse, cos, sin, cos, sin)


def gather_gains(gains):
    blks, rank = lax.axis_size("blk"), lax.axis_index("blk")
    width = gains.shape[1]
    full = jnp.zeros((2, blks * width), gains.dtype)
    full = lax.dynamic_update_slice(full, gains, (0, rank * width))
    for k in range(1, blks):
        full = lax.dynamic_update_slice(full, turn(gains, "blk", k), (0, (rank - k) % blks * width))
    near = [swap(full, "slot", 1), swap(full, "slot", 2)]
    return jnp.concatenate([full, near[0], near[1], swap(near[0], "slot", 2)], axis=1)


def sum_gain(term):
    blks, rank = lax.axis_size("blk"), lax.axis_index("blk")
    term = term[None]
    bit = 1
    while bit < lax.axis_size("seq"):
        term = term + swap(term, "seq", bit)
        bit *= 2
    width = term.shape[1] // lax.axis_size("slot")
    parts = [term[:, i * width : (i + 1) * width] for i in range(4)]
    relay = parts[2] + swap(parts[3], "slot", 1)
    mine = parts[0] + swap(parts[1], "slot", 1) + swap(relay, "slot", 2)
    total = mine
    for k in range(1, blks):
        total = total + turn(mine, "blk", k)
    shard = width // blks
    return lax.dynamic_slice(total, (0, rank * shard), (1, shard))[0]


def shards(
    tokens, out_grad, lengths, attn_gain, w_query, w_key, w_value, output_weight, mlp_gain, gate_weight, up_weight, down_weight
):
    seqs, blks = lax.axis_size("seq"), lax.axis_size("blk")
    seq_rank, blk_rank = lax.axis_index("seq"), lax.axis_index("blk")
    size, model = tokens.shape[1], tokens.shape[2]
    total = size * seqs * blks
    length = lengths[0]
    width = w_query.shape[1] // blks
    hidden = gate_weight.shape[1] // blks
    positions = (blk_rank * seqs + seq_rank) * size + jnp.arange(size, dtype=jnp.int32)
    live_rows = (positions < length)[:, None]
    place = jnp.stack([blk_rank, seq_rank, length]).astype(jnp.int32)

    all_pos = row_positions(jnp.arange(total, dtype=jnp.int32), blk_rank, seq_rank, blks, seqs, size)
    half = HEAD_DIM // 2
    frequency = ROPE_BASE ** (-jnp.arange(half, dtype=WIDE) * 2.0 / HEAD_DIM)
    angles = all_pos.astype(WIDE)[:, None] * frequency[None, :]
    cos_tab, sin_tab = jnp.cos(angles), jnp.sin(angles)
    cos_wide = jnp.tile(cos_tab, (1, width // half))
    sin_wide = jnp.tile(jnp.concatenate([-sin_tab, sin_tab], axis=1), (1, width // HEAD_DIM))

    own_tokens = slot_order(tokens[0])
    own_cot = jnp.where(live_rows, slot_order(out_grad[0]), 0)
    gains = gather_gains(jnp.stack([attn_gain, mlp_gain])).astype(WIDE)
    gain_attn, gain_mlp = gains[0], gains[1]

    all_tokens = gather_rows(own_tokens)
    part_qkv = blk_weights([w_query, w_key, w_value])
    full_qkv = slot_weights(part_qkv, 2)
    rest = after((output_weight, gate_weight, up_weight, down_weight), part_qkv, all_tokens)
    part_output = blk_weights([rest[0]])
    full_output = slot_weights(part_output, 1)
    part_gate = blk_weights([rest[1]])
    full_gate = slot_weights(part_gate, 1)
    part_up = blk_weights([rest[2]])
    full_up = slot_weights(part_up, 2)
    part_down = blk_weights([rest[3]])
    full_down = slot_weights(part_down, 1)
    all_cot = gather_rows(after(own_cot, part_down))

    normed_attn, inverse_all = norm_rows(all_tokens.astype(WIDE), gain_attn)
    hidden_attn = normed_attn.astype(LOW)
    qkv_pre = matmul(hidden_attn, full_qkv)
    queries, key_rows, val_rows, attended, lse = attend(qkv_pre, place, cos_wide, sin_wide, size)
    rows_f = own_tokens.astype(WIDE)
    resid = rows_f + scatter_rows(over_cols(attended, full_output).astype(LOW))
    normed_mlp, inverse_mlp = norm_rows(resid, gain_mlp)
    hidden_mlp = gather_rows(normed_mlp.astype(LOW))
    gate_pre = matmul(hidden_mlp, full_gate)
    up_pre = matmul(hidden_mlp, full_up)
    sigmoid_gate = jax.nn.sigmoid(gate_pre)
    activation = (gate_pre * sigmoid_gate * up_pre).astype(LOW)

    grad_act = matmul(all_cot, full_down)
    grad_gate = (grad_act * up_pre * sigmoid_gate * (1.0 + gate_pre * (1.0 - sigmoid_gate))).astype(LOW)
    grad_up = (grad_act * gate_pre * sigmoid_gate).astype(LOW)
    grad_hidden_mlp = scatter_rows((over_cols(grad_gate, full_gate) + over_cols(grad_up, full_up)).astype(LOW))
    grad_resid_part, gain_mlp_term = norm_back(resid, inverse_mlp, gain_mlp, grad_hidden_mlp)
    grad_resid = own_cot.astype(WIDE) + grad_resid_part
    resid_low = gather_rows(grad_resid.astype(LOW))

    def groups(left, right):
        step = model // 4
        return [over_rows(left[:, i * step : (i + 1) * step], right).astype(LOW) for i in range(4)]

    sum_down = slot_sum(groups(all_cot, activation), 1)
    sum_gate = slot_sum(groups(hidden_mlp, grad_gate), 1)
    sum_up = slot_sum(groups(hidden_mlp, grad_up), 2)

    grad_attended = matmul(resid_low, full_output).astype(LOW)
    sum_output = slot_sum(groups(resid_low, attended), 1)
    grad_qkv = attend_back(
        queries, key_rows, val_rows, attended, grad_attended, lse, place, cos_wide, sin_wide, size
    )
    mlp_out = scatter_rows(over_cols(activation, full_down).astype(LOW))
    layer_out = jnp.where(live_rows, resid + mlp_out, 0.0)

    grad_hidden_attn = scatter_rows(over_cols(grad_qkv, full_qkv).astype(LOW))
    sum_qkv = slot_sum(groups(hidden_attn, grad_qkv), 2)
    inverse_attn = lax.rsqrt(jnp.mean(rows_f * rows_f, axis=-1, keepdims=True) + EPSILON)
    grad_in_part, gain_attn_term = norm_back(rows_f, inverse_attn, gain_attn, grad_hidden_attn)
    (grad_wdown,) = blk_grads(sum_down, [hidden])
    (grad_wgate,) = blk_grads(sum_gate, [hidden])
    (grad_wup,) = blk_grads(sum_up, [hidden])
    (grad_woutput,) = blk_grads(sum_output, [width])
    grad_wquery, grad_wkey, grad_wvalue = blk_grads(sum_qkv, [width] * 3)
    return (
        slot_order(layer_out).astype(LOW)[None],
        slot_order(grad_resid + grad_in_part)[None],
        sum_gain(gain_attn_term),
        grad_wquery,
        grad_wkey,
        grad_wvalue,
        grad_woutput,
        sum_gain(gain_mlp_term),
        grad_wgate,
        grad_wup,
        grad_wdown,
    )


def solution(mesh):
    rows = P("slot", ("blk", "seq"), None)
    gain = P(("slot", "blk"))
    weight = P(("slot", "blk"), "seq")
    return jax.shard_map(
        shards,
        mesh=mesh,
        in_specs=(rows, rows, P("slot"), gain, weight, weight, weight, weight, gain, weight, weight, weight),
        out_specs=(rows, rows, gain, weight, weight, weight, weight, gain, weight, weight, weight),
        check_vma=False,
    )
```

```python
from functools import partial

import jax
import jax.numpy as jnp
from jax import lax
from jax.experimental import pallas as pl
from jax.experimental.pallas import tpu as pltpu
from jax.sharding import PartitionSpec as P

HEADS = 32
HEAD_DIM = 64
HALF = HEAD_DIM // 2
EPSILON = 1e-05
ROPE_BASE = 130000.0
LOW = jnp.bfloat16
WIDE = jnp.float32
GROUPS = 4
ANY = pl.BlockSpec(memory_space=pl.ANY)


def turn(value, axis, by):
    count = lax.axis_size(axis)
    return lax.ppermute(value, axis, [(i, (i + by) % count) for i in range(count)])


def swap(value, axis, mask):
    count = lax.axis_size(axis)
    return lax.ppermute(value, axis, [(i, i ^ mask) for i in range(count)])


def after(value, *others):
    return lax.optimization_barrier((value, *others))[0]


def matmul(left, right):
    return jnp.dot(left, right, preferred_element_type=WIDE)


def over_rows(left, right):
    return lax.dot_general(left, right, (((0,), (0,)), ((), ())), preferred_element_type=WIDE)


def over_cols(left, right):
    return lax.dot_general(left, right, (((1,), (1,)), ((), ())), preferred_element_type=WIDE)


def slot_order(array):
    rank = lax.axis_index("slot")
    parts = jnp.split(array, GROUPS, axis=-1)
    for bit in (1, 2):
        flip = (rank & bit) != 0
        parts = [jnp.where(flip, parts[i ^ bit], parts[i]) for i in range(GROUPS)]
    return jnp.concatenate(parts, axis=-1)


def seq_gather(rows):
    count = lax.axis_size("seq")
    held = [rows]
    bit = 1
    while bit < count:
        held = held + [swap(part, "seq", bit) for part in held]
        bit *= 2
    return held


def seq_reduce(parts):
    bit = lax.axis_size("seq") // 2
    parts = [[part] for part in parts]
    while bit >= 1:
        kept = parts[:bit]
        for mine, other in zip(kept, parts[bit:]):
            mine.append(swap(add_up(other).astype(LOW), "seq", bit))
        parts = kept
        bit //= 2
    return parts[0]


def add_up(summands):
    total = summands[0]
    for summand in summands[1:]:
        total = total.astype(WIDE) + summand.astype(WIDE)
    return total


class Phases:
    def __init__(self):
        self.ended = ()

    def take(self, *values):
        values = tuple(values)
        if self.ended:
            values = lax.optimization_barrier((values, self.ended))[0]
        return values[0] if len(values) == 1 else values

    def end(self, *values):
        self.ended = values


class Exchange:
    def __init__(self, pieces):
        self.pieces = pieces
        self.got = {0: pieces[0]}

    def send(self, *steps):
        for k in steps:
            self.got[k] = turn(self.pieces[k], "blk", k)
        return [self.got[k] for k in steps]

    def by_rank(self):
        blks, rank = lax.axis_size("blk"), lax.axis_index("blk")
        rows, cols = self.got[0].shape
        full = jnp.zeros((blks * rows, cols), self.got[0].dtype)
        for k in range(blks):
            full = lax.dynamic_update_slice(full, self.got[k], ((rank - k) % blks * rows, 0))
        return full


def column_pieces(arrays, parts=1):
    blks, rank = lax.axis_size("blk"), lax.axis_index("blk")

    def cut(array, owner, part):
        width = array.shape[1] // (blks * parts)
        return lax.dynamic_slice(array, (0, (owner * parts + part) * width), (array.shape[0], width))

    return [
        jnp.concatenate([cut(a, (rank + k) % blks, part) for part in range(parts) for a in arrays], axis=1)
        for k in range(blks)
    ]


def row_pieces(summands):
    blks, rank = lax.axis_size("blk"), lax.axis_index("blk")
    rows = summands[0].shape[0] // blks

    def cut(owner):
        parts = [lax.dynamic_slice(s, (owner * rows, 0), (rows, s.shape[1])) for s in summands]
        return add_up(parts).astype(LOW)

    return [cut((rank + k) % blks) for k in range(blks)]


def join_owners(exchanged, cuts, scale):
    blks, rank = lax.axis_size("blk"), lax.axis_index("blk")
    wide = sum(width for _, width in cuts)
    out = jnp.zeros((exchanged.got[0].shape[0], blks * wide), WIDE)
    for k in range(blks):
        first = (rank - k) % blks * wide
        for at, width in cuts:
            part = exchanged.got[k][:, at : at + width].astype(WIDE) * scale
            out = lax.dynamic_update_slice(out, part, (0, first))
            first = first + width
    return out


def norm_rows(rows):
    inverse = lax.rsqrt(jnp.mean(rows * rows, axis=-1, keepdims=True) + EPSILON)
    return rows * inverse, inverse


def norm_back(normed, inverse, upstream):
    product = upstream * normed
    return inverse * (upstream - normed * jnp.mean(product, axis=-1, keepdims=True)), product


def vmem(shape):
    return pl.BlockSpec(shape, lambda *_: (0,) * len(shape))


def params(mebibytes):
    return pltpu.CompilerParams(vmem_limit_bytes=mebibytes << 20)


def cost():
    return pl.CostEstimate(flops=1, bytes_accessed=1, transcendentals=0)


def partner(vectors):
    width = vectors.shape[1]
    if width % 128 == 0:
        lanes = lax.broadcasted_iota(jnp.int32, (1, width), 1)
        ahead = pltpu.roll(vectors, width - HALF, 1)
        behind = pltpu.roll(vectors, HALF, 1)
        return jnp.where(lanes % HEAD_DIM < HALF, ahead, behind)
    parts = []
    for first in range(0, width, HEAD_DIM):
        parts += [vectors[:, first + HALF : first + HEAD_DIM], vectors[:, first : first + HALF]]
    return jnp.concatenate(parts, axis=1)


def widen(table, width):
    return table if table.shape[1] == width else jnp.concatenate([table] * (width // table.shape[1]), axis=1)


def qkv_kernel(width, *refs):
    parts, weights, (cos_ref, sin_ref) = refs[:-10], refs[-10:-6], refs[-6:-4]
    h_ref, q_ref, k_ref, v_ref = refs[-4:]
    size, model = parts[0].shape
    step = model // GROUPS
    for n, part in enumerate(parts):
        normed, _ = norm_rows(part[...].astype(WIDE))
        h_ref[n * size : (n + 1) * size, :] = normed.astype(LOW)
    total = h_ref.shape[0]
    rows = min(512, total)

    def some(first):
        here = slice(first, first + rows)
        pre = matmul(h_ref[here, :step], weights[0][:, : 3 * width])
        for i in range(1, GROUPS):
            pre += matmul(h_ref[here, i * step : (i + 1) * step], weights[i][:, : 3 * width])
        cos, sin = widen(cos_ref[here, :], width), widen(sin_ref[here, :], width)
        for at, out_ref in ((0, q_ref), (1, k_ref)):
            half = pre[:, at * width : (at + 1) * width]
            out_ref[here, :] = (half * cos + partner(half) * sin).astype(LOW)
        v_ref[here, :] = pre[:, 2 * width :].astype(LOW)

    for first in range(0, total, rows):
        some(first)


def project_qkv(parts, weights, cos, sin, width):
    size, model = parts[0].shape
    total = size * len(parts)
    return pl.pallas_call(
        partial(qkv_kernel, width),
        grid=(1,),
        in_specs=[vmem((size, model))] * len(parts) + [vmem(w.shape) for w in weights] + [vmem(cos.shape)] * 2,
        out_specs=[vmem((total, model))] + [vmem((total, width))] * 3,
        out_shape=[jax.ShapeDtypeStruct((total, model), LOW)] + [jax.ShapeDtypeStruct((total, width), LOW)] * 3,
        compiler_params=params(60),
        cost_estimate=cost(),
        name="project_qkv",
    )(*parts, *weights, cos, sin)


def row_positions(index, blk_rank, seq_rank, blks, seqs, size):
    sub = index // size
    k, m = sub // seqs, sub % seqs
    return ((blk_rank - k + blks) % blks * seqs + (seq_rank ^ m)) * size + index % size


def allowed_pairs(dims, place_ref, firsts, rows):
    total, blks, seqs, size = dims
    blk_rank, seq_rank, length = place_ref[0], place_ref[1], place_ref[2]
    k_index = lax.broadcasted_iota(jnp.int32, (1, total), 1)
    k_pos = row_positions(k_index, blk_rank, seq_rank, blks, seqs, size)
    k_pos = jnp.where(k_pos < length, k_pos, jnp.int32(1 << 30))
    index = lax.broadcasted_iota(jnp.int32, (rows, 1), 0)
    q_pos = [row_positions(first + index, blk_rank, seq_rank, blks, seqs, size) for first in firsts]
    return k_pos <= jnp.concatenate(q_pos, axis=0)


def tiles_of(count, block):
    if count * block <= 512:
        return [[(g, 0, block) for g in range(count)]]
    rows = min(256, block)
    return [[(g, first, rows)] for g in range(count) for first in range(0, block, rows)]


def rows_of(refs, tile):
    return jnp.concatenate([refs[g][first : first + rows, :] for g, first, rows in tile], axis=0)


def put_rows(refs, tile, value):
    at = 0
    for g, first, rows in tile:
        refs[g][first : first + rows, :] = value[at : at + rows]
        at += rows


def put_parts(terms, size, column, value):
    seqs = len(terms)
    for n in range(value.shape[0] // size):
        g, m = n // seqs, n % seqs
        terms[m][g * size : (g + 1) * size, column : column + value.shape[1]] = value[n * size : (n + 1) * size]


def attend_kernel(dims, ks, width, place_ref, *refs):
    count, seqs = len(ks), dims[2]
    q_refs, (k_ref, v_ref), weights = refs[:count], refs[count : count + 2], refs[count + 2 : count + 6]
    out_refs, lse_refs, terms = refs[count + 6 : 2 * count + 6], refs[2 * count + 6 : 3 * count + 6], refs[3 * count + 6 :]
    block = q_refs[0].shape[0]
    lanes = lax.broadcasted_iota(jnp.int32, (1, width), 1)
    lse_lanes = lax.broadcasted_iota(jnp.int32, (1, 128), 1)
    for tile in tiles_of(count, block):
        rows = tile[0][2]
        allowed = allowed_pairs(dims, place_ref, [ks[g] * block + first for g, first, _ in tile], rows)
        queries = rows_of(q_refs, tile).astype(WIDE) * HEAD_DIM**-0.5
        wide = rows * len(tile)

        def one_head(head, carried):
            out, lse = carried
            mine = lanes // HEAD_DIM == head
            picked = jnp.where(mine, queries, 0.0).astype(LOW)
            scores = jnp.where(allowed, over_cols(picked, k_ref[...]), -1e30)
            top = jnp.max(scores, axis=1, keepdims=True)
            probs = jnp.exp(scores - top)
            weight = jnp.sum(probs, axis=1, keepdims=True)
            mixed = matmul(probs.astype(LOW), v_ref[...]) / weight
            return jnp.where(mine, mixed, out), jnp.where(lse_lanes == head, top + jnp.log(weight), lse)

        out, lse = lax.fori_loop(
            0, width // HEAD_DIM, one_head, (jnp.zeros((wide, width), WIDE), jnp.zeros((wide, 128), WIDE))
        )
        put_rows(out_refs, tile, out.astype(LOW))
        put_rows(lse_refs, tile, lse)
    attended = jnp.concatenate([ref[...] for ref in out_refs], axis=0)
    for i, weight in enumerate(weights):
        step = weight.shape[0]
        put_parts(terms, block // seqs, i * step, over_cols(attended, weight[:, 3 * width :]).astype(LOW))


def attend_blocks(ks, place, queries, key_rows, val_rows, weights, size, model):
    total, width = queries.shape
    blks, seqs, count = lax.axis_size("blk"), lax.axis_size("seq"), len(ks)
    block = total // blks
    rows_at = lambda k, wide: pl.BlockSpec((block, wide), lambda *_: (k, 0))
    got = pl.pallas_call(
        partial(attend_kernel, (total, blks, seqs, size), ks, width),
        grid_spec=pltpu.PrefetchScalarGridSpec(
            num_scalar_prefetch=1,
            grid=(1,),
            in_specs=[rows_at(k, width) for k in ks] + [vmem((total, width))] * 2 + [vmem(w.shape) for w in weights],
            out_specs=[vmem((block, width))] * count + [vmem((block, 128))] * count + [vmem((count * size, model))] * seqs,
        ),
        out_shape=[jax.ShapeDtypeStruct((block, width), LOW)] * count
        + [jax.ShapeDtypeStruct((block, 128), WIDE)] * count
        + [jax.ShapeDtypeStruct((count * size, model), LOW)] * seqs,
        compiler_params=params(56),
        cost_estimate=cost(),
        name="attend_blocks",
    )(place, *[queries] * count, key_rows, val_rows, *weights)
    return got[:count], got[count : 2 * count], got[2 * count :]


def mlp_kernel(count, seqs, place_ref, *refs):
    parts, pairs, down = refs[:count], (refs[count : count + 4], refs[count + 4 : count + 8]), refs[count + 8 : count + 12]
    grad_acc, out_acc, h_rel = refs[-3:]
    outs = refs[-3 - 4 - 2 * seqs : -3]
    h_ref, c_ref, act_ref, pair_ref = outs[:4]
    grad_terms, out_terms = outs[4 : 4 + seqs], outs[4 + seqs :]
    size, model = parts[0].shape[0], h_ref.shape[1]
    step, hidden = model // GROUPS, down[0].shape[1]
    j = pl.program_id(0)
    groups = [slice(i * step, (i + 1) * step) for i in range(GROUPS)]

    @pl.when(j == 0)
    def _():
        for m in range(count):
            rows = slice(m * size, (m + 1) * size)
            h_rel[rows, :] = parts[m][:, :model]
            c_ref[rows, :] = parts[m][:, model:]
            for i in range(GROUPS):
                there = pl.multiple_of((place_ref[3] ^ i) * step, step)
                h_ref[rows, pl.ds(there, step)] = parts[m][:, groups[i]]

    def pair_weight(i):
        return jnp.where(j == 0, pairs[0][i][...], pairs[1][i][...])

    both = matmul(h_rel[:, groups[0]], pair_weight(0))
    grad_act = matmul(c_ref[:, groups[0]], down[0][...])
    for i in range(1, GROUPS):
        both += matmul(h_rel[:, groups[i]], pair_weight(i))
        grad_act += matmul(c_ref[:, groups[i]], down[i][...])
    gate, up = both[:, :hidden], both[:, hidden:]
    sig = jax.nn.sigmoid(gate)
    act_ref[...] = (gate * sig * up).astype(LOW)
    pair_ref[:, :hidden] = (grad_act * up * sig * (1.0 + gate * (1.0 - sig))).astype(LOW)
    pair_ref[:, hidden:] = (grad_act * gate * sig).astype(LOW)
    for i, here in enumerate(groups):
        grad = over_cols(pair_ref[...], pair_weight(i))
        out = over_cols(act_ref[...], down[i][...])

        @pl.when(j == 0)
        def _():
            grad_acc[:, here] = grad
            out_acc[:, here] = out

        @pl.when(j == 1)
        def _():
            grad_sum, out_sum = grad_acc[:, here] + grad, out_acc[:, here] + out
            put_parts(grad_terms, size, i * step, grad_sum.astype(LOW))
            put_parts(out_terms, size, i * step, out_sum.astype(LOW))


def mlp_blocks(at, seqs, place, parts, pairs, down, held, total):
    count, (size, model) = len(parts), (parts[0].shape[0], parts[0].shape[1] // 2)
    step, hidden = model // GROUPS, down[0].shape[1] // 2
    rows = count * size
    old = [] if held is None else list(held)
    mine = lambda wide: pl.BlockSpec((rows, wide), lambda j, place: (at, 0))
    mine_half = lambda wide: pl.BlockSpec((rows, wide), lambda j, place: (at, j))
    half = lambda wide: pl.BlockSpec((step, wide), lambda j, place: (0, j))
    got = pl.pallas_call(
        partial(mlp_kernel, count, seqs),
        grid_spec=pltpu.PrefetchScalarGridSpec(
            num_scalar_prefetch=1,
            grid=(2,),
            in_specs=[vmem((size, 2 * model))] * count
            + [vmem((step, 2 * hidden))] * 8
            + [half(hidden)] * 4
            + [ANY] * len(old),
            out_specs=[mine(model), mine(model), mine_half(hidden), mine_half(2 * hidden)]
            + [vmem((rows // seqs, model))] * (2 * seqs),
            scratch_shapes=[pltpu.VMEM((rows, model), WIDE)] * 2 + [pltpu.VMEM((rows, model), LOW)],
        ),
        out_shape=[jax.ShapeDtypeStruct((total, model), LOW)] * 2
        + [jax.ShapeDtypeStruct((total, 2 * hidden), LOW), jax.ShapeDtypeStruct((total, 4 * hidden), LOW)]
        + [jax.ShapeDtypeStruct((rows // seqs, model), LOW)] * (2 * seqs),
        input_output_aliases={count + 13 + i: i for i in range(4)} if old else {},
        compiler_params=params(60),
        cost_estimate=cost(),
        name="mlp_blocks",
    )(place, *parts, *pairs[0], *pairs[1], *down, *old)
    return got[:4], got[4 : 4 + seqs], got[4 + seqs :]


def attend_back_kernel(dims, ks, width, fresh, place_ref, *refs):
    count, seqs = len(ks), dims[2]

    def some(number):
        nonlocal refs
        taken, refs = refs[:number], refs[number:]
        return taken

    q_refs, (k_ref, v_ref), out_refs, lse_refs = some(count), some(2), some(count), some(count)
    cos_refs, sin_refs, weights, parts = some(count), some(count), some(4), some(count * seqs)
    old = [] if fresh else some(3)
    (r_ref, gk_ref, gv_ref), gq_refs, (cot_ref,) = some(3), some(count), some(1)
    block = q_refs[0].shape[0]
    size = block // seqs
    lanes = lax.broadcasted_iota(jnp.int32, (1, width), 1)
    lse_lanes = lax.broadcasted_iota(jnp.int32, (1, 128), 1)
    gk_ref[...] = jnp.zeros_like(gk_ref) if fresh else old[1][...]
    gv_ref[...] = jnp.zeros_like(gv_ref) if fresh else old[2][...]
    for n, part in enumerate(parts):
        r_ref[n * size : (n + 1) * size, :] = part[...]
    step = weights[0].shape[0]
    cot = matmul(r_ref[:, :step], weights[0][:, 3 * width :])
    for i in range(1, GROUPS):
        cot += matmul(r_ref[:, i * step : (i + 1) * step], weights[i][:, 3 * width :])
    cot_ref[...] = cot.astype(LOW).astype(WIDE)
    for tile in tiles_of(count, block):
        rows = tile[0][2]
        allowed = allowed_pairs(dims, place_ref, [ks[g] * block + first for g, first, _ in tile], rows)
        queries = rows_of(q_refs, tile).astype(WIDE) * HEAD_DIM**-0.5
        tile_cot = jnp.concatenate([cot_ref[g * block + first : g * block + first + n, :] for g, first, n in tile], axis=0)
        dots = tile_cot * rows_of(out_refs, tile).astype(WIDE)
        tile_lse = rows_of(lse_refs, tile)
        wide = rows * len(tile)

        def one_head(head, grad_q):
            mine = lanes // HEAD_DIM == head
            picked = jnp.where(mine, queries, 0.0).astype(LOW)
            cot_head = jnp.where(mine, tile_cot, 0.0).astype(LOW)
            row_dot = jnp.sum(jnp.where(mine, dots, 0.0), axis=1, keepdims=True)
            lse = jnp.sum(jnp.where(lse_lanes == head, tile_lse, 0.0), axis=1, keepdims=True)
            scores = jnp.where(allowed, over_cols(picked, k_ref[...]), -1e30)
            probs = jnp.exp(scores - lse)
            gv_ref[...] += over_rows(probs.astype(LOW), cot_head)
            grad_probs = over_cols(cot_head, v_ref[...])
            grad_scores = (probs * (grad_probs - row_dot)).astype(LOW)
            gk_ref[...] += over_rows(grad_scores, picked)
            return jnp.where(mine, matmul(grad_scores, k_ref[...]) * HEAD_DIM**-0.5, grad_q)

        grad_q = lax.fori_loop(0, width // HEAD_DIM, one_head, jnp.zeros((wide, width), WIDE))
        low = grad_q.astype(LOW).astype(WIDE)
        cos, sin = widen(rows_of(cos_refs, tile), width), widen(rows_of(sin_refs, tile), width)
        put_rows(gq_refs, tile, (low * cos - partner(low) * sin).astype(LOW))


def attend_back_blocks(at, ks, place, queries, key_rows, val_rows, attended, lse, cos, sin, weights, parts, held):
    total, width = queries.shape
    blks, seqs, count = lax.axis_size("blk"), lax.axis_size("seq"), len(ks)
    size, model = parts[0].shape
    block = total // blks
    rows_at = lambda k, wide: pl.BlockSpec((block, wide), lambda *_: (k, 0))
    whole = vmem((total, width))
    old = [] if held is None else list(held)
    first_old = 1 + count + 2 + 2 * count + 2 * count + 4 + count * seqs
    tables = [rows_at(k, cos.shape[1]) for k in ks]
    got = pl.pallas_call(
        partial(attend_back_kernel, (total, blks, seqs, size), ks, width, held is None),
        grid_spec=pltpu.PrefetchScalarGridSpec(
            num_scalar_prefetch=1,
            grid=(1,),
            in_specs=[rows_at(k, width) for k in ks]
            + [whole] * 2
            + [vmem((block, width))] * count
            + [vmem((block, 128))] * count
            + tables * 2
            + [vmem(w.shape) for w in weights]
            + [vmem((size, model))] * (count * seqs)
            + ([ANY, whole, whole] if old else []),
            out_specs=[pl.BlockSpec((count * block, model), lambda *_: (at, 0)), whole, whole] + [vmem((block, width))] * count,
            scratch_shapes=[pltpu.VMEM((count * block, width), WIDE)],
        ),
        out_shape=[jax.ShapeDtypeStruct((total, model), LOW)]
        + [jax.ShapeDtypeStruct((total, width), WIDE)] * 2
        + [jax.ShapeDtypeStruct((block, width), LOW)] * count,
        input_output_aliases={first_old + i: i for i in range(3)} if old else {},
        compiler_params=params(60),
        cost_estimate=cost(),
        name="attend_back_blocks",
    )(
        place, *[queries] * count, key_rows, val_rows, *[attended[k] for k in ks], *[lse[k] for k in ks],
        *[cos] * count, *[sin] * count, *weights, *parts, *old,
    )
    return got[:3], got[3:]


def finish_kernel(width, count, seqs, *refs):
    def some(number):
        nonlocal refs
        taken, refs = refs[:number], refs[number:]
        return taken

    gq_refs, gk_refs, gv_refs, cos_refs, sin_refs = (some(count) for _ in range(5))
    weights, parts = some(4), some(count * seqs)
    outs, (gain_ref,), terms = some(count), some(1), some(seqs)
    size = parts[0].shape[0]
    step = weights[0].shape[0]
    for g, out_ref in enumerate(outs):
        low_k = gk_refs[g][...].astype(LOW).astype(WIDE)
        cos, sin = widen(cos_refs[g][...], width), widen(sin_refs[g][...], width)
        out_ref[:, :width] = gq_refs[g][...]
        out_ref[:, width : 2 * width] = (low_k * cos - partner(low_k) * sin).astype(LOW)
        out_ref[:, 2 * width :] = gv_refs[g][...].astype(LOW)
    grads = jnp.concatenate([ref[...] for ref in outs], axis=0)
    inverses = []
    for part in parts:
        rows = part[...].astype(WIDE)
        inverses.append(lax.rsqrt(jnp.mean(rows * rows, axis=-1, keepdims=True) + EPSILON))
    for i in range(GROUPS):
        here = slice(i * step, (i + 1) * step)
        grad = over_cols(grads, weights[i][:, : 3 * width])
        put_parts(terms, size, i * step, grad.astype(LOW))
        gain = 0.0
        for n, part in enumerate(parts):
            mine = grad[n * size : (n + 1) * size]
            gain += jnp.sum(mine * (part[:, here].astype(WIDE) * inverses[n]), axis=0, keepdims=True)
        gain_ref[:, here] = gain


def finish_blocks(ks, grad_q, grad_k, grad_v, cos, sin, weights, parts):
    count = len(ks)
    total, width = grad_k.shape
    seqs, (size, model) = len(parts) // count, parts[0].shape
    block = size * seqs
    rows_at = lambda k, wide: pl.BlockSpec((block, wide), lambda _: (k, 0))
    tables = [rows_at(k, cos.shape[1]) for k in ks]
    got = pl.pallas_call(
        partial(finish_kernel, width, count, seqs),
        grid=(1,),
        in_specs=[vmem((block, width))] * count
        + [rows_at(k, width) for k in ks] * 2
        + tables * 2
        + [vmem(w.shape) for w in weights]
        + [vmem((size, model))] * (count * seqs),
        out_specs=[vmem((block, 3 * width))] * count + [vmem((1, model))] + [vmem((count * size, model))] * seqs,
        out_shape=[jax.ShapeDtypeStruct((block, 3 * width), LOW)] * count
        + [jax.ShapeDtypeStruct((1, model), WIDE)]
        + [jax.ShapeDtypeStruct((count * size, model), LOW)] * seqs,
        compiler_params=params(56),
        cost_estimate=cost(),
        name="finish_blocks",
    )(*[grad_q[k] for k in ks], *[grad_k] * count, *[grad_v] * count, *[cos] * count, *[sin] * count, *weights, *parts)
    return got[:count], got[count], got[count + 1 :]


def weight_kernel(counts, *refs):
    outs = refs[-GROUPS:]
    step = outs[0].shape[0]
    for i, out_ref in enumerate(outs):
        at, column = 0, 0
        for count in counts:
            left_ref, rights = refs[at], refs[at + 1 : at + 1 + count]
            rows, wide = rights[0].shape
            here = slice(i * step, (i + 1) * step)
            total = over_rows(left_ref[:rows, here], rights[0][...])
            for g in range(1, count):
                total += over_rows(left_ref[g * rows : (g + 1) * rows, here], rights[g][...])
            out_ref[:, column : column + wide] = total.astype(LOW)
            at, column = at + 1 + count, column + wide


def weight_terms(*pairs):
    step = pairs[0][0].shape[1] // GROUPS
    cols = sum(rights[0].shape[1] for _, rights in pairs)
    arrays = [a for left, rights in pairs for a in (left, *rights)]
    return pl.pallas_call(
        partial(weight_kernel, [len(rights) for _, rights in pairs]),
        grid=(1,),
        in_specs=[vmem(a.shape) for a in arrays],
        out_specs=[vmem((step, cols))] * GROUPS,
        out_shape=[jax.ShapeDtypeStruct((step, cols), LOW)] * GROUPS,
        compiler_params=params(60),
        cost_estimate=cost(),
        name="weight_terms",
    )(*arrays)


def pair_kernel(left_ref, right_ref, out_ref):
    out_ref[...] = over_rows(left_ref[...], right_ref[...]).astype(LOW)


def pair_term(left, right):
    (total, model), cols = left.shape, right.shape[1]
    tall, wide = min(model, 1024), min(cols, 1024)
    return pl.pallas_call(
        pair_kernel,
        grid=(model // tall, cols // wide),
        in_specs=[pl.BlockSpec((total, tall), lambda i, j: (0, i)), pl.BlockSpec((total, wide), lambda i, j: (0, j))],
        out_specs=pl.BlockSpec((tall, wide), lambda i, j: (i, j)),
        out_shape=jax.ShapeDtypeStruct((model, cols), LOW),
        compiler_params=params(60),
        cost_estimate=cost(),
        name="pair_term",
    )(left, right)


def shards(
    tokens, out_grad, lengths, attn_gain, w_query, w_key, w_value, output_weight, mlp_gain, gate_weight, up_weight, down_weight
):
    seqs, blks = lax.axis_size("seq"), lax.axis_size("blk")
    seq_rank, blk_rank = lax.axis_index("seq"), lax.axis_index("blk")
    size, model = tokens.shape[1], tokens.shape[2]
    block = size * seqs
    total = block * blks
    length = lengths[0]
    width = w_query.shape[1] // blks
    hidden = gate_weight.shape[1] // blks
    positions = (blk_rank * seqs + seq_rank) * size + jnp.arange(size, dtype=jnp.int32)
    live_rows = (positions < length)[:, None]
    place = jnp.stack([blk_rank, seq_rank, length, lax.axis_index("slot")]).astype(jnp.int32)

    all_pos = row_positions(jnp.arange(total, dtype=jnp.int32), blk_rank, seq_rank, blks, seqs, size)
    frequency = ROPE_BASE ** (-jnp.arange(HALF, dtype=WIDE) * 2.0 / HEAD_DIM)
    angles = all_pos.astype(WIDE)[:, None] * frequency[None, :]
    cos_tab, sin_tab = jnp.cos(angles), jnp.sin(angles)
    table = min(width, 128)
    cos_wide = jnp.tile(cos_tab, (1, table // HALF))
    sin_wide = jnp.tile(jnp.concatenate([-sin_tab, sin_tab], axis=1), (1, table // HEAD_DIM))

    own_tokens = slot_order(tokens[0])
    own_cot = jnp.where(live_rows, slot_order(out_grad[0]), 0)
    gain_attn, gain_mlp = attn_gain.astype(WIDE)[:, None], mlp_gain.astype(WIDE)[:, None]
    rows_f = own_tokens.astype(WIDE)

    def scaled(weight, gain):
        return (weight.astype(WIDE) * gain).astype(LOW)

    attn_out = Exchange(
        column_pieces([scaled(w, gain_attn) for w in (w_query, w_key, w_value)] + [output_weight])
    )
    pair_out = Exchange(column_pieces([scaled(gate_weight, gain_mlp), scaled(up_weight, gain_mlp)], 2))
    down_out = Exchange(column_pieces([down_weight]))
    phase = Phases()
    flat = lambda lists: [item for items in lists for item in items]
    in_order, in_turn = [[0, 1], [2, 3]], [[1, 2], [3, 0]]

    def calls(ks):
        return [ks] if block * len(ks) <= 512 else [[k] for k in ks]

    def reduced(ks, parts):
        summands = seq_reduce(parts)
        return [[s[g * size : (g + 1) * size] for s in summands] for g in range(len(ks))]

    def reduce_calls(got):
        for ks, parts in got:
            for k, summands in zip(ks, reduced(ks, parts)):
                terms[k] = summands

    token_blocks = [None] * blks
    ahead = turn(own_tokens, "blk", 1)
    attn_out.send(1, 2, 3)
    token_blocks[0] = seq_gather(own_tokens)
    part_attn = attn_out.by_rank()
    phase.end(ahead, part_attn, token_blocks[0], cos_wide, sin_wide, place)

    moving, part_attn, down_out.pieces = phase.take(ahead, part_attn, down_out.pieces)
    ahead = turn(moving, "blk", 1)
    near_x, near_y = swap(part_attn, "slot", 1), swap(part_attn, "slot", 2)
    down_out.send(1, 3)
    phase.end(ahead, near_x, near_y, down_out.got)

    second, moving, near_x, down_out.pieces = phase.take(moving, ahead, near_x, down_out.pieces)
    ahead = turn(moving, "blk", 1)
    far = swap(near_x, "slot", 2)
    down_out.send(2)
    token_blocks[1], token_blocks[2] = seq_gather(second), seq_gather(moving)
    full_attn = [part_attn, near_x, near_y, far]
    part_down = down_out.by_rank()
    phase.end(ahead, far, token_blocks[1:3], part_down)

    moving, part_down, pair_out.pieces = phase.take(ahead, part_down, pair_out.pieces)
    token_blocks[3] = seq_gather(moving)
    near_x, near_y = swap(part_down, "slot", 1), swap(part_down, "slot", 2)
    pair_out.send(1, 3)
    got = []
    for ks in [list(range(blks))] if total <= 1024 else [[k] for k in range(blks)]:
        here = slice(ks[0] * block, (ks[-1] + 1) * block)
        got.append(project_qkv(flat([token_blocks[k] for k in ks]), full_attn, cos_wide[here], sin_wide[here], width))
    hidden_attn, queries, key_rows, val_rows = (
        parts[0] if len(parts) == 1 else jnp.concatenate(parts, axis=0) for parts in zip(*got)
    )
    attended, lse, terms = [None] * blks, [None] * blks, [None] * blks

    def attend(ks, queries):
        got = []
        for some in calls(ks):
            outs, lses, parts = attend_blocks(some, place, queries, key_rows, val_rows, full_attn, size, model)
            got.append((some, parts))
            for k, out, log in zip(some, outs, lses):
                attended[k], lse[k] = out, log
        return [ks for ks, _ in got], [parts for _, parts in got]

    takers, parts = attend(in_turn[0], queries)
    phase.end(near_x, near_y, pair_out.got, parts)

    queries, near_y, pair_out.pieces, parts = phase.take(queries, near_y, pair_out.pieces, parts)
    pair_out.send(2)
    full_down = [part_down, near_x, near_y, swap(near_y, "slot", 1)]
    reduce_calls(zip(takers, parts))
    takers, parts = attend(in_turn[1], queries)
    part_pair = pair_out.by_rank()
    phase.end(part_pair, full_down, parts, terms[1], terms[2])

    moving, part_pair, parts = phase.take(add_up(terms[1]).astype(LOW), part_pair, parts)
    halves = [part_pair[:, :hidden], part_pair[:, hidden:]]
    near_x, near_y = [swap(halves[0], "slot", 1)], [swap(halves[0], "slot", 2)]
    reduce_calls(zip(takers, parts))
    moving = turn(moving, "blk", 1)
    phase.end(moving, terms)
    moving, half_b = phase.take(add_up([moving, *terms[2]]).astype(LOW), halves[1])
    near_x, near_y = near_x + [swap(half_b, "slot", 1)], near_y + [swap(half_b, "slot", 2)]
    moving = turn(moving, "blk", 1)
    phase.end(moving, near_x[0], near_y[0])
    moving, far = phase.take(add_up([moving, *terms[3]]).astype(LOW), near_x[0])
    far_a = swap(far, "slot", 2)
    moving = turn(moving, "blk", 1)
    phase.end(moving, near_x, near_y)
    resid = rows_f + add_up([moving, *terms[0]])
    normed_mlp, inverse_mlp = norm_rows(resid)

    def feed(ks, held):
        got = []
        for some in calls(ks):
            held, grads, outs = mlp_blocks(
                some[0] // len(some), seqs, place, flat([blocks[k] for k in some]), full_pair, full_down, held, total
            )
            got.append([grads, outs])
        return held, calls(ks), got

    def reduce_pairs(takers, got):
        for ks, (grads, outs) in zip(takers, got):
            for k, grad, out in zip(ks, reduced(ks, grads), reduced(ks, outs)):
                terms[k] = [grad, out]

    def join_pair(moving, pair):
        sums = pair if moving is None else [[moving[:, i * model : (i + 1) * model], *part] for i, part in enumerate(pair)]
        return jnp.concatenate([add_up(part).astype(LOW) for part in sums], axis=1)

    blocks, terms = [None] * blks, [None] * blks
    moving, far = phase.take(jnp.concatenate([normed_mlp.astype(LOW), own_cot], axis=1), near_y[1])
    far_b = swap(far, "slot", 1)
    full_pair = [[halves[0], near_x[0], near_y[0], far_a], [halves[1], near_x[1], near_y[1], far_b]]
    ahead = turn(moving, "blk", 1)
    blocks[0] = seq_gather(moving)
    phase.end(ahead, far_a, far_b, blocks[0])

    moving, blocks[0] = phase.take(ahead, blocks[0])
    ahead = turn(moving, "blk", 1)
    blocks[1] = seq_gather(moving)
    held, takers, got = feed(in_order[0], None)
    phase.end(ahead, blocks[1], held)

    moving, got = phase.take(ahead, got)
    ahead = turn(moving, "blk", 1)
    blocks[2] = seq_gather(moving)
    reduce_pairs(takers, got)
    phase.end(ahead, blocks[2], terms[1])

    moving, summed, blocks[2] = phase.take(ahead, join_pair(None, terms[1]), blocks[2])
    blocks[3] = seq_gather(moving)
    moving = turn(summed, "blk", 1)
    held, takers, got = feed(in_order[1], held)
    phase.end(moving, held)
    hidden_mlp, all_cot, activation, grad_pair = held

    moving, got, grad_pair, activation = phase.take(moving, got, grad_pair, activation)
    reduce_pairs(takers, got)
    moving = turn(join_pair(moving, terms[2]), "blk", 1)
    term = pair_term(hidden_mlp, grad_pair)
    down_terms = weight_terms((all_cot, [activation]))
    phase.end(moving, terms, term, down_terms)

    moving, far, term = phase.take(join_pair(moving, terms[3]), down_terms[3], term)
    sum_pair = lax.psum_scatter(term, "slot", scatter_dimension=0, tiled=True)
    moving = turn(moving, "blk", 1)
    far = swap(far, "slot", 1)
    phase.end(moving, far)
    grad_part, out_part = (add_up([moving[:, i * model : (i + 1) * model], *terms[0][i]]) for i in range(2))
    layer_out = jnp.where(live_rows, resid + out_part, 0.0)
    grad_resid_part, gain_mlp_term = norm_back(normed_mlp, inverse_mlp, grad_part)
    grad_resid = own_cot.astype(WIDE) + grad_resid_part

    moving, relay, near_term = phase.take(
        grad_resid.astype(LOW), add_up([down_terms[2], far]).astype(LOW), down_terms[1]
    )
    ahead = turn(moving, "blk", 1)
    one, two = swap(relay, "slot", 2), swap(near_term, "slot", 1)
    blocks = [seq_gather(moving), None, None, None]
    phase.end(ahead, blocks[0])

    grad_q = [None] * blks

    def attend_back(ks, held):
        for some in calls(ks):
            held, grads = attend_back_blocks(
                some[0] // len(some), some, place, queries, key_rows, val_rows, attended, lse, cos_wide, sin_wide,
                full_attn, flat([blocks[k] for k in some]), held,
            )
            for k, grad in zip(some, grads):
                grad_q[k] = grad
        return held

    moving, blocks[0] = phase.take(ahead, blocks[0])
    ahead = turn(moving, "blk", 1)
    blocks[1] = seq_gather(moving)
    held = attend_back(in_order[0], None)
    phase.end(ahead, blocks[1], held)

    moving = phase.take(ahead)
    ahead = turn(moving, "blk", 1)
    blocks[2] = seq_gather(moving)
    phase.end(ahead, blocks[2], one, two)

    down_back = Exchange(row_pieces([down_terms[0], one, two]))
    moving, blocks[2], down_back.pieces = phase.take(ahead, blocks[2], down_back.pieces)
    blocks[3] = seq_gather(moving)
    down_back.send(1, 3)
    held = attend_back(in_order[1], held)
    all_resid, grad_k, grad_v = held
    phase.end(held)

    grad_qkv, terms, gain_terms = [None] * blks, [None] * blks, []

    def finish(ks, grad_k):
        got = []
        for some in calls(ks):
            outs, gain_term, parts = finish_blocks(
                some, grad_q, grad_k, grad_v, cos_wide, sin_wide, full_attn, flat([token_blocks[k] for k in some])
            )
            gain_terms.append(gain_term)
            got.append(parts)
            for k, out in zip(some, outs):
                grad_qkv[k] = out
        return calls(ks), got

    grad_k = phase.take(grad_k)
    takers, parts = finish(in_turn[0], grad_k)
    phase.end(parts, down_back.got)

    parts, grad_k, down_back.pieces = phase.take(parts, grad_k, down_back.pieces)
    reduce_calls(zip(takers, parts))
    moving = turn(add_up(terms[1]).astype(LOW), "blk", 1)
    down_back.send(2)
    takers, parts = finish(in_turn[1], grad_k)
    last_terms = weight_terms((hidden_attn, grad_qkv), (all_resid, attended))
    gain_terms = jnp.concatenate([add_up(gain_terms), jnp.sum(gain_mlp_term, axis=0, keepdims=True)], axis=0)
    phase.end(moving, terms[1], terms[2], parts, gain_terms, last_terms, down_back.got, sum_pair)

    pair_back = Exchange(row_pieces([sum_pair]))
    moving, parts, gain_terms, far, pair_back.pieces = phase.take(
        add_up([moving, *terms[2]]).astype(LOW), parts, gain_terms, last_terms[3], pair_back.pieces
    )
    moving = turn(moving, "blk", 1)
    far = swap(far, "slot", 2)
    pair_back.send(1)
    bit = 1
    while bit < seqs:
        gain_terms = gain_terms + swap(gain_terms, "seq", bit)
        bit *= 2
    reduce_calls(zip(takers, parts))
    phase.end(moving, far, terms, gain_terms, pair_back.got)

    gain_parts = jnp.split(gain_terms, GROUPS, axis=1)
    moving, relay, near_term, gain_far, gain_two, pair_back.pieces = phase.take(
        add_up([moving, *terms[3]]).astype(LOW), add_up([last_terms[1], far]).astype(LOW), last_terms[2],
        gain_parts[3], gain_parts[1], pair_back.pieces,
    )
    gain_far, gain_two = swap(gain_far, "slot", 1), swap(gain_two, "slot", 1)
    moving = turn(moving, "blk", 1)
    one, two = swap(relay, "slot", 1), swap(near_term, "slot", 2)
    pair_back.send(3)
    phase.end(moving, one, two, pair_back.got, gain_far, gain_two)

    last_back = Exchange(row_pieces([last_terms[0], one, two]))
    gain_relay, last_back.pieces, pair_back.pieces = phase.take(
        gain_parts[2] + gain_far, last_back.pieces, pair_back.pieces
    )
    gain_one = swap(gain_relay, "slot", 2)
    gain_sum = gain_parts[0] + gain_two + gain_one
    pair_back.send(2)
    last_back.send(1, 2, 3)
    gain_sums = [gain_sum] + [turn(gain_sum, "blk", k) for k in range(1, blks)]

    grad_hidden_attn = add_up([moving, *terms[0]])
    normed_attn, inverse_attn = norm_rows(rows_f)
    grad_in_part, _ = norm_back(normed_attn, inverse_attn, grad_hidden_attn)
    shard = attn_gain.shape[0]
    gain_grads = lax.dynamic_slice(add_up(gain_sums), (0, blk_rank * shard), (2, shard))
    half = hidden // 2
    return (
        slot_order(layer_out).astype(LOW)[None],
        slot_order(grad_resid + grad_in_part)[None],
        gain_grads[0] / gain_attn[:, 0],
        join_owners(last_back, [(0, width)], gain_attn),
        join_owners(last_back, [(width, width)], gain_attn),
        join_owners(last_back, [(2 * width, width)], gain_attn),
        join_owners(last_back, [(3 * width, width)], 1.0),
        gain_grads[1] / gain_mlp[:, 0],
        join_owners(pair_back, [(0, half), (hidden, half)], gain_mlp),
        join_owners(pair_back, [(half, half), (hidden + half, half)], gain_mlp),
        join_owners(down_back, [(0, hidden)], 1.0),
    )


def solution(mesh):
    rows = P("slot", ("blk", "seq"), None)
    gain = P(("slot", "blk"))
    weight = P(("slot", "blk"), "seq")
    return jax.shard_map(
        shards,
        mesh=mesh,
        in_specs=(rows, rows, P("slot"), gain, weight, weight, weight, weight, gain, weight, weight, weight),
        out_specs=(rows, rows, gain, weight, weight, weight, weight, gain, weight, weight, weight),
        check_vma=False,
    )
```

```python
import math
from functools import partial

import jax
import jax.numpy as jnp
from jax import lax
from jax.experimental import pallas as pl
from jax.experimental.pallas import tpu as pltpu
from jax.sharding import PartitionSpec as P

HEADS = 32
HEAD_DIM = 64
HALF = HEAD_DIM // 2
EPSILON = 1e-05
ROPE_BASE = 130000.0
LOW = jnp.bfloat16
WIDE = jnp.float32
GROUPS = 4
ANY = pl.BlockSpec(memory_space=pl.ANY)


def turn(value, axis, by):
    count = lax.axis_size(axis)
    return lax.ppermute(value, axis, [(i, (i + by) % count) for i in range(count)])


def swap(value, axis, mask):
    count = lax.axis_size(axis)
    return lax.ppermute(value, axis, [(i, i ^ mask) for i in range(count)])


def after(value, *others):
    return lax.optimization_barrier((value, *others))[0]


def matmul(left, right):
    return jnp.dot(left, right, preferred_element_type=WIDE)


def over_rows(left, right):
    return lax.dot_general(left, right, (((0,), (0,)), ((), ())), preferred_element_type=WIDE)


def over_cols(left, right):
    return lax.dot_general(left, right, (((1,), (1,)), ((), ())), preferred_element_type=WIDE)


def slot_order(array):
    rank = lax.axis_index("slot")
    parts = jnp.split(array, GROUPS, axis=-1)
    for bit in (1, 2):
        flip = (rank & bit) != 0
        parts = [jnp.where(flip, parts[i ^ bit], parts[i]) for i in range(GROUPS)]
    return jnp.concatenate(parts, axis=-1)


def seq_gather(rows):
    count = lax.axis_size("seq")
    held = [rows]
    bit = 1
    while bit < count:
        held = held + [swap(part, "seq", bit) for part in held]
        bit *= 2
    return held


def seq_reduce(parts):
    bit = lax.axis_size("seq") // 2
    parts = [[part] for part in parts]
    while bit >= 1:
        kept = parts[:bit]
        for mine, other in zip(kept, parts[bit:]):
            mine.append(swap(add_up(other).astype(LOW), "seq", bit))
        parts = kept
        bit //= 2
    return parts[0]


def add_up(summands):
    total = summands[0]
    for summand in summands[1:]:
        total = total.astype(WIDE) + summand.astype(WIDE)
    return total


class Phases:
    def __init__(self):
        self.ended = ()

    def take(self, *values):
        values = tuple(values)
        if self.ended:
            values = lax.optimization_barrier((values, self.ended))[0]
        return values[0] if len(values) == 1 else values

    def end(self, *values):
        self.ended = values


class Exchange:
    def __init__(self, pieces):
        self.pieces = pieces
        self.got = {0: pieces[0]}

    def send(self, *steps):
        for k in steps:
            self.got[k] = turn(self.pieces[k], "blk", k)
        return [self.got[k] for k in steps]

    def by_rank(self):
        blks, rank = lax.axis_size("blk"), lax.axis_index("blk")
        rows, cols = self.got[0].shape
        full = jnp.zeros((blks * rows, cols), self.got[0].dtype)
        for k in range(blks):
            full = lax.dynamic_update_slice(full, self.got[k], ((rank - k) % blks * rows, 0))
        return full


def column_pieces(arrays, parts=1):
    blks, rank = lax.axis_size("blk"), lax.axis_index("blk")

    def cut(array, owner, part):
        width = array.shape[1] // (blks * parts)
        return lax.dynamic_slice(array, (0, (owner * parts + part) * width), (array.shape[0], width))

    return [
        jnp.concatenate([cut(a, (rank + k) % blks, part) for part in range(parts) for a in arrays], axis=1)
        for k in range(blks)
    ]


def row_pieces(summands):
    blks, rank = lax.axis_size("blk"), lax.axis_index("blk")
    rows = summands[0].shape[0] // blks

    def cut(owner):
        parts = [lax.dynamic_slice(s, (owner * rows, 0), (rows, s.shape[1])) for s in summands]
        return add_up(parts).astype(LOW)

    return [cut((rank + k) % blks) for k in range(blks)]


def join_owners(exchanges, cuts, scale):
    blks, rank = lax.axis_size("blk"), lax.axis_index("blk")
    wide = sum(width for _, width in cuts)
    out = jnp.zeros((exchanges[0].got[0].shape[0], blks * wide * len(exchanges)), WIDE)
    for n, exchanged in enumerate(exchanges):
        for k in range(blks):
            first = ((rank - k) % blks * len(exchanges) + n) * wide
            for at, width in cuts:
                part = exchanged.got[k][:, at : at + width].astype(WIDE) * scale
                out = lax.dynamic_update_slice(out, part, (0, first))
                first = first + width
    return out


def norm_rows(rows):
    inverse = lax.rsqrt(jnp.mean(rows * rows, axis=-1, keepdims=True) + EPSILON)
    return rows * inverse, inverse


def norm_back(normed, inverse, upstream):
    product = upstream * normed
    return inverse * (upstream - normed * jnp.mean(product, axis=-1, keepdims=True)), product


def vmem(shape):
    return pl.BlockSpec(shape, lambda *_: (0,) * len(shape))


def params(mebibytes):
    return pltpu.CompilerParams(vmem_limit_bytes=mebibytes << 20)


def cost():
    return pl.CostEstimate(flops=1, bytes_accessed=1, transcendentals=0)


def partner(vectors):
    width = vectors.shape[1]
    if width % 128 == 0:
        lanes = lax.broadcasted_iota(jnp.int32, (1, width), 1)
        ahead = pltpu.roll(vectors, width - HALF, 1)
        behind = pltpu.roll(vectors, HALF, 1)
        return jnp.where(lanes % HEAD_DIM < HALF, ahead, behind)
    parts = []
    for first in range(0, width, HEAD_DIM):
        parts += [vectors[:, first + HALF : first + HEAD_DIM], vectors[:, first : first + HALF]]
    return jnp.concatenate(parts, axis=1)


def table_kernel(dims, place_ref, cos_ref, sin_ref):
    total, blks, seqs, size = dims
    wide = cos_ref.shape[1]
    index = lax.broadcasted_iota(jnp.int32, (total, 1), 0)
    position = row_positions(index, place_ref[0], place_ref[1], blks, seqs, size).astype(WIDE)
    lane = lax.broadcasted_iota(jnp.int32, (1, wide), 1)
    power = (lane % HALF).astype(WIDE) * (-2.0 / HEAD_DIM)
    angle = position * jnp.exp(power * math.log(ROPE_BASE))
    cos_ref[...] = jnp.cos(angle)
    sin_ref[...] = jnp.where(lane % HEAD_DIM < HALF, -jnp.sin(angle), jnp.sin(angle))


def rotary_tables(place, total, size, wide):
    dims = (total, lax.axis_size("blk"), lax.axis_size("seq"), size)
    return pl.pallas_call(
        partial(table_kernel, dims),
        grid_spec=pltpu.PrefetchScalarGridSpec(
            num_scalar_prefetch=1, grid=(1,), in_specs=[], out_specs=[vmem((total, wide))] * 2
        ),
        out_shape=[jax.ShapeDtypeStruct((total, wide), WIDE)] * 2,
        compiler_params=params(32),
        cost_estimate=cost(),
        name="rotary_tables",
    )(place)


def widen(table, width):
    return table if table.shape[1] == width else jnp.concatenate([table] * (width // table.shape[1]), axis=1)


def qkv_kernel(width, *refs):
    parts, weights, (cos_ref, sin_ref) = refs[:-10], refs[-10:-6], refs[-6:-4]
    h_ref, q_ref, k_ref, v_ref = refs[-4:]
    size, model = parts[0].shape
    step = model // GROUPS
    for n, part in enumerate(parts):
        normed, _ = norm_rows(part[...].astype(WIDE))
        h_ref[n * size : (n + 1) * size, :] = normed.astype(LOW)
    total = h_ref.shape[0]
    rows = min(512, total)

    def some(first):
        here = slice(first, first + rows)
        pre = matmul(h_ref[here, :step], weights[0][:, : 3 * width])
        for i in range(1, GROUPS):
            pre += matmul(h_ref[here, i * step : (i + 1) * step], weights[i][:, : 3 * width])
        cos, sin = widen(cos_ref[here, :], width), widen(sin_ref[here, :], width)
        for at, out_ref in ((0, q_ref), (1, k_ref)):
            half = pre[:, at * width : (at + 1) * width]
            out_ref[here, :] = (half * cos + partner(half) * sin).astype(LOW)
        v_ref[here, :] = pre[:, 2 * width :].astype(LOW)

    for first in range(0, total, rows):
        some(first)


def project_qkv(parts, weights, cos, sin, width):
    size, model = parts[0].shape
    total = size * len(parts)
    return pl.pallas_call(
        partial(qkv_kernel, width),
        grid=(1,),
        in_specs=[vmem((size, model))] * len(parts) + [vmem(w.shape) for w in weights] + [vmem(cos.shape)] * 2,
        out_specs=[vmem((total, model))] + [vmem((total, width))] * 3,
        out_shape=[jax.ShapeDtypeStruct((total, model), LOW)] + [jax.ShapeDtypeStruct((total, width), LOW)] * 3,
        compiler_params=params(60),
        cost_estimate=cost(),
        name="project_qkv",
    )(*parts, *weights, cos, sin)


def row_positions(index, blk_rank, seq_rank, blks, seqs, size):
    sub = index // size
    k, m = sub // seqs, sub % seqs
    return ((blk_rank - k + blks) % blks * seqs + (seq_rank ^ m)) * size + index % size


def allowed_pairs(dims, place_ref, firsts, rows):
    total, blks, seqs, size = dims
    blk_rank, seq_rank, length = place_ref[0], place_ref[1], place_ref[2]
    k_index = lax.broadcasted_iota(jnp.int32, (1, total), 1)
    k_pos = row_positions(k_index, blk_rank, seq_rank, blks, seqs, size)
    k_pos = jnp.where(k_pos < length, k_pos, jnp.int32(1 << 30))
    index = lax.broadcasted_iota(jnp.int32, (rows, 1), 0)
    q_pos = [row_positions(first + index, blk_rank, seq_rank, blks, seqs, size) for first in firsts]
    return k_pos <= jnp.concatenate(q_pos, axis=0)


def tiles_of(count, block):
    if count * block <= 512:
        return [[(g, 0, block) for g in range(count)]]
    rows = min(256, block)
    return [[(g, first, rows)] for g in range(count) for first in range(0, block, rows)]


def rows_of(refs, tile):
    return jnp.concatenate([refs[g][first : first + rows, :] for g, first, rows in tile], axis=0)


def put_rows(refs, tile, value):
    at = 0
    for g, first, rows in tile:
        refs[g][first : first + rows, :] = value[at : at + rows]
        at += rows


def put_parts(terms, size, column, value):
    for n, term in enumerate(terms):
        term[:, column : column + value.shape[1]] = value[n * size : (n + 1) * size]


def by_block(terms, count):
    some = len(terms) // count
    return [terms[g * some : (g + 1) * some] for g in range(count)]


def attend_kernel(dims, ks, width, place_ref, *refs):
    count, seqs = len(ks), dims[2]
    q_refs, (k_ref, v_ref), weights = refs[:count], refs[count : count + 2], refs[count + 2 : count + 6]
    out_refs, lse_refs, terms = refs[count + 6 : 2 * count + 6], refs[2 * count + 6 : 3 * count + 6], refs[3 * count + 6 :]
    block = q_refs[0].shape[0]
    lanes = lax.broadcasted_iota(jnp.int32, (1, width), 1)
    lse_lanes = lax.broadcasted_iota(jnp.int32, (1, 128), 1)
    for tile in tiles_of(count, block):
        rows = tile[0][2]
        allowed = allowed_pairs(dims, place_ref, [ks[g] * block + first for g, first, _ in tile], rows)
        queries = rows_of(q_refs, tile).astype(WIDE) * HEAD_DIM**-0.5
        wide = rows * len(tile)

        def one_head(head, carried):
            out, lse = carried
            mine = lanes // HEAD_DIM == head
            picked = jnp.where(mine, queries, 0.0).astype(LOW)
            scores = jnp.where(allowed, over_cols(picked, k_ref[...]), -1e30)
            top = jnp.max(scores, axis=1, keepdims=True)
            probs = jnp.exp(scores - top)
            weight = jnp.sum(probs, axis=1, keepdims=True)
            mixed = matmul(probs.astype(LOW), v_ref[...]) / weight
            return jnp.where(mine, mixed, out), jnp.where(lse_lanes == head, top + jnp.log(weight), lse)

        out, lse = lax.fori_loop(
            0, width // HEAD_DIM, one_head, (jnp.zeros((wide, width), WIDE), jnp.zeros((wide, 128), WIDE))
        )
        put_rows(out_refs, tile, out.astype(LOW))
        put_rows(lse_refs, tile, lse)
    attended = jnp.concatenate([ref[...] for ref in out_refs], axis=0)
    for i, weight in enumerate(weights):
        step = weight.shape[0]
        put_parts(terms, block // seqs, i * step, over_cols(attended, weight[:, 3 * width :]).astype(LOW))


def attend_blocks(ks, place, queries, key_rows, val_rows, weights, size, model):
    total, width = queries.shape
    blks, seqs, count = lax.axis_size("blk"), lax.axis_size("seq"), len(ks)
    block = total // blks
    rows_at = lambda k, wide: pl.BlockSpec((block, wide), lambda *_: (k, 0))
    got = pl.pallas_call(
        partial(attend_kernel, (total, blks, seqs, size), ks, width),
        grid_spec=pltpu.PrefetchScalarGridSpec(
            num_scalar_prefetch=1,
            grid=(1,),
            in_specs=[rows_at(k, width) for k in ks] + [vmem((total, width))] * 2 + [vmem(w.shape) for w in weights],
            out_specs=[vmem((block, width))] * count + [vmem((block, 128))] * count + [vmem((size, model))] * (count * seqs),
        ),
        out_shape=[jax.ShapeDtypeStruct((block, width), LOW)] * count
        + [jax.ShapeDtypeStruct((block, 128), WIDE)] * count
        + [jax.ShapeDtypeStruct((size, model), LOW)] * (count * seqs),
        compiler_params=params(56),
        cost_estimate=cost(),
        name="attend_blocks",
    )(place, *[queries] * count, key_rows, val_rows, *weights)
    return got[:count], got[count : 2 * count], by_block(got[2 * count :], count)


def mlp_kernel(count, *refs):
    parts, pairs, down = refs[:count], (refs[count : count + 4], refs[count + 4 : count + 8]), refs[count + 8 : count + 13]
    outs = refs[-5 - 2 * count :]
    h_ref, c_ref, act_ref, pair_refs = outs[0], outs[1], outs[2], outs[3:5]
    grad_terms, out_terms = outs[5 : 5 + count], outs[5 + count :]
    size, model = parts[0].shape[0], h_ref.shape[1]
    step, hidden = model // GROUPS, down[0].shape[1] // 2
    groups = [slice(i * step, (i + 1) * step) for i in range(GROUPS)]
    for m in range(count):
        rows = slice(m * size, (m + 1) * size)
        h_ref[rows, :] = parts[m][:, :model]
        c_ref[rows, :] = parts[m][:, model:]
    down_half = lambda i, j: down[i][:, j * hidden : (j + 1) * hidden] if i < 3 else down[3 + j][...]
    for j, pair_ref in enumerate(pair_refs):
        half = slice(j * hidden, (j + 1) * hidden)
        both = matmul(h_ref[:, groups[0]], pairs[j][0][...])
        grad_act = matmul(c_ref[:, groups[0]], down_half(0, j))
        for i in range(1, GROUPS):
            both += matmul(h_ref[:, groups[i]], pairs[j][i][...])
            grad_act += matmul(c_ref[:, groups[i]], down_half(i, j))
        gate, up = both[:, :hidden], both[:, hidden:]
        sig = jax.nn.sigmoid(gate)
        act_ref[:, half] = (gate * sig * up).astype(LOW)
        pair_ref[:, :hidden] = (grad_act * up * sig * (1.0 + gate * (1.0 - sig))).astype(LOW)
        pair_ref[:, hidden:] = (grad_act * gate * sig).astype(LOW)
    for i in range(GROUPS):
        grad = over_cols(pair_refs[0][...], pairs[0][i][...]) + over_cols(pair_refs[1][...], pairs[1][i][...])
        put_parts(grad_terms, size, i * step, grad.astype(LOW))
        if i < 3:
            out = over_cols(act_ref[...], down[i][...])
        else:
            out = over_cols(act_ref[:, :hidden], down[3][...]) + over_cols(act_ref[:, hidden:], down[4][...])
        put_parts(out_terms, size, i * step, out.astype(LOW))


def mlp_blocks(at, seqs, parts, pairs, down, held, total):
    count, (size, model) = len(parts), (parts[0].shape[0], parts[0].shape[1] // 2)
    hidden = down[0].shape[1]
    rows = count * size
    old = [] if held is None else list(held)
    widths = [model, model, hidden, hidden, hidden]
    got = pl.pallas_call(
        partial(mlp_kernel, count),
        grid=(1,),
        in_specs=[vmem((size, 2 * model))] * count
        + [vmem(w.shape) for w in (*pairs[0], *pairs[1], *down)]
        + [ANY] * len(old),
        out_specs=[pl.BlockSpec((rows, wide), lambda _: (at, 0)) for wide in widths] + [vmem((size, model))] * (2 * count),
        out_shape=[jax.ShapeDtypeStruct((total, wide), LOW) for wide in widths]
        + [jax.ShapeDtypeStruct((size, model), LOW)] * (2 * count),
        input_output_aliases={count + 13 + i: i for i in range(5)} if old else {},
        compiler_params=params(60),
        cost_estimate=cost(),
        name="mlp_blocks",
    )(*parts, *pairs[0], *pairs[1], *down, *old)
    return got[:5], by_block(got[5 : 5 + count], count // seqs), by_block(got[5 + count :], count // seqs)


def attend_back_kernel(dims, ks, width, fresh, place_ref, *refs):
    count, seqs = len(ks), dims[2]

    def some(number):
        nonlocal refs
        taken, refs = refs[:number], refs[number:]
        return taken

    q_refs, (k_ref, v_ref), out_refs, lse_refs = some(count), some(2), some(count), some(count)
    cos_refs, sin_refs, weights, parts = some(count), some(count), some(4), some(count * seqs)
    old = [] if fresh else some(3)
    (r_ref, gk_ref, gv_ref), gq_refs, (cot_ref,) = some(3), some(count), some(1)
    block = q_refs[0].shape[0]
    size = block // seqs
    lanes = lax.broadcasted_iota(jnp.int32, (1, width), 1)
    lse_lanes = lax.broadcasted_iota(jnp.int32, (1, 128), 1)
    gk_ref[...] = jnp.zeros_like(gk_ref) if fresh else old[1][...]
    gv_ref[...] = jnp.zeros_like(gv_ref) if fresh else old[2][...]
    for n, part in enumerate(parts):
        r_ref[n * size : (n + 1) * size, :] = part[...]
    step = weights[0].shape[0]
    cot = matmul(r_ref[:, :step], weights[0][:, 3 * width :])
    for i in range(1, GROUPS):
        cot += matmul(r_ref[:, i * step : (i + 1) * step], weights[i][:, 3 * width :])
    cot_ref[...] = cot.astype(LOW).astype(WIDE)
    for tile in tiles_of(count, block):
        rows = tile[0][2]
        allowed = allowed_pairs(dims, place_ref, [ks[g] * block + first for g, first, _ in tile], rows)
        queries = rows_of(q_refs, tile).astype(WIDE) * HEAD_DIM**-0.5
        tile_cot = jnp.concatenate([cot_ref[g * block + first : g * block + first + n, :] for g, first, n in tile], axis=0)
        dots = tile_cot * rows_of(out_refs, tile).astype(WIDE)
        tile_lse = rows_of(lse_refs, tile)
        wide = rows * len(tile)

        def one_head(head, grad_q):
            mine = lanes // HEAD_DIM == head
            picked = jnp.where(mine, queries, 0.0).astype(LOW)
            cot_head = jnp.where(mine, tile_cot, 0.0).astype(LOW)
            row_dot = jnp.sum(jnp.where(mine, dots, 0.0), axis=1, keepdims=True)
            lse = jnp.sum(jnp.where(lse_lanes == head, tile_lse, 0.0), axis=1, keepdims=True)
            scores = jnp.where(allowed, over_cols(picked, k_ref[...]), -1e30)
            probs = jnp.exp(scores - lse)
            gv_ref[...] += over_rows(probs.astype(LOW), cot_head)
            grad_probs = over_cols(cot_head, v_ref[...])
            grad_scores = (probs * (grad_probs - row_dot)).astype(LOW)
            gk_ref[...] += over_rows(grad_scores, picked)
            return jnp.where(mine, matmul(grad_scores, k_ref[...]) * HEAD_DIM**-0.5, grad_q)

        grad_q = lax.fori_loop(0, width // HEAD_DIM, one_head, jnp.zeros((wide, width), WIDE))
        low = grad_q.astype(LOW).astype(WIDE)
        cos, sin = widen(rows_of(cos_refs, tile), width), widen(rows_of(sin_refs, tile), width)
        put_rows(gq_refs, tile, (low * cos - partner(low) * sin).astype(LOW))


def attend_back_blocks(at, ks, place, queries, key_rows, val_rows, attended, lse, cos, sin, weights, parts, held):
    total, width = queries.shape
    blks, seqs, count = lax.axis_size("blk"), lax.axis_size("seq"), len(ks)
    size, model = parts[0].shape
    block = total // blks
    rows_at = lambda k, wide: pl.BlockSpec((block, wide), lambda *_: (k, 0))
    whole = vmem((total, width))
    old = [] if held is None else list(held)
    first_old = 1 + count + 2 + 2 * count + 2 * count + 4 + count * seqs
    tables = [rows_at(k, cos.shape[1]) for k in ks]
    got = pl.pallas_call(
        partial(attend_back_kernel, (total, blks, seqs, size), ks, width, held is None),
        grid_spec=pltpu.PrefetchScalarGridSpec(
            num_scalar_prefetch=1,
            grid=(1,),
            in_specs=[rows_at(k, width) for k in ks]
            + [whole] * 2
            + [vmem((block, width))] * count
            + [vmem((block, 128))] * count
            + tables * 2
            + [vmem(w.shape) for w in weights]
            + [vmem((size, model))] * (count * seqs)
            + ([ANY, whole, whole] if old else []),
            out_specs=[pl.BlockSpec((count * block, model), lambda *_: (at, 0)), whole, whole] + [vmem((block, width))] * count,
            scratch_shapes=[pltpu.VMEM((count * block, width), WIDE)],
        ),
        out_shape=[jax.ShapeDtypeStruct((total, model), LOW)]
        + [jax.ShapeDtypeStruct((total, width), WIDE)] * 2
        + [jax.ShapeDtypeStruct((block, width), LOW)] * count,
        input_output_aliases={first_old + i: i for i in range(3)} if old else {},
        compiler_params=params(60),
        cost_estimate=cost(),
        name="attend_back_blocks",
    )(
        place, *[queries] * count, key_rows, val_rows, *[attended[k] for k in ks], *[lse[k] for k in ks],
        *[cos] * count, *[sin] * count, *weights, *parts, *old,
    )
    return got[:3], got[3:]


def finish_kernel(width, count, seqs, *refs):
    def some(number):
        nonlocal refs
        taken, refs = refs[:number], refs[number:]
        return taken

    gq_refs, gk_refs, gv_refs, cos_refs, sin_refs = (some(count) for _ in range(5))
    weights, parts = some(4), some(count * seqs)
    outs, (gain_ref,), terms = some(count), some(1), some(count * seqs)
    size = parts[0].shape[0]
    step = weights[0].shape[0]
    for g, out_ref in enumerate(outs):
        low_k = gk_refs[g][...].astype(LOW).astype(WIDE)
        cos, sin = widen(cos_refs[g][...], width), widen(sin_refs[g][...], width)
        out_ref[:, :width] = gq_refs[g][...]
        out_ref[:, width : 2 * width] = (low_k * cos - partner(low_k) * sin).astype(LOW)
        out_ref[:, 2 * width :] = gv_refs[g][...].astype(LOW)
    grads = jnp.concatenate([ref[...] for ref in outs], axis=0)
    inverses = []
    for part in parts:
        rows = part[...].astype(WIDE)
        inverses.append(lax.rsqrt(jnp.mean(rows * rows, axis=-1, keepdims=True) + EPSILON))
    for i in range(GROUPS):
        here = slice(i * step, (i + 1) * step)
        grad = over_cols(grads, weights[i][:, : 3 * width])
        put_parts(terms, size, i * step, grad.astype(LOW))
        gain = 0.0
        for n, part in enumerate(parts):
            mine = grad[n * size : (n + 1) * size]
            gain += jnp.sum(mine * (part[:, here].astype(WIDE) * inverses[n]), axis=0, keepdims=True)
        gain_ref[:, here] = gain


def finish_blocks(ks, grad_q, grad_k, grad_v, cos, sin, weights, parts):
    count = len(ks)
    total, width = grad_k.shape
    seqs, (size, model) = len(parts) // count, parts[0].shape
    block = size * seqs
    rows_at = lambda k, wide: pl.BlockSpec((block, wide), lambda _: (k, 0))
    tables = [rows_at(k, cos.shape[1]) for k in ks]
    got = pl.pallas_call(
        partial(finish_kernel, width, count, seqs),
        grid=(1,),
        in_specs=[vmem((block, width))] * count
        + [rows_at(k, width) for k in ks] * 2
        + tables * 2
        + [vmem(w.shape) for w in weights]
        + [vmem((size, model))] * (count * seqs),
        out_specs=[vmem((block, 3 * width))] * count + [vmem((1, model))] + [vmem((size, model))] * (count * seqs),
        out_shape=[jax.ShapeDtypeStruct((block, 3 * width), LOW)] * count
        + [jax.ShapeDtypeStruct((1, model), WIDE)]
        + [jax.ShapeDtypeStruct((size, model), LOW)] * (count * seqs),
        compiler_params=params(56),
        cost_estimate=cost(),
        name="finish_blocks",
    )(*[grad_q[k] for k in ks], *[grad_k] * count, *[grad_v] * count, *[cos] * count, *[sin] * count, *weights, *parts)
    return got[:count], got[count], by_block(got[count + 1 :], count)


def weight_kernel(counts, *refs):
    outs = refs[-GROUPS:]
    step = outs[0].shape[0]
    for i, out_ref in enumerate(outs):
        at, column = 0, 0
        for count in counts:
            left_ref, rights = refs[at], refs[at + 1 : at + 1 + count]
            rows, wide = rights[0].shape
            here = slice(i * step, (i + 1) * step)
            total = over_rows(left_ref[:rows, here], rights[0][...])
            for g in range(1, count):
                total += over_rows(left_ref[g * rows : (g + 1) * rows, here], rights[g][...])
            out_ref[:, column : column + wide] = total.astype(LOW)
            at, column = at + 1 + count, column + wide


def weight_terms(*pairs):
    step = pairs[0][0].shape[1] // GROUPS
    cols = sum(rights[0].shape[1] for _, rights in pairs)
    arrays = [a for left, rights in pairs for a in (left, *rights)]
    return pl.pallas_call(
        partial(weight_kernel, [len(rights) for _, rights in pairs]),
        grid=(1,),
        in_specs=[vmem(a.shape) for a in arrays],
        out_specs=[vmem((step, cols))] * GROUPS,
        out_shape=[jax.ShapeDtypeStruct((step, cols), LOW)] * GROUPS,
        compiler_params=params(60),
        cost_estimate=cost(),
        name="weight_terms",
    )(*arrays)


def shards(
    tokens, out_grad, lengths, attn_gain, w_query, w_key, w_value, output_weight, mlp_gain, gate_weight, up_weight, down_weight
):
    seqs, blks = lax.axis_size("seq"), lax.axis_size("blk")
    seq_rank, blk_rank = lax.axis_index("seq"), lax.axis_index("blk")
    size, model = tokens.shape[1], tokens.shape[2]
    block = size * seqs
    total = block * blks
    length = lengths[0]
    width = w_query.shape[1] // blks
    hidden = gate_weight.shape[1] // blks
    positions = (blk_rank * seqs + seq_rank) * size + jnp.arange(size, dtype=jnp.int32)
    live_rows = (positions < length)[:, None]
    place = jnp.stack([blk_rank, seq_rank, length, lax.axis_index("slot")]).astype(jnp.int32)

    cos_wide, sin_wide = rotary_tables(place, total, size, min(width, 128))
    own_tokens = slot_order(tokens[0])
    own_cot = jnp.where(live_rows, slot_order(out_grad[0]), 0)
    gain_attn, gain_mlp = attn_gain.astype(WIDE)[:, None], mlp_gain.astype(WIDE)[:, None]
    rows_f = own_tokens.astype(WIDE)

    def scaled(weight, gain):
        return (weight.astype(WIDE) * gain).astype(LOW)

    attn_out = Exchange(
        column_pieces([scaled(w, gain_attn) for w in (w_query, w_key, w_value)] + [output_weight])
    )
    pair_out = Exchange(column_pieces([scaled(gate_weight, gain_mlp), scaled(up_weight, gain_mlp)], 2))
    down_out = Exchange(column_pieces([down_weight]))
    phase = Phases()
    flat = lambda lists: [item for items in lists for item in items]
    in_order, in_turn = [[0, 1], [2, 3]], [[1, 2], [3, 0]]

    def calls(ks):
        return [ks] if block * len(ks) <= 512 else [[k] for k in ks]

    token_blocks = [None] * blks
    ahead = turn(own_tokens, "blk", 1)
    attn_out.send(1, 2, 3)
    token_blocks[0] = seq_gather(own_tokens)
    phase.end(ahead, attn_out.got, token_blocks[0])

    moving, part_attn, pair_out.pieces = phase.take(ahead, attn_out.by_rank(), pair_out.pieces)
    ahead = turn(moving, "blk", 1)
    near_x, near_y = swap(part_attn, "slot", 1), swap(part_attn, "slot", 2)
    pair_out.send(1)
    phase.end(ahead, near_x, near_y, pair_out.got, cos_wide, sin_wide)

    second, moving, near_x, pair_out.pieces = phase.take(moving, ahead, near_x, pair_out.pieces)
    ahead = turn(moving, "blk", 1)
    far = swap(near_x, "slot", 2)
    pair_out.send(3)
    token_blocks[1], token_blocks[2] = seq_gather(second), seq_gather(moving)
    full_attn = [part_attn, near_x, near_y, far]
    phase.end(ahead, far, token_blocks[1:3], pair_out.got)

    moving, pair_out.pieces = phase.take(ahead, pair_out.pieces)
    token_blocks[3] = seq_gather(moving)
    pair_out.send(2)
    got = []
    for ks in [list(range(blks))] if total <= 1024 else [[k] for k in range(blks)]:
        here = slice(ks[0] * block, (ks[-1] + 1) * block)
        got.append(project_qkv(flat([token_blocks[k] for k in ks]), full_attn, cos_wide[here], sin_wide[here], width))
    hidden_attn, queries, key_rows, val_rows = (
        parts[0] if len(parts) == 1 else jnp.concatenate(parts, axis=0) for parts in zip(*got)
    )
    attended, lse, terms = [None] * blks, [None] * blks, [None] * blks

    def attend(ks, queries):
        for some in calls(ks):
            for k, *got in zip(some, *attend_blocks(some, place, queries, key_rows, val_rows, full_attn, size, model)):
                attended[k], lse[k], terms[k] = got

    attend(in_turn[0], queries)
    phase.end(pair_out.got, terms[1], terms[2])

    queries, pair_out.got, down_out.pieces, terms[1], terms[2] = phase.take(
        queries, pair_out.got, down_out.pieces, terms[1], terms[2]
    )
    part_pair = pair_out.by_rank()
    half_a, half_b = part_pair[:, :hidden], part_pair[:, hidden:]
    near_x, near_y = [swap(half_a, "slot", 1)], [swap(half_a, "slot", 2)]
    terms[1] = seq_reduce(terms[1])
    moving = turn(add_up(terms[1]).astype(LOW), "blk", 1)
    down_out.send(2)
    terms[2] = seq_reduce(terms[2])
    attend(in_turn[1], queries)
    phase.end(moving, terms, near_x, near_y, down_out.got)

    moving, half_b, down_out.pieces, terms[3], terms[0] = phase.take(
        add_up([moving, *terms[2]]).astype(LOW), half_b, down_out.pieces, terms[3], terms[0]
    )
    near_x, near_y = near_x + [swap(half_b, "slot", 1)], near_y + [swap(half_b, "slot", 2)]
    moving = turn(moving, "blk", 1)
    down_out.send(1)
    terms[3] = seq_reduce(terms[3])
    phase.end(moving, terms[3], near_x, near_y, down_out.got)

    moving, far_x, far_y, down_out.pieces, terms[0] = phase.take(
        add_up([moving, *terms[3]]).astype(LOW), near_x[0], near_y[1], down_out.pieces, terms[0]
    )
    moving = turn(moving, "blk", 1)
    down_out.send(3)
    far_a, far_b = swap(far_x, "slot", 2), swap(far_y, "slot", 1)
    terms[0] = seq_reduce(terms[0])
    full_pair = [[half_a, near_x[0], near_y[0], far_a], [half_b, near_x[1], near_y[1], far_b]]
    phase.end(moving, terms[0], down_out.got)
    resid = rows_f + add_up([moving, *terms[0]])
    normed_mlp, inverse_mlp = norm_rows(resid)

    grads_of, outs_of = [None] * blks, [None] * blks

    def feed(ks, held):
        for some in calls(ks):
            held, grads, outs = mlp_blocks(
                some[0] // len(some), seqs, flat([blocks[k] for k in some]), full_pair, full_down, held, total
            )
            for k, grad, out in zip(some, grads, outs):
                grads_of[k], outs_of[k] = grad, out
        return held

    blocks = [None] * blks
    moving, part_down = phase.take(
        jnp.concatenate([normed_mlp.astype(LOW), own_cot], axis=1), down_out.by_rank()
    )
    ahead = turn(moving, "blk", 1)
    near_x, near_y = swap(part_down, "slot", 1), swap(part_down, "slot", 2)
    blocks[0] = seq_gather(moving)
    phase.end(ahead, far_a, far_b, blocks[0])

    moving = phase.take(ahead)
    ahead = turn(moving, "blk", 1)
    cut = hidden // 2
    full_down = [part_down, near_x, near_y, swap(near_x[:, :cut], "slot", 2), swap(near_y[:, cut:], "slot", 1)]
    blocks[1] = seq_gather(moving)
    phase.end(ahead, blocks[1], full_down)

    moving, blocks[0], blocks[1] = phase.take(ahead, blocks[0], blocks[1])
    ahead = turn(moving, "blk", 1)
    blocks[2] = seq_gather(moving)
    held = feed(in_order[0], None)
    phase.end(ahead, blocks[2], held)

    moving, blocks[2], grads_of[:2], outs_of[:2] = phase.take(ahead, blocks[2], grads_of[:2], outs_of[:2])
    grads_of[1] = seq_reduce(grads_of[1])
    blocks[3] = seq_gather(moving)
    grad = turn(add_up(grads_of[1]).astype(LOW), "blk", 1)
    outs_of[1] = seq_reduce(outs_of[1])
    out = turn(add_up(outs_of[1]).astype(LOW), "blk", 1)
    held = feed(in_order[1], held)
    phase.end(grad, out, held)
    hidden_mlp, all_cot, activation, *grad_pair = held

    grad, grads_of[2], outs_of[2], out, activation, grad_pair[1] = phase.take(
        grad, grads_of[2], outs_of[2], out, activation, grad_pair[1]
    )
    grads_of[2], outs_of[2] = seq_reduce(grads_of[2]), seq_reduce(outs_of[2])
    grad = turn(add_up([grad, *grads_of[2]]).astype(LOW), "blk", 1)
    out = turn(add_up([out, *outs_of[2]]).astype(LOW), "blk", 1)
    down_terms = weight_terms((all_cot, [activation]))
    pair_b = weight_terms((hidden_mlp, [grad_pair[1]]))
    phase.end(grad, out, down_terms, pair_b)

    grad, grads_of[3], grads_of[0], far_down, far_b, half = phase.take(
        grad, grads_of[3], grads_of[0], down_terms[3], pair_b[3], grad_pair[0]
    )
    grads_of[3] = seq_reduce(grads_of[3])
    grad = turn(add_up([grad, *grads_of[3]]).astype(LOW), "blk", 1)
    far_down, far_b = swap(far_down, "slot", 1), swap(far_b, "slot", 2)
    grads_of[0] = seq_reduce(grads_of[0])
    pair_a = weight_terms((hidden_mlp, [half]))
    phase.end(grad, grads_of[0], pair_a)
    grad_part = add_up([grad, *grads_of[0]])
    grad_resid_part, gain_mlp_term = norm_back(normed_mlp, inverse_mlp, grad_part)
    grad_resid = own_cot.astype(WIDE) + grad_resid_part

    grad_q = [None] * blks

    def attend_back(ks, held):
        for some in calls(ks):
            held, grads = attend_back_blocks(
                some[0] // len(some), some, place, queries, key_rows, val_rows, attended, lse, cos_wide, sin_wide,
                full_attn, flat([blocks[k] for k in some]), held,
            )
            for k, grad in zip(some, grads):
                grad_q[k] = grad
        return held

    moving, out, outs_of[3], outs_of[0] = phase.take(grad_resid.astype(LOW), out, outs_of[3], outs_of[0])
    ahead = turn(moving, "blk", 1)
    blocks = [seq_gather(moving), None, None, None]
    outs_of[3] = seq_reduce(outs_of[3])
    phase.end(ahead, blocks[0], outs_of[3], far_down, far_b)

    moving, blocks[0], far_down, down_terms, out = phase.take(
        ahead, blocks[0], far_down, down_terms, add_up([out, *outs_of[3]]).astype(LOW)
    )
    ahead = turn(moving, "blk", 1)
    one = swap(add_up([down_terms[2], far_down]).astype(LOW), "slot", 2)
    two = swap(down_terms[1], "slot", 1)
    out = turn(out, "blk", 1)
    blocks[1] = seq_gather(moving)
    held = attend_back(in_order[0], None)
    phase.end(ahead, blocks[1], held)

    moving, far_a = phase.take(ahead, pair_a[3])
    ahead = turn(moving, "blk", 1)
    far_a = swap(far_a, "slot", 1)
    blocks[2] = seq_gather(moving)
    phase.end(ahead, blocks[2], one, two, out)

    moving, blocks[2], two_b, one_b, one, two = phase.take(
        ahead, blocks[2], pair_b[2], add_up([pair_b[1], far_b]).astype(LOW), one, two
    )
    blocks[3] = seq_gather(moving)
    two_b, one_b = swap(two_b, "slot", 2), swap(one_b, "slot", 1)
    held = attend_back(in_order[1], held)
    all_resid, grad_k, grad_v = held
    down_back = Exchange(row_pieces([down_terms[0], one, two]))
    phase.end(held, far_a, down_back.pieces)

    grad_qkv, terms, gain_terms = [None] * blks, [None] * blks, []

    def finish(ks, grad_k):
        for some in calls(ks):
            outs, gain_term, parts = finish_blocks(
                some, grad_q, grad_k, grad_v, cos_wide, sin_wide, full_attn, flat([token_blocks[k] for k in some])
            )
            gain_terms.append(gain_term)
            for k, out, part in zip(some, outs, parts):
                grad_qkv[k], terms[k] = out, part

    grad_k, down_back.pieces, outs_of[0] = phase.take(grad_k, down_back.pieces, outs_of[0])
    down_back.send(1, 2, 3)
    outs_of[0] = seq_reduce(outs_of[0])
    finish(in_turn[0], grad_k)
    finish(in_turn[1], grad_k)
    phase.end(terms, one_b, two_b)

    terms[1] = phase.take(terms[1])
    terms[1] = seq_reduce(terms[1])
    phase.end(terms[1])

    moving, terms[2], grad_qkv, one_a, two_a, one_b, two_b = phase.take(
        add_up(terms[1]).astype(LOW), terms[2], grad_qkv, add_up([pair_a[2], far_a]).astype(LOW), pair_a[1], one_b, two_b
    )
    moving = turn(moving, "blk", 1)
    one_a, two_a = swap(one_a, "slot", 2), swap(two_a, "slot", 1)
    terms[2] = seq_reduce(terms[2])
    last_terms = weight_terms((hidden_attn, grad_qkv), (all_resid, attended))
    gain_terms = jnp.concatenate([add_up(gain_terms), jnp.sum(gain_mlp_term, axis=0, keepdims=True)], axis=0)
    back_b = Exchange(row_pieces([pair_b[0], one_b, two_b]))
    phase.end(moving, terms[2], last_terms, down_back.got, gain_terms, back_b.pieces)

    moving, gain_terms, far, back_b.pieces, terms[3], one_a, two_a = phase.take(
        add_up([moving, *terms[2]]).astype(LOW), gain_terms, last_terms[3], back_b.pieces, terms[3], one_a, two_a
    )
    moving = turn(moving, "blk", 1)
    far = swap(far, "slot", 2)
    back_b.send(1, 3)
    bit = 1
    while bit < seqs:
        gain_terms = gain_terms + swap(gain_terms, "seq", bit)
        bit *= 2
    terms[3] = seq_reduce(terms[3])
    back_a = Exchange(row_pieces([pair_a[0], one_a, two_a]))
    phase.end(moving, far, terms[3], back_b.got, back_a.pieces, gain_terms)

    gain_parts = jnp.split(gain_terms, GROUPS, axis=1)
    moving, relay, near_term, back_a.pieces, back_b.pieces, terms[0], gain_far, gain_two = phase.take(
        add_up([moving, *terms[3]]).astype(LOW), add_up([last_terms[1], far]).astype(LOW), last_terms[2],
        back_a.pieces, back_b.pieces, terms[0], gain_parts[3], gain_parts[1],
    )
    gain_far, gain_two = swap(gain_far, "slot", 1), swap(gain_two, "slot", 1)
    moving = turn(moving, "blk", 1)
    one, two = swap(relay, "slot", 1), swap(near_term, "slot", 2)
    back_b.send(2)
    phase.end(moving, one, two, back_b.got, gain_far, gain_two)

    last_back = Exchange(row_pieces([last_terms[0], one, two]))
    gain_relay, last_back.pieces, back_a.pieces, terms[0] = phase.take(
        gain_parts[2] + gain_far, last_back.pieces, back_a.pieces, terms[0]
    )
    back_a.send(1, 2, 3)
    terms[0] = seq_reduce(terms[0])
    last_back.send(1, 2, 3)
    gain_one = swap(gain_relay, "slot", 2)
    gain_sum = after(gain_parts[0] + gain_two + gain_one, back_a.got[1])
    gain_sums = [gain_sum] + [turn(gain_sum, "blk", k) for k in range(1, blks)]

    layer_out = jnp.where(live_rows, resid + add_up([out, *outs_of[0]]), 0.0)
    grad_hidden_attn = add_up([moving, *terms[0]])
    normed_attn, inverse_attn = norm_rows(rows_f)
    grad_in_part, _ = norm_back(normed_attn, inverse_attn, grad_hidden_attn)
    shard = attn_gain.shape[0]
    gain_grads = lax.dynamic_slice(add_up(gain_sums), (0, blk_rank * shard), (2, shard))
    half = hidden // 2
    return (
        slot_order(layer_out).astype(LOW)[None],
        slot_order(grad_resid + grad_in_part)[None],
        gain_grads[0] / gain_attn[:, 0],
        join_owners([last_back], [(0, width)], gain_attn),
        join_owners([last_back], [(width, width)], gain_attn),
        join_owners([last_back], [(2 * width, width)], gain_attn),
        join_owners([last_back], [(3 * width, width)], 1.0),
        gain_grads[1] / gain_mlp[:, 0],
        join_owners([back_a, back_b], [(0, half)], gain_mlp),
        join_owners([back_a, back_b], [(half, half)], gain_mlp),
        join_owners([down_back], [(0, hidden)], 1.0),
    )


def solution(mesh):
    rows = P("slot", ("blk", "seq"), None)
    gain = P(("slot", "blk"))
    weight = P(("slot", "blk"), "seq")
    return jax.shard_map(
        shards,
        mesh=mesh,
        in_specs=(rows, rows, P("slot"), gain, weight, weight, weight, weight, gain, weight, weight, weight),
        out_specs=(rows, rows, gain, weight, weight, weight, weight, gain, weight, weight, weight),
        check_vma=False,
    )
```

```python
import math
from functools import partial

import jax
import jax.numpy as jnp
from jax import lax
from jax.experimental import pallas as pl
from jax.experimental.pallas import tpu as pltpu
from jax.sharding import PartitionSpec as P

HEADS = 32
HEAD_DIM = 64
HALF = HEAD_DIM // 2
EPSILON = 1e-05
ROPE_BASE = 130000.0
LOW = jnp.bfloat16
WIDE = jnp.float32
GROUPS = 4
ANY = pl.BlockSpec(memory_space=pl.ANY)


def turn(value, axis, by):
    count = lax.axis_size(axis)
    return lax.ppermute(value, axis, [(i, (i + by) % count) for i in range(count)])


def swap(value, axis, mask):
    count = lax.axis_size(axis)
    return lax.ppermute(value, axis, [(i, i ^ mask) for i in range(count)])


def after(value, *others):
    return lax.optimization_barrier((value, *others))[0]


def matmul(left, right):
    return jnp.dot(left, right, preferred_element_type=WIDE)


def over_rows(left, right):
    return lax.dot_general(left, right, (((0,), (0,)), ((), ())), preferred_element_type=WIDE)


def over_cols(left, right):
    return lax.dot_general(left, right, (((1,), (1,)), ((), ())), preferred_element_type=WIDE)


def slot_order(array):
    rank = lax.axis_index("slot")
    parts = jnp.split(array, GROUPS, axis=-1)
    for bit in (1, 2):
        flip = (rank & bit) != 0
        parts = [jnp.where(flip, parts[i ^ bit], parts[i]) for i in range(GROUPS)]
    return jnp.concatenate(parts, axis=-1)


def seq_gather(rows):
    count = lax.axis_size("seq")
    held = [rows]
    bit = 1
    while bit < count:
        held = held + [swap(part, "seq", bit) for part in held]
        bit *= 2
    return held


def seq_reduce(parts):
    bit = lax.axis_size("seq") // 2
    parts = [[part] for part in parts]
    while bit >= 1:
        kept = parts[:bit]
        for mine, other in zip(kept, parts[bit:]):
            mine.append(swap(add_up(other).astype(LOW), "seq", bit))
        parts = kept
        bit //= 2
    return parts[0]


def add_up(summands):
    total = summands[0]
    for summand in summands[1:]:
        total = total.astype(WIDE) + summand.astype(WIDE)
    return total


class Phases:
    def __init__(self):
        self.ended = ()

    def take(self, *values):
        values = tuple(values)
        if self.ended:
            values = lax.optimization_barrier((values, self.ended))[0]
        return values[0] if len(values) == 1 else values

    def end(self, *values):
        self.ended = values


class Exchange:
    def __init__(self, pieces):
        self.pieces = pieces
        self.got = {0: pieces[0]}

    def send(self, *steps):
        for k in steps:
            self.got[k] = turn(self.pieces[k], "blk", k)
        return [self.got[k] for k in steps]

    def by_rank(self, columns=slice(None)):
        blks, rank = lax.axis_size("blk"), lax.axis_index("blk")
        parts = [self.got[k][:, columns] for k in range(blks)]
        rows, cols = parts[0].shape
        full = jnp.zeros((blks * rows, cols), parts[0].dtype)
        for k in range(blks):
            full = lax.dynamic_update_slice(full, parts[k], ((rank - k) % blks * rows, 0))
        return full


def column_pieces(arrays, parts=1):
    blks, rank = lax.axis_size("blk"), lax.axis_index("blk")

    def cut(array, owner, part):
        width = array.shape[1] // (blks * parts)
        return lax.dynamic_slice(array, (0, (owner * parts + part) * width), (array.shape[0], width))

    return [
        jnp.concatenate([cut(a, (rank + k) % blks, part) for part in range(parts) for a in arrays], axis=1)
        for k in range(blks)
    ]


def row_pieces(summands):
    blks, rank = lax.axis_size("blk"), lax.axis_index("blk")
    rows = summands[0].shape[0] // blks

    def cut(owner):
        parts = [lax.dynamic_slice(s, (owner * rows, 0), (rows, s.shape[1])) for s in summands]
        return add_up(parts).astype(LOW)

    return [cut((rank + k) % blks) for k in range(blks)]


def join_owners(exchanges, cuts, scale):
    blks, rank = lax.axis_size("blk"), lax.axis_index("blk")
    wide = sum(width for _, width in cuts)
    out = jnp.zeros((exchanges[0].got[0].shape[0], blks * wide * len(exchanges)), WIDE)
    for n, exchanged in enumerate(exchanges):
        for k in range(blks):
            first = ((rank - k) % blks * len(exchanges) + n) * wide
            for at, width in cuts:
                part = exchanged.got[k][:, at : at + width].astype(WIDE) * scale
                out = lax.dynamic_update_slice(out, part, (0, first))
                first = first + width
    return out


def norm_rows(rows):
    inverse = lax.rsqrt(jnp.mean(rows * rows, axis=-1, keepdims=True) + EPSILON)
    return rows * inverse, inverse


def norm_back(normed, inverse, upstream):
    product = upstream * normed
    return inverse * (upstream - normed * jnp.mean(product, axis=-1, keepdims=True)), product


def vmem(shape):
    return pl.BlockSpec(shape, lambda *_: (0,) * len(shape))


def params(mebibytes):
    return pltpu.CompilerParams(vmem_limit_bytes=mebibytes << 20)


def cost():
    return pl.CostEstimate(flops=1, bytes_accessed=1, transcendentals=0)


def partner(vectors):
    width = vectors.shape[1]
    if width % 128 == 0:
        lanes = lax.broadcasted_iota(jnp.int32, (1, width), 1)
        ahead = pltpu.roll(vectors, width - HALF, 1)
        behind = pltpu.roll(vectors, HALF, 1)
        return jnp.where(lanes % HEAD_DIM < HALF, ahead, behind)
    parts = []
    for first in range(0, width, HEAD_DIM):
        parts += [vectors[:, first + HALF : first + HEAD_DIM], vectors[:, first : first + HALF]]
    return jnp.concatenate(parts, axis=1)


def table_kernel(dims, place_ref, cos_ref, sin_ref):
    total, blks, seqs, size = dims
    wide = cos_ref.shape[1]
    index = lax.broadcasted_iota(jnp.int32, (total, 1), 0)
    position = row_positions(index, place_ref[0], place_ref[1], blks, seqs, size).astype(WIDE)
    lane = lax.broadcasted_iota(jnp.int32, (1, wide), 1)
    power = (lane % HALF).astype(WIDE) * (-2.0 / HEAD_DIM)
    angle = position * jnp.exp(power * math.log(ROPE_BASE))
    cos_ref[...] = jnp.cos(angle)
    sin_ref[...] = jnp.where(lane % HEAD_DIM < HALF, -jnp.sin(angle), jnp.sin(angle))


def rotary_tables(place, total, size, wide):
    dims = (total, lax.axis_size("blk"), lax.axis_size("seq"), size)
    return pl.pallas_call(
        partial(table_kernel, dims),
        grid_spec=pltpu.PrefetchScalarGridSpec(
            num_scalar_prefetch=1, grid=(1,), in_specs=[], out_specs=[vmem((total, wide))] * 2
        ),
        out_shape=[jax.ShapeDtypeStruct((total, wide), WIDE)] * 2,
        compiler_params=params(32),
        cost_estimate=cost(),
        name="rotary_tables",
    )(place)


def widen(table, width):
    return table if table.shape[1] == width else jnp.concatenate([table] * (width // table.shape[1]), axis=1)


def qkv_kernel(width, *refs):
    parts, weights, (cos_ref, sin_ref) = refs[:-10], refs[-10:-6], refs[-6:-4]
    h_ref, q_ref, k_ref, v_ref = refs[-4:]
    size, model = parts[0].shape
    step = model // GROUPS
    for n, part in enumerate(parts):
        normed, _ = norm_rows(part[...].astype(WIDE))
        h_ref[n * size : (n + 1) * size, :] = normed.astype(LOW)
    total = h_ref.shape[0]
    rows = min(512, total)

    def some(first):
        here = slice(first, first + rows)
        pre = matmul(h_ref[here, :step], weights[0][:, : 3 * width])
        for i in range(1, GROUPS):
            pre += matmul(h_ref[here, i * step : (i + 1) * step], weights[i][:, : 3 * width])
        cos, sin = widen(cos_ref[here, :], width), widen(sin_ref[here, :], width)
        for at, out_ref in ((0, q_ref), (1, k_ref)):
            half = pre[:, at * width : (at + 1) * width]
            out_ref[here, :] = (half * cos + partner(half) * sin).astype(LOW)
        v_ref[here, :] = pre[:, 2 * width :].astype(LOW)

    for first in range(0, total, rows):
        some(first)


def project_qkv(parts, weights, cos, sin, width):
    size, model = parts[0].shape
    total = size * len(parts)
    return pl.pallas_call(
        partial(qkv_kernel, width),
        grid=(1,),
        in_specs=[vmem((size, model))] * len(parts) + [vmem(w.shape) for w in weights] + [vmem(cos.shape)] * 2,
        out_specs=[vmem((total, model))] + [vmem((total, width))] * 3,
        out_shape=[jax.ShapeDtypeStruct((total, model), LOW)] + [jax.ShapeDtypeStruct((total, width), LOW)] * 3,
        compiler_params=params(60),
        cost_estimate=cost(),
        name="project_qkv",
    )(*parts, *weights, cos, sin)


def row_positions(index, blk_rank, seq_rank, blks, seqs, size):
    sub = index // size
    k, m = sub // seqs, sub % seqs
    return ((blk_rank - k + blks) % blks * seqs + (seq_rank ^ m)) * size + index % size


def allowed_pairs(dims, place_ref, firsts, rows):
    total, blks, seqs, size = dims
    blk_rank, seq_rank, length = place_ref[0], place_ref[1], place_ref[2]
    k_index = lax.broadcasted_iota(jnp.int32, (1, total), 1)
    k_pos = row_positions(k_index, blk_rank, seq_rank, blks, seqs, size)
    k_pos = jnp.where(k_pos < length, k_pos, jnp.int32(1 << 30))
    index = lax.broadcasted_iota(jnp.int32, (rows, 1), 0)
    q_pos = [row_positions(first + index, blk_rank, seq_rank, blks, seqs, size) for first in firsts]
    return k_pos <= jnp.concatenate(q_pos, axis=0)


def tiles_of(count, block):
    if count * block <= 512:
        return [[(g, 0, block) for g in range(count)]]
    rows = min(256, block)
    return [[(g, first, rows)] for g in range(count) for first in range(0, block, rows)]


def rows_of(refs, tile):
    return jnp.concatenate([refs[g][first : first + rows, :] for g, first, rows in tile], axis=0)


def put_rows(refs, tile, value):
    at = 0
    for g, first, rows in tile:
        refs[g][first : first + rows, :] = value[at : at + rows]
        at += rows


def put_parts(terms, size, column, value):
    for n, term in enumerate(terms):
        term[:, column : column + value.shape[1]] = value[n * size : (n + 1) * size]


def by_block(terms, count):
    some = len(terms) // count
    return [terms[g * some : (g + 1) * some] for g in range(count)]


def attend_kernel(dims, ks, width, place_ref, *refs):
    count, seqs = len(ks), dims[2]
    q_refs, (k_ref, v_ref), weights = refs[:count], refs[count : count + 2], refs[count + 2 : count + 6]
    out_refs, lse_refs, terms = refs[count + 6 : 2 * count + 6], refs[2 * count + 6 : 3 * count + 6], refs[3 * count + 6 :]
    block = q_refs[0].shape[0]
    lanes = lax.broadcasted_iota(jnp.int32, (1, width), 1)
    lse_lanes = lax.broadcasted_iota(jnp.int32, (1, 128), 1)
    for tile in tiles_of(count, block):
        rows = tile[0][2]
        allowed = allowed_pairs(dims, place_ref, [ks[g] * block + first for g, first, _ in tile], rows)
        queries = rows_of(q_refs, tile).astype(WIDE) * HEAD_DIM**-0.5
        wide = rows * len(tile)

        def one_head(head, carried):
            out, lse = carried
            mine = lanes // HEAD_DIM == head
            picked = jnp.where(mine, queries, 0.0).astype(LOW)
            scores = jnp.where(allowed, over_cols(picked, k_ref[...]), -1e30)
            top = jnp.max(scores, axis=1, keepdims=True)
            probs = jnp.exp(scores - top)
            weight = jnp.sum(probs, axis=1, keepdims=True)
            mixed = matmul(probs.astype(LOW), v_ref[...]) / weight
            return jnp.where(mine, mixed, out), jnp.where(lse_lanes == head, top + jnp.log(weight), lse)

        out, lse = lax.fori_loop(
            0, width // HEAD_DIM, one_head, (jnp.zeros((wide, width), WIDE), jnp.zeros((wide, 128), WIDE))
        )
        put_rows(out_refs, tile, out.astype(LOW))
        put_rows(lse_refs, tile, lse)
    attended = jnp.concatenate([ref[...] for ref in out_refs], axis=0)
    for i, weight in enumerate(weights):
        step = weight.shape[0]
        put_parts(terms, block // seqs, i * step, over_cols(attended, weight[:, 3 * width :]).astype(LOW))


def attend_blocks(ks, place, queries, key_rows, val_rows, weights, size, model):
    total, width = queries.shape
    blks, seqs, count = lax.axis_size("blk"), lax.axis_size("seq"), len(ks)
    block = total // blks
    rows_at = lambda k, wide: pl.BlockSpec((block, wide), lambda *_: (k, 0))
    got = pl.pallas_call(
        partial(attend_kernel, (total, blks, seqs, size), ks, width),
        grid_spec=pltpu.PrefetchScalarGridSpec(
            num_scalar_prefetch=1,
            grid=(1,),
            in_specs=[rows_at(k, width) for k in ks] + [vmem((total, width))] * 2 + [vmem(w.shape) for w in weights],
            out_specs=[vmem((block, width))] * count + [vmem((block, 128))] * count + [vmem((size, model))] * (count * seqs),
        ),
        out_shape=[jax.ShapeDtypeStruct((block, width), LOW)] * count
        + [jax.ShapeDtypeStruct((block, 128), WIDE)] * count
        + [jax.ShapeDtypeStruct((size, model), LOW)] * (count * seqs),
        compiler_params=params(56),
        cost_estimate=cost(),
        name="attend_blocks",
    )(place, *[queries] * count, key_rows, val_rows, *weights)
    return got[:count], got[count : 2 * count], by_block(got[2 * count :], count)


def mlp_kernel(count, *refs):
    parts, pairs, down = refs[:count], (refs[count : count + 4], refs[count + 4 : count + 8]), refs[count + 8 : count + 13]
    outs = refs[-5 - 2 * count :]
    h_ref, c_ref, act_ref, pair_refs = outs[0], outs[1], outs[2], outs[3:5]
    grad_terms, out_terms = outs[5 : 5 + count], outs[5 + count :]
    size, model = parts[0].shape[0], h_ref.shape[1]
    step, hidden = model // GROUPS, down[0].shape[1] // 2
    groups = [slice(i * step, (i + 1) * step) for i in range(GROUPS)]
    for m in range(count):
        rows = slice(m * size, (m + 1) * size)
        h_ref[rows, :] = parts[m][:, :model]
        c_ref[rows, :] = parts[m][:, model:]
    down_half = lambda i, j: down[i][:, j * hidden : (j + 1) * hidden] if i < 3 else down[3 + j][...]
    for j, pair_ref in enumerate(pair_refs):
        half = slice(j * hidden, (j + 1) * hidden)
        both = matmul(h_ref[:, groups[0]], pairs[j][0][...])
        grad_act = matmul(c_ref[:, groups[0]], down_half(0, j))
        for i in range(1, GROUPS):
            both += matmul(h_ref[:, groups[i]], pairs[j][i][...])
            grad_act += matmul(c_ref[:, groups[i]], down_half(i, j))
        gate, up = both[:, :hidden], both[:, hidden:]
        sig = jax.nn.sigmoid(gate)
        act_ref[:, half] = (gate * sig * up).astype(LOW)
        pair_ref[:, :hidden] = (grad_act * up * sig * (1.0 + gate * (1.0 - sig))).astype(LOW)
        pair_ref[:, hidden:] = (grad_act * gate * sig).astype(LOW)
    for i in range(GROUPS):
        grad = over_cols(pair_refs[0][...], pairs[0][i][...]) + over_cols(pair_refs[1][...], pairs[1][i][...])
        put_parts(grad_terms, size, i * step, grad.astype(LOW))
        if i < 3:
            out = over_cols(act_ref[...], down[i][...])
        else:
            out = over_cols(act_ref[:, :hidden], down[3][...]) + over_cols(act_ref[:, hidden:], down[4][...])
        put_parts(out_terms, size, i * step, out.astype(LOW))


def mlp_blocks(at, seqs, parts, pairs, down, held, total):
    count, (size, model) = len(parts), (parts[0].shape[0], parts[0].shape[1] // 2)
    hidden = down[0].shape[1]
    rows = count * size
    old = [] if held is None else list(held)
    widths = [model, model, hidden, hidden, hidden]
    got = pl.pallas_call(
        partial(mlp_kernel, count),
        grid=(1,),
        in_specs=[vmem((size, 2 * model))] * count
        + [vmem(w.shape) for w in (*pairs[0], *pairs[1], *down)]
        + [ANY] * len(old),
        out_specs=[pl.BlockSpec((rows, wide), lambda _: (at, 0)) for wide in widths] + [vmem((size, model))] * (2 * count),
        out_shape=[jax.ShapeDtypeStruct((total, wide), LOW) for wide in widths]
        + [jax.ShapeDtypeStruct((size, model), LOW)] * (2 * count),
        input_output_aliases={count + 13 + i: i for i in range(5)} if old else {},
        compiler_params=params(60),
        cost_estimate=cost(),
        name="mlp_blocks",
    )(*parts, *pairs[0], *pairs[1], *down, *old)
    return got[:5], by_block(got[5 : 5 + count], count // seqs), by_block(got[5 + count :], count // seqs)


def attend_back_kernel(dims, ks, width, fresh, place_ref, *refs):
    count, seqs = len(ks), dims[2]

    def some(number):
        nonlocal refs
        taken, refs = refs[:number], refs[number:]
        return taken

    q_refs, (k_ref, v_ref), out_refs, lse_refs = some(count), some(2), some(count), some(count)
    cos_refs, sin_refs, weights, parts = some(count), some(count), some(4), some(count * seqs)
    old = [] if fresh else some(3)
    (r_ref, gk_ref, gv_ref), gq_refs, (cot_ref,) = some(3), some(count), some(1)
    block = q_refs[0].shape[0]
    size = block // seqs
    lanes = lax.broadcasted_iota(jnp.int32, (1, width), 1)
    lse_lanes = lax.broadcasted_iota(jnp.int32, (1, 128), 1)
    gk_ref[...] = jnp.zeros_like(gk_ref) if fresh else old[1][...]
    gv_ref[...] = jnp.zeros_like(gv_ref) if fresh else old[2][...]
    for n, part in enumerate(parts):
        r_ref[n * size : (n + 1) * size, :] = part[...]
    step = weights[0].shape[0]
    cot = matmul(r_ref[:, :step], weights[0][:, 3 * width :])
    for i in range(1, GROUPS):
        cot += matmul(r_ref[:, i * step : (i + 1) * step], weights[i][:, 3 * width :])
    cot_ref[...] = cot.astype(LOW).astype(WIDE)
    for tile in tiles_of(count, block):
        rows = tile[0][2]
        allowed = allowed_pairs(dims, place_ref, [ks[g] * block + first for g, first, _ in tile], rows)
        queries = rows_of(q_refs, tile).astype(WIDE) * HEAD_DIM**-0.5
        tile_cot = jnp.concatenate([cot_ref[g * block + first : g * block + first + n, :] for g, first, n in tile], axis=0)
        dots = tile_cot * rows_of(out_refs, tile).astype(WIDE)
        tile_lse = rows_of(lse_refs, tile)
        wide = rows * len(tile)

        def one_head(head, grad_q):
            mine = lanes // HEAD_DIM == head
            picked = jnp.where(mine, queries, 0.0).astype(LOW)
            cot_head = jnp.where(mine, tile_cot, 0.0).astype(LOW)
            row_dot = jnp.sum(jnp.where(mine, dots, 0.0), axis=1, keepdims=True)
            lse = jnp.sum(jnp.where(lse_lanes == head, tile_lse, 0.0), axis=1, keepdims=True)
            scores = jnp.where(allowed, over_cols(picked, k_ref[...]), -1e30)
            probs = jnp.exp(scores - lse)
            gv_ref[...] += over_rows(probs.astype(LOW), cot_head)
            grad_probs = over_cols(cot_head, v_ref[...])
            grad_scores = (probs * (grad_probs - row_dot)).astype(LOW)
            gk_ref[...] += over_rows(grad_scores, picked)
            return jnp.where(mine, matmul(grad_scores, k_ref[...]) * HEAD_DIM**-0.5, grad_q)

        grad_q = lax.fori_loop(0, width // HEAD_DIM, one_head, jnp.zeros((wide, width), WIDE))
        low = grad_q.astype(LOW).astype(WIDE)
        cos, sin = widen(rows_of(cos_refs, tile), width), widen(rows_of(sin_refs, tile), width)
        put_rows(gq_refs, tile, (low * cos - partner(low) * sin).astype(LOW))


def attend_back_blocks(at, ks, place, queries, key_rows, val_rows, attended, lse, cos, sin, weights, parts, held):
    total, width = queries.shape
    blks, seqs, count = lax.axis_size("blk"), lax.axis_size("seq"), len(ks)
    size, model = parts[0].shape
    block = total // blks
    rows_at = lambda k, wide: pl.BlockSpec((block, wide), lambda *_: (k, 0))
    whole = vmem((total, width))
    old = [] if held is None else list(held)
    first_old = 1 + count + 2 + 2 * count + 2 * count + 4 + count * seqs
    tables = [rows_at(k, cos.shape[1]) for k in ks]
    got = pl.pallas_call(
        partial(attend_back_kernel, (total, blks, seqs, size), ks, width, held is None),
        grid_spec=pltpu.PrefetchScalarGridSpec(
            num_scalar_prefetch=1,
            grid=(1,),
            in_specs=[rows_at(k, width) for k in ks]
            + [whole] * 2
            + [vmem((block, width))] * count
            + [vmem((block, 128))] * count
            + tables * 2
            + [vmem(w.shape) for w in weights]
            + [vmem((size, model))] * (count * seqs)
            + ([ANY, whole, whole] if old else []),
            out_specs=[pl.BlockSpec((count * block, model), lambda *_: (at, 0)), whole, whole] + [vmem((block, width))] * count,
            scratch_shapes=[pltpu.VMEM((count * block, width), WIDE)],
        ),
        out_shape=[jax.ShapeDtypeStruct((total, model), LOW)]
        + [jax.ShapeDtypeStruct((total, width), WIDE)] * 2
        + [jax.ShapeDtypeStruct((block, width), LOW)] * count,
        input_output_aliases={first_old + i: i for i in range(3)} if old else {},
        compiler_params=params(60),
        cost_estimate=cost(),
        name="attend_back_blocks",
    )(
        place, *[queries] * count, key_rows, val_rows, *[attended[k] for k in ks], *[lse[k] for k in ks],
        *[cos] * count, *[sin] * count, *weights, *parts, *old,
    )
    return got[:3], got[3:]


def finish_kernel(width, count, seqs, *refs):
    def some(number):
        nonlocal refs
        taken, refs = refs[:number], refs[number:]
        return taken

    gq_refs, gk_refs, gv_refs, cos_refs, sin_refs = (some(count) for _ in range(5))
    weights, normed = some(4), some(count)
    outs, (gain_ref,), terms = some(count), some(1), some(count * seqs)
    size = terms[0].shape[0]
    step = weights[0].shape[0]
    for g, out_ref in enumerate(outs):
        low_k = gk_refs[g][...].astype(LOW).astype(WIDE)
        cos, sin = widen(cos_refs[g][...], width), widen(sin_refs[g][...], width)
        out_ref[:, :width] = gq_refs[g][...]
        out_ref[:, width : 2 * width] = (low_k * cos - partner(low_k) * sin).astype(LOW)
        out_ref[:, 2 * width :] = gv_refs[g][...].astype(LOW)
    grads = jnp.concatenate([ref[...] for ref in outs], axis=0)
    for i in range(GROUPS):
        here = slice(i * step, (i + 1) * step)
        grad = over_cols(grads, weights[i][:, : 3 * width])
        put_parts(terms, size, i * step, grad.astype(LOW))
        rows = jnp.concatenate([ref[:, here] for ref in normed], axis=0).astype(WIDE)
        gain_ref[:, here] = jnp.sum(grad * rows, axis=0, keepdims=True)


def finish_blocks(ks, seqs, grad_q, grad_k, grad_v, cos, sin, weights, normed):
    count = len(ks)
    total, width = grad_k.shape
    model = normed.shape[1]
    block = total // lax.axis_size("blk")
    size = block // seqs
    rows_at = lambda k, wide: pl.BlockSpec((block, wide), lambda _: (k, 0))
    tables = [rows_at(k, cos.shape[1]) for k in ks]
    got = pl.pallas_call(
        partial(finish_kernel, width, count, seqs),
        grid=(1,),
        in_specs=[vmem((block, width))] * count
        + [rows_at(k, width) for k in ks] * 2
        + tables * 2
        + [vmem(w.shape) for w in weights]
        + [rows_at(k, model) for k in ks],
        out_specs=[vmem((block, 3 * width))] * count + [vmem((1, model))] + [vmem((size, model))] * (count * seqs),
        out_shape=[jax.ShapeDtypeStruct((block, 3 * width), LOW)] * count
        + [jax.ShapeDtypeStruct((1, model), WIDE)]
        + [jax.ShapeDtypeStruct((size, model), LOW)] * (count * seqs),
        compiler_params=params(56),
        cost_estimate=cost(),
        name="finish_blocks",
    )(*[grad_q[k] for k in ks], *[grad_k] * count, *[grad_v] * count, *[cos] * count, *[sin] * count, *weights, *[normed] * count)
    return got[:count], got[count], by_block(got[count + 1 :], count)


def weight_kernel(counts, *refs):
    outs = refs[-GROUPS:]
    step = outs[0].shape[0]
    for i, out_ref in enumerate(outs):
        at, column = 0, 0
        for count in counts:
            left_ref, rights = refs[at], refs[at + 1 : at + 1 + count]
            rows, wide = rights[0].shape
            here = slice(i * step, (i + 1) * step)
            total = over_rows(left_ref[:rows, here], rights[0][...])
            for g in range(1, count):
                total += over_rows(left_ref[g * rows : (g + 1) * rows, here], rights[g][...])
            out_ref[:, column : column + wide] = total.astype(LOW)
            at, column = at + 1 + count, column + wide


def weight_terms(*pairs):
    step = pairs[0][0].shape[1] // GROUPS
    cols = sum(rights[0].shape[1] for _, rights in pairs)
    arrays = [a for left, rights in pairs for a in (left, *rights)]
    return pl.pallas_call(
        partial(weight_kernel, [len(rights) for _, rights in pairs]),
        grid=(1,),
        in_specs=[vmem(a.shape) for a in arrays],
        out_specs=[vmem((step, cols))] * GROUPS,
        out_shape=[jax.ShapeDtypeStruct((step, cols), LOW)] * GROUPS,
        compiler_params=params(60),
        cost_estimate=cost(),
        name="weight_terms",
    )(*arrays)


def shards(
    tokens, out_grad, lengths, attn_gain, w_query, w_key, w_value, output_weight, mlp_gain, gate_weight, up_weight, down_weight
):
    seqs, blks = lax.axis_size("seq"), lax.axis_size("blk")
    seq_rank, blk_rank = lax.axis_index("seq"), lax.axis_index("blk")
    size, model = tokens.shape[1], tokens.shape[2]
    block = size * seqs
    total = block * blks
    length = lengths[0]
    width = w_query.shape[1] // blks
    hidden = gate_weight.shape[1] // blks
    positions = (blk_rank * seqs + seq_rank) * size + jnp.arange(size, dtype=jnp.int32)
    live_rows = (positions < length)[:, None]
    place = jnp.stack([blk_rank, seq_rank, length, lax.axis_index("slot")]).astype(jnp.int32)

    cos_wide, sin_wide = rotary_tables(place, total, size, min(width, 128))
    own_tokens = slot_order(tokens[0])
    own_cot = jnp.where(live_rows, slot_order(out_grad[0]), 0)
    gain_attn, gain_mlp = attn_gain.astype(WIDE)[:, None], mlp_gain.astype(WIDE)[:, None]
    rows_f = own_tokens.astype(WIDE)

    def scaled(weight, gain):
        return (weight.astype(WIDE) * gain).astype(LOW)

    attn_out = Exchange(
        column_pieces([scaled(w, gain_attn) for w in (w_query, w_key, w_value)] + [output_weight])
    )
    pair_out = Exchange(column_pieces([scaled(gate_weight, gain_mlp), scaled(up_weight, gain_mlp)], 2))
    down_out = Exchange(column_pieces([down_weight]))
    phase = Phases()
    flat = lambda lists: [item for items in lists for item in items]
    in_order, in_turn = [[0, 1], [2, 3]], [[1, 2], [3, 0]]

    def calls(ks, most=512):
        return [ks] if block * len(ks) <= most else [[k] for k in ks]

    token_blocks = [None] * blks
    ahead = turn(own_tokens, "blk", 1)
    attn_out.send(1, 2, 3)
    token_blocks[0] = seq_gather(own_tokens)
    phase.end(ahead, attn_out.got, token_blocks[0])

    moving, part_attn, pair_out.pieces = phase.take(ahead, attn_out.by_rank(), pair_out.pieces)
    ahead = turn(moving, "blk", 1)
    near_x, near_y = swap(part_attn, "slot", 1), swap(part_attn, "slot", 2)
    pair_out.send(1)
    phase.end(ahead, near_x, near_y, pair_out.got, pair_out.pieces, down_out.pieces, cos_wide, sin_wide)

    second, moving, near_x, pair_out.pieces = phase.take(moving, ahead, near_x, pair_out.pieces)
    ahead = turn(moving, "blk", 1)
    far = swap(near_x, "slot", 2)
    pair_out.send(3)
    token_blocks[1], token_blocks[2] = seq_gather(second), seq_gather(moving)
    full_attn = [part_attn, near_x, near_y, far]
    phase.end(ahead, far, token_blocks[1:3], pair_out.got)

    moving, pair_out.pieces = phase.take(ahead, pair_out.pieces)
    token_blocks[3] = seq_gather(moving)
    pair_out.send(2)
    got = []
    for ks in [list(range(blks))] if total <= 1024 else [[k] for k in range(blks)]:
        here = slice(ks[0] * block, (ks[-1] + 1) * block)
        got.append(project_qkv(flat([token_blocks[k] for k in ks]), full_attn, cos_wide[here], sin_wide[here], width))
    hidden_attn, queries, key_rows, val_rows = (
        parts[0] if len(parts) == 1 else jnp.concatenate(parts, axis=0) for parts in zip(*got)
    )
    attended, lse, terms = [None] * blks, [None] * blks, [None] * blks

    def attend(ks, queries):
        for some in calls(ks):
            for k, *got in zip(some, *attend_blocks(some, place, queries, key_rows, val_rows, full_attn, size, model)):
                attended[k], lse[k], terms[k] = got

    attend(in_turn[0], queries)
    phase.end(pair_out.got, terms[1], terms[2])

    queries, pair_out.got, down_out.pieces, terms[1], terms[2] = phase.take(
        queries, pair_out.got, down_out.pieces, terms[1], terms[2]
    )
    half_a = pair_out.by_rank(slice(0, hidden))
    near_x, near_y = [swap(half_a, "slot", 1)], [swap(half_a, "slot", 2)]
    terms[1] = seq_reduce(terms[1])
    moving = turn(add_up(terms[1]).astype(LOW), "blk", 1)
    down_out.send(2)
    terms[2] = seq_reduce(terms[2])
    attend(in_turn[1], queries)
    phase.end(moving, terms, near_x, near_y, down_out.got)

    half_b = pair_out.by_rank(slice(hidden, None))
    moving, half_b, down_out.pieces, terms[3], terms[0] = phase.take(
        add_up([moving, *terms[2]]).astype(LOW), half_b, down_out.pieces, terms[3], terms[0]
    )
    near_x, near_y = near_x + [swap(half_b, "slot", 1)], near_y + [swap(half_b, "slot", 2)]
    moving = turn(moving, "blk", 1)
    down_out.send(1)
    terms[3] = seq_reduce(terms[3])
    phase.end(moving, terms[3], near_x, near_y, down_out.got)

    moving, far_x, far_y, down_out.pieces, terms[0] = phase.take(
        add_up([moving, *terms[3]]).astype(LOW), near_x[0], near_y[1], down_out.pieces, terms[0]
    )
    moving = turn(moving, "blk", 1)
    down_out.send(3)
    far_a, far_b = swap(far_x, "slot", 2), swap(far_y, "slot", 1)
    terms[0] = seq_reduce(terms[0])
    full_pair = [[half_a, near_x[0], near_y[0], far_a], [half_b, near_x[1], near_y[1], far_b]]
    phase.end(moving, terms[0], down_out.got)
    resid = rows_f + add_up([moving, *terms[0]])
    normed_mlp, inverse_mlp = norm_rows(resid)

    grads_of, outs_of = [None] * blks, [None] * blks

    def feed(ks, held):
        for some in calls(ks):
            held, grads, outs = mlp_blocks(
                some[0] // len(some), seqs, flat([blocks[k] for k in some]), full_pair, full_down, held, total
            )
            for k, grad, out in zip(some, grads, outs):
                grads_of[k], outs_of[k] = grad, out
        return held

    blocks = [None] * blks
    moving, part_down = phase.take(
        jnp.concatenate([normed_mlp.astype(LOW), own_cot], axis=1), down_out.by_rank()
    )
    ahead = turn(moving, "blk", 1)
    near_x, near_y = swap(part_down, "slot", 1), swap(part_down, "slot", 2)
    blocks[0] = seq_gather(moving)
    phase.end(ahead, far_a, far_b, blocks[0])

    moving = phase.take(ahead)
    ahead = turn(moving, "blk", 1)
    cut = hidden // 2
    full_down = [part_down, near_x, near_y, swap(near_x[:, :cut], "slot", 2), swap(near_y[:, cut:], "slot", 1)]
    blocks[1] = seq_gather(moving)
    phase.end(ahead, blocks[1], full_down)

    moving, blocks[0], blocks[1] = phase.take(ahead, blocks[0], blocks[1])
    ahead = turn(moving, "blk", 1)
    blocks[2] = seq_gather(moving)
    held = feed(in_order[0], None)
    phase.end(ahead, blocks[2], held)

    moving, blocks[2], grads_of[:2], outs_of[:2] = phase.take(ahead, blocks[2], grads_of[:2], outs_of[:2])
    grads_of[1] = seq_reduce(grads_of[1])
    blocks[3] = seq_gather(moving)
    grad = turn(add_up(grads_of[1]).astype(LOW), "blk", 1)
    outs_of[1] = seq_reduce(outs_of[1])
    out = turn(add_up(outs_of[1]).astype(LOW), "blk", 1)
    held = feed(in_order[1], held)
    phase.end(grad, out, held)
    hidden_mlp, all_cot, activation, *grad_pair = held

    grad, grads_of[2], outs_of[2], out, activation, grad_pair[1] = phase.take(
        grad, grads_of[2], outs_of[2], out, activation, grad_pair[1]
    )
    grads_of[2], outs_of[2] = seq_reduce(grads_of[2]), seq_reduce(outs_of[2])
    grad = turn(add_up([grad, *grads_of[2]]).astype(LOW), "blk", 1)
    out = turn(add_up([out, *outs_of[2]]).astype(LOW), "blk", 1)
    down_terms = weight_terms((all_cot, [activation]))
    pair_b = weight_terms((hidden_mlp, [grad_pair[1]]))
    phase.end(grad, out, down_terms, pair_b)

    grad, grads_of[3], grads_of[0], far_down, far_b = phase.take(
        grad, grads_of[3], grads_of[0], down_terms[3], pair_b[3]
    )
    grads_of[3] = seq_reduce(grads_of[3])
    grad = turn(add_up([grad, *grads_of[3]]).astype(LOW), "blk", 1)
    far_down, far_b = swap(far_down, "slot", 1), swap(far_b, "slot", 2)
    grads_of[0] = seq_reduce(grads_of[0])
    phase.end(grad, grads_of[0])
    grad_part = add_up([grad, *grads_of[0]])
    grad_resid_part, gain_mlp_term = norm_back(normed_mlp, inverse_mlp, grad_part)
    grad_resid = own_cot.astype(WIDE) + grad_resid_part

    grad_q = [None] * blks

    def attend_back(ks, held):
        for some in calls(ks):
            held, grads = attend_back_blocks(
                some[0] // len(some), some, place, queries, key_rows, val_rows, attended, lse, cos_wide, sin_wide,
                full_attn, flat([blocks[k] for k in some]), held,
            )
            for k, grad in zip(some, grads):
                grad_q[k] = grad
        return held

    moving, out, outs_of[3], outs_of[0], half = phase.take(
        grad_resid.astype(LOW), out, outs_of[3], outs_of[0], grad_pair[0]
    )
    ahead = turn(moving, "blk", 1)
    pair_a = weight_terms((hidden_mlp, [half]))
    blocks = [seq_gather(moving), None, None, None]
    outs_of[3] = seq_reduce(outs_of[3])
    phase.end(ahead, blocks[0], outs_of[3], far_down, far_b, pair_a)

    moving, blocks[0], far_down, down_terms, out = phase.take(
        ahead, blocks[0], far_down, down_terms, add_up([out, *outs_of[3]]).astype(LOW)
    )
    ahead = turn(moving, "blk", 1)
    one = swap(add_up([down_terms[2], far_down]).astype(LOW), "slot", 2)
    two = swap(down_terms[1], "slot", 1)
    out = turn(out, "blk", 1)
    blocks[1] = seq_gather(moving)
    held = attend_back(in_order[0], None)
    phase.end(ahead, blocks[1], held, one, two)

    moving, far_a, down_terms, one, two = phase.take(ahead, pair_a[3], down_terms, one, two)
    ahead = turn(moving, "blk", 1)
    far_a = swap(far_a, "slot", 1)
    blocks[2] = seq_gather(moving)
    down_back = Exchange(row_pieces([down_terms[0], one, two]))
    relay_b = add_up([pair_b[1], far_b]).astype(LOW)
    phase.end(ahead, blocks[2], down_back.pieces, relay_b, out)

    moving, blocks[2], two_b, one_b, down_back.pieces = phase.take(ahead, blocks[2], pair_b[2], relay_b, down_back.pieces)
    blocks[3] = seq_gather(moving)
    two_b, one_b = swap(two_b, "slot", 2), swap(one_b, "slot", 1)
    down_back.send(1, 2)
    held = attend_back(in_order[1], held)
    all_resid, grad_k, grad_v = held
    phase.end(held, far_a, down_back.got)

    grad_qkv, terms, gain_terms = [None] * blks, [None] * blks, []

    def finish(ks, grad_k):
        for some in calls(ks, 1024):
            outs, gain_term, parts = finish_blocks(
                some, seqs, grad_q, grad_k, grad_v, cos_wide, sin_wide, full_attn, hidden_attn
            )
            gain_terms.append(gain_term)
            for k, out, part in zip(some, outs, parts):
                grad_qkv[k], terms[k] = out, part

    grad_k, down_back.pieces, outs_of[0] = phase.take(grad_k, down_back.pieces, outs_of[0])
    down_back.send(3)
    outs_of[0] = seq_reduce(outs_of[0])
    finish([*in_turn[0], *in_turn[1]], grad_k)
    phase.end(terms, one_b, two_b, gain_terms, down_back.got)

    terms[1] = seq_reduce(phase.take(terms[1]))
    phase.end(terms[1])

    moving, terms[2], terms[3], grad_qkv, gain_terms, far_a, near_a, middle_a, one_b, two_b = phase.take(
        add_up(terms[1]).astype(LOW), terms[2], terms[3], grad_qkv, gain_terms, far_a, pair_a[1], pair_a[2], one_b, two_b
    )
    moving = turn(moving, "blk", 1)
    one_a, two_a = swap(add_up([middle_a, far_a]).astype(LOW), "slot", 2), swap(near_a, "slot", 1)
    terms[2], terms[3] = seq_reduce(terms[2]), seq_reduce(terms[3])
    gain_terms = jnp.concatenate([add_up(gain_terms), jnp.sum(gain_mlp_term, axis=0, keepdims=True)], axis=0)
    bit = 1
    while bit < seqs:
        gain_terms = gain_terms + swap(gain_terms, "seq", bit)
        bit *= 2
    last_terms = weight_terms((hidden_attn, grad_qkv), (all_resid, attended))
    back_b = Exchange(row_pieces([pair_b[0], one_b, two_b]))
    phase.end(moving, terms[2], terms[3], last_terms, back_b.pieces, gain_terms)

    gain_parts = jnp.split(gain_terms, GROUPS, axis=1)
    moving, far, back_b.pieces, gain_far, gain_two = phase.take(
        add_up([moving, *terms[2]]).astype(LOW), last_terms[3], back_b.pieces, gain_parts[3], gain_parts[1]
    )
    moving = turn(moving, "blk", 1)
    far = swap(far, "slot", 2)
    back_b.send(1, 3)
    gain_far, gain_two = swap(gain_far, "slot", 1), swap(gain_two, "slot", 1)
    phase.end(moving, far, back_b.got, gain_far, gain_two, one_a, two_a)

    moving, relay, near_term, back_b.pieces, terms[0], one_a, two_a = phase.take(
        add_up([moving, *terms[3]]).astype(LOW), add_up([last_terms[1], far]).astype(LOW), last_terms[2],
        back_b.pieces, terms[0], one_a, two_a,
    )
    moving = turn(moving, "blk", 1)
    one, two = swap(relay, "slot", 1), swap(near_term, "slot", 2)
    back_b.send(2)
    back_a = Exchange(row_pieces([pair_a[0], one_a, two_a]))
    phase.end(moving, one, two, back_b.got, back_a.pieces)

    last_back = Exchange(row_pieces([last_terms[0], one, two]))
    gain_relay, last_back.pieces, back_a.pieces, terms[0] = phase.take(
        gain_parts[2] + gain_far, last_back.pieces, back_a.pieces, terms[0]
    )
    back_a.send(1, 2, 3)
    terms[0] = seq_reduce(terms[0])
    last_back.send(1, 2, 3)
    gain_one = swap(gain_relay, "slot", 2)
    gain_sum = after(gain_parts[0] + gain_two + gain_one, back_a.got[1])
    gain_sums = [gain_sum] + [turn(gain_sum, "blk", k) for k in range(1, blks)]

    layer_out = jnp.where(live_rows, resid + add_up([out, *outs_of[0]]), 0.0)
    grad_hidden_attn = add_up([moving, *terms[0]])
    normed_attn, inverse_attn = norm_rows(rows_f)
    grad_in_part, _ = norm_back(normed_attn, inverse_attn, grad_hidden_attn)
    shard = attn_gain.shape[0]
    gain_grads = lax.dynamic_slice(add_up(gain_sums), (0, blk_rank * shard), (2, shard))
    half = hidden // 2
    return (
        slot_order(layer_out).astype(LOW)[None],
        slot_order(grad_resid + grad_in_part)[None],
        gain_grads[0] / gain_attn[:, 0],
        join_owners([last_back], [(0, width)], gain_attn),
        join_owners([last_back], [(width, width)], gain_attn),
        join_owners([last_back], [(2 * width, width)], gain_attn),
        join_owners([last_back], [(3 * width, width)], 1.0),
        gain_grads[1] / gain_mlp[:, 0],
        join_owners([back_a, back_b], [(0, half)], gain_mlp),
        join_owners([back_a, back_b], [(half, half)], gain_mlp),
        join_owners([down_back], [(0, hidden)], 1.0),
    )


def solution(mesh):
    rows = P("slot", ("blk", "seq"), None)
    gain = P(("slot", "blk"))
    weight = P(("slot", "blk"), "seq")
    return jax.shard_map(
        shards,
        mesh=mesh,
        in_specs=(rows, rows, P("slot"), gain, weight, weight, weight, weight, gain, weight, weight, weight),
        out_specs=(rows, rows, gain, weight, weight, weight, weight, gain, weight, weight, weight),
        check_vma=False,
    )
```

```python
import math
from functools import partial

import jax
import jax.numpy as jnp
from jax import lax
from jax.experimental import pallas as pl
from jax.experimental.pallas import tpu as pltpu
from jax.sharding import PartitionSpec as P

HEADS = 32
HEAD_DIM = 64
HALF = HEAD_DIM // 2
EPSILON = 1e-05
ROPE_BASE = 130000.0
LOW = jnp.bfloat16
WIDE = jnp.float32
GROUPS = 4
ANY = pl.BlockSpec(memory_space=pl.ANY)


def turn(value, axis, by):
    count = lax.axis_size(axis)
    return lax.ppermute(value, axis, [(i, (i + by) % count) for i in range(count)])


def swap(value, axis, mask):
    count = lax.axis_size(axis)
    return lax.ppermute(value, axis, [(i, i ^ mask) for i in range(count)])


def after(value, *others):
    return lax.optimization_barrier((value, *others))[0]


def matmul(left, right):
    return jnp.dot(left, right, preferred_element_type=WIDE)


def over_rows(left, right):
    return lax.dot_general(left, right, (((0,), (0,)), ((), ())), preferred_element_type=WIDE)


def over_cols(left, right):
    return lax.dot_general(left, right, (((1,), (1,)), ((), ())), preferred_element_type=WIDE)


def slot_order(array):
    rank = lax.axis_index("slot")
    parts = jnp.split(array, GROUPS, axis=-1)
    for bit in (1, 2):
        flip = (rank & bit) != 0
        parts = [jnp.where(flip, parts[i ^ bit], parts[i]) for i in range(GROUPS)]
    return jnp.concatenate(parts, axis=-1)


def seq_gather(rows):
    count = lax.axis_size("seq")
    held = [rows]
    bit = 1
    while bit < count:
        held = held + [swap(part, "seq", bit) for part in held]
        bit *= 2
    return held


def seq_reduce(parts):
    bit = lax.axis_size("seq") // 2
    parts = [[part] for part in parts]
    while bit >= 1:
        kept = parts[:bit]
        for mine, other in zip(kept, parts[bit:]):
            mine.append(swap(add_up(other).astype(LOW), "seq", bit))
        parts = kept
        bit //= 2
    return parts[0]


def add_up(summands):
    total = summands[0]
    for summand in summands[1:]:
        total = total.astype(WIDE) + summand.astype(WIDE)
    return total


class Phases:
    def __init__(self):
        self.ended = ()

    def take(self, *values):
        values = tuple(values)
        if self.ended:
            values = lax.optimization_barrier((values, self.ended))[0]
        return values[0] if len(values) == 1 else values

    def end(self, *values):
        self.ended = values


class Exchange:
    def __init__(self, pieces):
        self.pieces = pieces
        self.got = {0: pieces[0]}

    def send(self, *steps):
        for k in steps:
            self.got[k] = turn(self.pieces[k], "blk", k)
        return [self.got[k] for k in steps]

    def by_rank(self, columns=slice(None)):
        blks, rank = lax.axis_size("blk"), lax.axis_index("blk")
        parts = [self.got[k][:, columns] for k in range(blks)]
        rows, cols = parts[0].shape
        full = jnp.zeros((blks * rows, cols), parts[0].dtype)
        for k in range(blks):
            full = lax.dynamic_update_slice(full, parts[k], ((rank - k) % blks * rows, 0))
        return full


def column_pieces(arrays, parts=1):
    blks, rank = lax.axis_size("blk"), lax.axis_index("blk")

    def cut(array, owner, part):
        width = array.shape[1] // (blks * parts)
        return lax.dynamic_slice(array, (0, (owner * parts + part) * width), (array.shape[0], width))

    return [
        jnp.concatenate([cut(a, (rank + k) % blks, part) for part in range(parts) for a in arrays], axis=1)
        for k in range(blks)
    ]


def row_pieces(summands):
    blks, rank = lax.axis_size("blk"), lax.axis_index("blk")
    rows = summands[0].shape[0] // blks

    def cut(owner):
        parts = [lax.dynamic_slice(s, (owner * rows, 0), (rows, s.shape[1])) for s in summands]
        return add_up(parts).astype(LOW)

    return [cut((rank + k) % blks) for k in range(blks)]


def join_owners(exchanges, cuts, scale):
    blks, rank = lax.axis_size("blk"), lax.axis_index("blk")
    wide = sum(width for _, width in cuts)
    out = jnp.zeros((exchanges[0].got[0].shape[0], blks * wide * len(exchanges)), WIDE)
    for n, exchanged in enumerate(exchanges):
        for k in range(blks):
            first = ((rank - k) % blks * len(exchanges) + n) * wide
            for at, width in cuts:
                part = exchanged.got[k][:, at : at + width].astype(WIDE) * scale
                out = lax.dynamic_update_slice(out, part, (0, first))
                first = first + width
    return out


def norm_rows(rows):
    inverse = lax.rsqrt(jnp.mean(rows * rows, axis=-1, keepdims=True) + EPSILON)
    return rows * inverse, inverse


def norm_back(normed, inverse, upstream):
    product = upstream * normed
    return inverse * (upstream - normed * jnp.mean(product, axis=-1, keepdims=True)), product


def vmem(shape):
    return pl.BlockSpec(shape, lambda *_: (0,) * len(shape))


def params(mebibytes):
    return pltpu.CompilerParams(vmem_limit_bytes=mebibytes << 20)


def cost():
    return pl.CostEstimate(flops=1, bytes_accessed=1, transcendentals=0)


def partner(vectors):
    width = vectors.shape[1]
    if width % 128 == 0:
        lanes = lax.broadcasted_iota(jnp.int32, (1, width), 1)
        ahead = pltpu.roll(vectors, width - HALF, 1)
        behind = pltpu.roll(vectors, HALF, 1)
        return jnp.where(lanes % HEAD_DIM < HALF, ahead, behind)
    parts = []
    for first in range(0, width, HEAD_DIM):
        parts += [vectors[:, first + HALF : first + HEAD_DIM], vectors[:, first : first + HALF]]
    return jnp.concatenate(parts, axis=1)


def table_kernel(dims, place_ref, cos_ref, sin_ref):
    total, blks, seqs, size = dims
    wide = cos_ref.shape[1]
    index = lax.broadcasted_iota(jnp.int32, (total, 1), 0)
    position = row_positions(index, place_ref[0], place_ref[1], blks, seqs, size).astype(WIDE)
    lane = lax.broadcasted_iota(jnp.int32, (1, wide), 1)
    power = (lane % HALF).astype(WIDE) * (-2.0 / HEAD_DIM)
    angle = position * jnp.exp(power * math.log(ROPE_BASE))
    cos_ref[...] = jnp.cos(angle)
    sin_ref[...] = jnp.where(lane % HEAD_DIM < HALF, -jnp.sin(angle), jnp.sin(angle))


def rotary_tables(place, total, size, wide):
    dims = (total, lax.axis_size("blk"), lax.axis_size("seq"), size)
    return pl.pallas_call(
        partial(table_kernel, dims),
        grid_spec=pltpu.PrefetchScalarGridSpec(
            num_scalar_prefetch=1, grid=(1,), in_specs=[], out_specs=[vmem((total, wide))] * 2
        ),
        out_shape=[jax.ShapeDtypeStruct((total, wide), WIDE)] * 2,
        compiler_params=params(32),
        cost_estimate=cost(),
        name="rotary_tables",
    )(place)


def widen(table, width):
    return table if table.shape[1] == width else jnp.concatenate([table] * (width // table.shape[1]), axis=1)


def qkv_kernel(width, *refs):
    parts, weights, (cos_ref, sin_ref) = refs[:-10], refs[-10:-6], refs[-6:-4]
    h_ref, q_ref, k_ref, v_ref = refs[-4:]
    size, model = parts[0].shape
    step = model // GROUPS
    for n, part in enumerate(parts):
        normed, _ = norm_rows(part[...].astype(WIDE))
        h_ref[n * size : (n + 1) * size, :] = normed.astype(LOW)
    total = h_ref.shape[0]
    rows = min(512, total)

    def some(first):
        here = slice(first, first + rows)
        pre = matmul(h_ref[here, :step], weights[0][:, : 3 * width])
        for i in range(1, GROUPS):
            pre += matmul(h_ref[here, i * step : (i + 1) * step], weights[i][:, : 3 * width])
        cos, sin = widen(cos_ref[here, :], width), widen(sin_ref[here, :], width)
        for at, out_ref in ((0, q_ref), (1, k_ref)):
            half = pre[:, at * width : (at + 1) * width]
            out_ref[here, :] = (half * cos + partner(half) * sin).astype(LOW)
        v_ref[here, :] = pre[:, 2 * width :].astype(LOW)

    for first in range(0, total, rows):
        some(first)


def project_qkv(parts, weights, cos, sin, width):
    size, model = parts[0].shape
    total = size * len(parts)
    return pl.pallas_call(
        partial(qkv_kernel, width),
        grid=(1,),
        in_specs=[vmem((size, model))] * len(parts) + [vmem(w.shape) for w in weights] + [vmem(cos.shape)] * 2,
        out_specs=[vmem((total, model))] + [vmem((total, width))] * 3,
        out_shape=[jax.ShapeDtypeStruct((total, model), LOW)] + [jax.ShapeDtypeStruct((total, width), LOW)] * 3,
        compiler_params=params(60),
        cost_estimate=cost(),
        name="project_qkv",
    )(*parts, *weights, cos, sin)


def row_positions(index, blk_rank, seq_rank, blks, seqs, size):
    sub = index // size
    k, m = sub // seqs, sub % seqs
    return ((blk_rank - k + blks) % blks * seqs + (seq_rank ^ m)) * size + index % size


def allowed_pairs(dims, place_ref, firsts, rows):
    total, blks, seqs, size = dims
    blk_rank, seq_rank, length = place_ref[0], place_ref[1], place_ref[2]
    k_index = lax.broadcasted_iota(jnp.int32, (1, total), 1)
    k_pos = row_positions(k_index, blk_rank, seq_rank, blks, seqs, size)
    k_pos = jnp.where(k_pos < length, k_pos, jnp.int32(1 << 30))
    index = lax.broadcasted_iota(jnp.int32, (rows, 1), 0)
    q_pos = [row_positions(first + index, blk_rank, seq_rank, blks, seqs, size) for first in firsts]
    return k_pos <= jnp.concatenate(q_pos, axis=0)


def tiles_of(count, block):
    if count * block <= 512:
        return [[(g, 0, block) for g in range(count)]]
    rows = min(256, block)
    return [[(g, first, rows)] for g in range(count) for first in range(0, block, rows)]


def rows_of(refs, tile):
    return jnp.concatenate([refs[g][first : first + rows, :] for g, first, rows in tile], axis=0)


def put_rows(refs, tile, value):
    at = 0
    for g, first, rows in tile:
        refs[g][first : first + rows, :] = value[at : at + rows]
        at += rows


def put_parts(terms, size, column, value):
    for n, term in enumerate(terms):
        term[:, column : column + value.shape[1]] = value[n * size : (n + 1) * size]


def by_block(terms, count):
    some = len(terms) // count
    return [terms[g * some : (g + 1) * some] for g in range(count)]


def attend_kernel(dims, ks, width, place_ref, *refs):
    count, seqs = len(ks), dims[2]
    q_refs, (k_ref, v_ref), weights = refs[:count], refs[count : count + 2], refs[count + 2 : count + 6]
    out_refs, lse_refs, terms = refs[count + 6 : 2 * count + 6], refs[2 * count + 6 : 3 * count + 6], refs[3 * count + 6 :]
    block = q_refs[0].shape[0]
    lanes = lax.broadcasted_iota(jnp.int32, (1, width), 1)
    lse_lanes = lax.broadcasted_iota(jnp.int32, (1, 128), 1)
    for tile in tiles_of(count, block):
        rows = tile[0][2]
        allowed = allowed_pairs(dims, place_ref, [ks[g] * block + first for g, first, _ in tile], rows)
        queries = rows_of(q_refs, tile).astype(WIDE) * HEAD_DIM**-0.5
        wide = rows * len(tile)

        def one_head(head, carried):
            out, lse = carried
            mine = lanes // HEAD_DIM == head
            picked = jnp.where(mine, queries, 0.0).astype(LOW)
            scores = jnp.where(allowed, over_cols(picked, k_ref[...]), -1e30)
            top = jnp.max(scores, axis=1, keepdims=True)
            probs = jnp.exp(scores - top)
            weight = jnp.sum(probs, axis=1, keepdims=True)
            mixed = matmul(probs.astype(LOW), v_ref[...]) / weight
            return jnp.where(mine, mixed, out), jnp.where(lse_lanes == head, top + jnp.log(weight), lse)

        out, lse = lax.fori_loop(
            0, width // HEAD_DIM, one_head, (jnp.zeros((wide, width), WIDE), jnp.zeros((wide, 128), WIDE))
        )
        put_rows(out_refs, tile, out.astype(LOW))
        put_rows(lse_refs, tile, lse)
    attended = jnp.concatenate([ref[...] for ref in out_refs], axis=0)
    for i, weight in enumerate(weights):
        step = weight.shape[0]
        put_parts(terms, block // seqs, i * step, over_cols(attended, weight[:, 3 * width :]).astype(LOW))


def attend_blocks(ks, place, queries, key_rows, val_rows, weights, size, model):
    total, width = queries.shape
    blks, seqs, count = lax.axis_size("blk"), lax.axis_size("seq"), len(ks)
    block = total // blks
    rows_at = lambda k, wide: pl.BlockSpec((block, wide), lambda *_: (k, 0))
    got = pl.pallas_call(
        partial(attend_kernel, (total, blks, seqs, size), ks, width),
        grid_spec=pltpu.PrefetchScalarGridSpec(
            num_scalar_prefetch=1,
            grid=(1,),
            in_specs=[rows_at(k, width) for k in ks] + [vmem((total, width))] * 2 + [vmem(w.shape) for w in weights],
            out_specs=[vmem((block, width))] * count + [vmem((block, 128))] * count + [vmem((size, model))] * (count * seqs),
        ),
        out_shape=[jax.ShapeDtypeStruct((block, width), LOW)] * count
        + [jax.ShapeDtypeStruct((block, 128), WIDE)] * count
        + [jax.ShapeDtypeStruct((size, model), LOW)] * (count * seqs),
        compiler_params=params(56),
        cost_estimate=cost(),
        name="attend_blocks",
    )(place, *[queries] * count, key_rows, val_rows, *weights)
    return got[:count], got[count : 2 * count], by_block(got[2 * count :], count)


def mlp_kernel(count, *refs):
    parts, pairs, down = refs[:count], (refs[count : count + 4], refs[count + 4 : count + 8]), refs[count + 8 : count + 13]
    outs = refs[-5 - 2 * count :]
    h_ref, c_ref, act_ref, pair_refs = outs[0], outs[1], outs[2], outs[3:5]
    grad_terms, out_terms = outs[5 : 5 + count], outs[5 + count :]
    size, model = parts[0].shape[0], h_ref.shape[1]
    step, hidden = model // GROUPS, down[0].shape[1] // 2
    groups = [slice(i * step, (i + 1) * step) for i in range(GROUPS)]
    for m in range(count):
        rows = slice(m * size, (m + 1) * size)
        h_ref[rows, :] = parts[m][:, :model]
        c_ref[rows, :] = parts[m][:, model:]
    down_half = lambda i, j: down[i][:, j * hidden : (j + 1) * hidden] if i < 3 else down[3 + j][...]
    for j, pair_ref in enumerate(pair_refs):
        half = slice(j * hidden, (j + 1) * hidden)
        both = matmul(h_ref[:, groups[0]], pairs[j][0][...])
        grad_act = matmul(c_ref[:, groups[0]], down_half(0, j))
        for i in range(1, GROUPS):
            both += matmul(h_ref[:, groups[i]], pairs[j][i][...])
            grad_act += matmul(c_ref[:, groups[i]], down_half(i, j))
        gate, up = both[:, :hidden], both[:, hidden:]
        sig = jax.nn.sigmoid(gate)
        act_ref[:, half] = (gate * sig * up).astype(LOW)
        pair_ref[:, :hidden] = (grad_act * up * sig * (1.0 + gate * (1.0 - sig))).astype(LOW)
        pair_ref[:, hidden:] = (grad_act * gate * sig).astype(LOW)
    for i in range(GROUPS):
        grad = over_cols(pair_refs[0][...], pairs[0][i][...]) + over_cols(pair_refs[1][...], pairs[1][i][...])
        put_parts(grad_terms, size, i * step, grad.astype(LOW))
        if i < 3:
            out = over_cols(act_ref[...], down[i][...])
        else:
            out = over_cols(act_ref[:, :hidden], down[3][...]) + over_cols(act_ref[:, hidden:], down[4][...])
        put_parts(out_terms, size, i * step, out.astype(LOW))


def mlp_blocks(at, seqs, parts, pairs, down, held, total):
    count, (size, model) = len(parts), (parts[0].shape[0], parts[0].shape[1] // 2)
    hidden = down[0].shape[1]
    rows = count * size
    old = [] if held is None else list(held)
    widths = [model, model, hidden, hidden, hidden]
    got = pl.pallas_call(
        partial(mlp_kernel, count),
        grid=(1,),
        in_specs=[vmem((size, 2 * model))] * count
        + [vmem(w.shape) for w in (*pairs[0], *pairs[1], *down)]
        + [ANY] * len(old),
        out_specs=[pl.BlockSpec((rows, wide), lambda _: (at, 0)) for wide in widths] + [vmem((size, model))] * (2 * count),
        out_shape=[jax.ShapeDtypeStruct((total, wide), LOW) for wide in widths]
        + [jax.ShapeDtypeStruct((size, model), LOW)] * (2 * count),
        input_output_aliases={count + 13 + i: i for i in range(5)} if old else {},
        compiler_params=params(60),
        cost_estimate=cost(),
        name="mlp_blocks",
    )(*parts, *pairs[0], *pairs[1], *down, *old)
    return got[:5], by_block(got[5 : 5 + count], count // seqs), by_block(got[5 + count :], count // seqs)


def attend_back_kernel(dims, ks, width, fresh, place_ref, *refs):
    count, seqs = len(ks), dims[2]

    def some(number):
        nonlocal refs
        taken, refs = refs[:number], refs[number:]
        return taken

    q_refs, (k_ref, v_ref), out_refs, lse_refs = some(count), some(2), some(count), some(count)
    cos_refs, sin_refs, weights, parts = some(count), some(count), some(4), some(count * seqs)
    old = [] if fresh else some(3)
    (r_ref, gk_ref, gv_ref), gq_refs, (cot_ref,) = some(3), some(count), some(1)
    block = q_refs[0].shape[0]
    size = block // seqs
    lanes = lax.broadcasted_iota(jnp.int32, (1, width), 1)
    lse_lanes = lax.broadcasted_iota(jnp.int32, (1, 128), 1)
    gk_ref[...] = jnp.zeros_like(gk_ref) if fresh else old[1][...]
    gv_ref[...] = jnp.zeros_like(gv_ref) if fresh else old[2][...]
    for n, part in enumerate(parts):
        r_ref[n * size : (n + 1) * size, :] = part[...]
    step = weights[0].shape[0]
    cot = matmul(r_ref[:, :step], weights[0][:, 3 * width :])
    for i in range(1, GROUPS):
        cot += matmul(r_ref[:, i * step : (i + 1) * step], weights[i][:, 3 * width :])
    cot_ref[...] = cot.astype(LOW).astype(WIDE)
    for tile in tiles_of(count, block):
        rows = tile[0][2]
        allowed = allowed_pairs(dims, place_ref, [ks[g] * block + first for g, first, _ in tile], rows)
        queries = rows_of(q_refs, tile).astype(WIDE) * HEAD_DIM**-0.5
        tile_cot = jnp.concatenate([cot_ref[g * block + first : g * block + first + n, :] for g, first, n in tile], axis=0)
        dots = tile_cot * rows_of(out_refs, tile).astype(WIDE)
        tile_lse = rows_of(lse_refs, tile)
        wide = rows * len(tile)

        def one_head(head, grad_q):
            mine = lanes // HEAD_DIM == head
            picked = jnp.where(mine, queries, 0.0).astype(LOW)
            cot_head = jnp.where(mine, tile_cot, 0.0).astype(LOW)
            row_dot = jnp.sum(jnp.where(mine, dots, 0.0), axis=1, keepdims=True)
            lse = jnp.sum(jnp.where(lse_lanes == head, tile_lse, 0.0), axis=1, keepdims=True)
            scores = jnp.where(allowed, over_cols(picked, k_ref[...]), -1e30)
            probs = jnp.exp(scores - lse)
            gv_ref[...] += over_rows(probs.astype(LOW), cot_head)
            grad_probs = over_cols(cot_head, v_ref[...])
            grad_scores = (probs * (grad_probs - row_dot)).astype(LOW)
            gk_ref[...] += over_rows(grad_scores, picked)
            return jnp.where(mine, matmul(grad_scores, k_ref[...]) * HEAD_DIM**-0.5, grad_q)

        grad_q = lax.fori_loop(0, width // HEAD_DIM, one_head, jnp.zeros((wide, width), WIDE))
        low = grad_q.astype(LOW).astype(WIDE)
        cos, sin = widen(rows_of(cos_refs, tile), width), widen(rows_of(sin_refs, tile), width)
        put_rows(gq_refs, tile, (low * cos - partner(low) * sin).astype(LOW))


def attend_back_blocks(at, ks, place, queries, key_rows, val_rows, attended, lse, cos, sin, weights, parts, held):
    total, width = queries.shape
    blks, seqs, count = lax.axis_size("blk"), lax.axis_size("seq"), len(ks)
    size, model = parts[0].shape
    block = total // blks
    rows_at = lambda k, wide: pl.BlockSpec((block, wide), lambda *_: (k, 0))
    whole = vmem((total, width))
    old = [] if held is None else list(held)
    first_old = 1 + count + 2 + 2 * count + 2 * count + 4 + count * seqs
    tables = [rows_at(k, cos.shape[1]) for k in ks]
    got = pl.pallas_call(
        partial(attend_back_kernel, (total, blks, seqs, size), ks, width, held is None),
        grid_spec=pltpu.PrefetchScalarGridSpec(
            num_scalar_prefetch=1,
            grid=(1,),
            in_specs=[rows_at(k, width) for k in ks]
            + [whole] * 2
            + [vmem((block, width))] * count
            + [vmem((block, 128))] * count
            + tables * 2
            + [vmem(w.shape) for w in weights]
            + [vmem((size, model))] * (count * seqs)
            + ([ANY, whole, whole] if old else []),
            out_specs=[pl.BlockSpec((count * block, model), lambda *_: (at, 0)), whole, whole] + [vmem((block, width))] * count,
            scratch_shapes=[pltpu.VMEM((count * block, width), WIDE)],
        ),
        out_shape=[jax.ShapeDtypeStruct((total, model), LOW)]
        + [jax.ShapeDtypeStruct((total, width), WIDE)] * 2
        + [jax.ShapeDtypeStruct((block, width), LOW)] * count,
        input_output_aliases={first_old + i: i for i in range(3)} if old else {},
        compiler_params=params(60),
        cost_estimate=cost(),
        name="attend_back_blocks",
    )(
        place, *[queries] * count, key_rows, val_rows, *[attended[k] for k in ks], *[lse[k] for k in ks],
        *[cos] * count, *[sin] * count, *weights, *parts, *old,
    )
    return got[:3], got[3:]


def finish_kernel(width, count, seqs, *refs):
    def some(number):
        nonlocal refs
        taken, refs = refs[:number], refs[number:]
        return taken

    gq_refs, gk_refs, gv_refs, cos_refs, sin_refs = (some(count) for _ in range(5))
    weights, normed = some(4), some(count)
    outs, (gain_ref,), terms = some(count), some(1), some(count * seqs)
    size = terms[0].shape[0]
    step = weights[0].shape[0]
    for g, out_ref in enumerate(outs):
        low_k = gk_refs[g][...].astype(LOW).astype(WIDE)
        cos, sin = widen(cos_refs[g][...], width), widen(sin_refs[g][...], width)
        out_ref[:, :width] = gq_refs[g][...]
        out_ref[:, width : 2 * width] = (low_k * cos - partner(low_k) * sin).astype(LOW)
        out_ref[:, 2 * width :] = gv_refs[g][...].astype(LOW)
    grads = jnp.concatenate([ref[...] for ref in outs], axis=0)
    for i in range(GROUPS):
        here = slice(i * step, (i + 1) * step)
        grad = over_cols(grads, weights[i][:, : 3 * width])
        put_parts(terms, size, i * step, grad.astype(LOW))
        rows = jnp.concatenate([ref[:, here] for ref in normed], axis=0).astype(WIDE)
        gain_ref[:, here] = jnp.sum(grad * rows, axis=0, keepdims=True)


def finish_blocks(ks, seqs, grad_q, grad_k, grad_v, cos, sin, weights, normed):
    count = len(ks)
    total, width = grad_k.shape
    model = normed.shape[1]
    block = total // lax.axis_size("blk")
    size = block // seqs
    rows_at = lambda k, wide: pl.BlockSpec((block, wide), lambda _: (k, 0))
    tables = [rows_at(k, cos.shape[1]) for k in ks]
    got = pl.pallas_call(
        partial(finish_kernel, width, count, seqs),
        grid=(1,),
        in_specs=[vmem((block, width))] * count
        + [rows_at(k, width) for k in ks] * 2
        + tables * 2
        + [vmem(w.shape) for w in weights]
        + [rows_at(k, model) for k in ks],
        out_specs=[vmem((block, 3 * width))] * count + [vmem((1, model))] + [vmem((size, model))] * (count * seqs),
        out_shape=[jax.ShapeDtypeStruct((block, 3 * width), LOW)] * count
        + [jax.ShapeDtypeStruct((1, model), WIDE)]
        + [jax.ShapeDtypeStruct((size, model), LOW)] * (count * seqs),
        compiler_params=params(56),
        cost_estimate=cost(),
        name="finish_blocks",
    )(*[grad_q[k] for k in ks], *[grad_k] * count, *[grad_v] * count, *[cos] * count, *[sin] * count, *weights, *[normed] * count)
    return got[:count], got[count], by_block(got[count + 1 :], count)


def weight_kernel(counts, *refs):
    outs = refs[-GROUPS:]
    step = outs[0].shape[0]
    for i, out_ref in enumerate(outs):
        at, column = 0, 0
        for count in counts:
            left_ref, rights = refs[at], refs[at + 1 : at + 1 + count]
            rows, wide = rights[0].shape
            here = slice(i * step, (i + 1) * step)
            total = over_rows(left_ref[:rows, here], rights[0][...])
            for g in range(1, count):
                total += over_rows(left_ref[g * rows : (g + 1) * rows, here], rights[g][...])
            out_ref[:, column : column + wide] = total.astype(LOW)
            at, column = at + 1 + count, column + wide


def weight_terms(*pairs):
    step = pairs[0][0].shape[1] // GROUPS
    cols = sum(rights[0].shape[1] for _, rights in pairs)
    arrays = [a for left, rights in pairs for a in (left, *rights)]
    return pl.pallas_call(
        partial(weight_kernel, [len(rights) for _, rights in pairs]),
        grid=(1,),
        in_specs=[vmem(a.shape) for a in arrays],
        out_specs=[vmem((step, cols))] * GROUPS,
        out_shape=[jax.ShapeDtypeStruct((step, cols), LOW)] * GROUPS,
        compiler_params=params(60),
        cost_estimate=cost(),
        name="weight_terms",
    )(*arrays)


def shards(
    tokens, out_grad, lengths, attn_gain, w_query, w_key, w_value, output_weight, mlp_gain, gate_weight, up_weight, down_weight
):
    seqs, blks = lax.axis_size("seq"), lax.axis_size("blk")
    seq_rank, blk_rank = lax.axis_index("seq"), lax.axis_index("blk")
    size, model = tokens.shape[1], tokens.shape[2]
    block = size * seqs
    total = block * blks
    length = lengths[0]
    width = w_query.shape[1] // blks
    hidden = gate_weight.shape[1] // blks
    positions = (blk_rank * seqs + seq_rank) * size + jnp.arange(size, dtype=jnp.int32)
    live_rows = (positions < length)[:, None]
    place = jnp.stack([blk_rank, seq_rank, length, lax.axis_index("slot")]).astype(jnp.int32)

    cos_wide, sin_wide = rotary_tables(place, total, size, min(width, 128))
    own_tokens = slot_order(tokens[0])
    own_cot = jnp.where(live_rows, slot_order(out_grad[0]), 0)
    gain_attn, gain_mlp = attn_gain.astype(WIDE)[:, None], mlp_gain.astype(WIDE)[:, None]
    rows_f = own_tokens.astype(WIDE)

    def scaled(weight, gain):
        return (weight.astype(WIDE) * gain).astype(LOW)

    attn_out = Exchange(
        column_pieces([scaled(w, gain_attn) for w in (w_query, w_key, w_value)] + [output_weight])
    )
    pair_out = Exchange(column_pieces([scaled(gate_weight, gain_mlp), scaled(up_weight, gain_mlp)], 2))
    down_out = Exchange(column_pieces([down_weight]))
    phase = Phases()
    flat = lambda lists: [item for items in lists for item in items]
    in_order, in_turn = [[0, 1], [2, 3]], [[1, 2], [3, 0]]

    def calls(ks, most=512):
        return [ks] if block * len(ks) <= most else [[k] for k in ks]

    token_blocks = [None] * blks
    attn_out.send(1, 2, 3)
    token_blocks[0] = seq_gather(own_tokens)
    phase.end(attn_out.got, token_blocks[0])

    part_attn, moving = phase.take(attn_out.by_rank(), own_tokens)
    second = turn(moving, "blk", 1)
    ahead = turn(second, "blk", 1)
    near_x, near_y = swap(part_attn, "slot", 1), swap(part_attn, "slot", 2)
    phase.end(second, ahead, near_x, near_y, pair_out.pieces, down_out.pieces, cos_wide, sin_wide)

    second, moving, near_x, pair_out.pieces = phase.take(second, ahead, near_x, pair_out.pieces)
    ahead = turn(moving, "blk", 1)
    far = swap(near_x, "slot", 2)
    pair_out.send(1)
    token_blocks[1], token_blocks[2] = seq_gather(second), seq_gather(moving)
    full_attn = [part_attn, near_x, near_y, far]
    phase.end(ahead, far, token_blocks[1:3], pair_out.got)

    moving, pair_out.pieces = phase.take(ahead, pair_out.pieces)
    token_blocks[3] = seq_gather(moving)
    pair_out.send(2, 3)
    got = []
    for ks in [list(range(blks))] if total <= 1024 else [[k] for k in range(blks)]:
        here = slice(ks[0] * block, (ks[-1] + 1) * block)
        got.append(project_qkv(flat([token_blocks[k] for k in ks]), full_attn, cos_wide[here], sin_wide[here], width))
    hidden_attn, queries, key_rows, val_rows = (
        parts[0] if len(parts) == 1 else jnp.concatenate(parts, axis=0) for parts in zip(*got)
    )
    attended, lse, terms = [None] * blks, [None] * blks, [None] * blks

    def attend(ks, queries):
        for some in calls(ks):
            for k, *got in zip(some, *attend_blocks(some, place, queries, key_rows, val_rows, full_attn, size, model)):
                attended[k], lse[k], terms[k] = got

    attend(in_turn[0], queries)
    phase.end(pair_out.got, terms[1], terms[2])

    queries, pair_out.got, down_out.pieces, terms[1], terms[2] = phase.take(
        queries, pair_out.got, down_out.pieces, terms[1], terms[2]
    )
    half_a = pair_out.by_rank(slice(0, hidden))
    near_x, near_y = [swap(half_a, "slot", 1)], [swap(half_a, "slot", 2)]
    terms[1] = seq_reduce(terms[1])
    moving = turn(add_up(terms[1]).astype(LOW), "blk", 1)
    down_out.send(2)
    terms[2] = seq_reduce(terms[2])
    attend(in_turn[1], queries)
    phase.end(moving, terms, near_x, near_y, down_out.got)

    half_b = pair_out.by_rank(slice(hidden, None))
    moving, half_b, down_out.pieces, terms[3], terms[0] = phase.take(
        add_up([moving, *terms[2]]).astype(LOW), half_b, down_out.pieces, terms[3], terms[0]
    )
    near_x, near_y = near_x + [swap(half_b, "slot", 1)], near_y + [swap(half_b, "slot", 2)]
    moving = turn(moving, "blk", 1)
    down_out.send(1)
    terms[3] = seq_reduce(terms[3])
    phase.end(moving, terms[3], near_x, near_y, down_out.got)

    moving, far_x, far_y, down_out.pieces, terms[0] = phase.take(
        add_up([moving, *terms[3]]).astype(LOW), near_x[0], near_y[1], down_out.pieces, terms[0]
    )
    moving = turn(moving, "blk", 1)
    down_out.send(3)
    far_a, far_b = swap(far_x, "slot", 2), swap(far_y, "slot", 1)
    terms[0] = seq_reduce(terms[0])
    full_pair = [[half_a, near_x[0], near_y[0], far_a], [half_b, near_x[1], near_y[1], far_b]]
    phase.end(moving, terms[0], down_out.got)
    resid = rows_f + add_up([moving, *terms[0]])
    normed_mlp, inverse_mlp = norm_rows(resid)

    grads_of, outs_of = [None] * blks, [None] * blks

    def feed(ks, held):
        for some in calls(ks):
            held, grads, outs = mlp_blocks(
                some[0] // len(some), seqs, flat([blocks[k] for k in some]), full_pair, full_down, held, total
            )
            for k, grad, out in zip(some, grads, outs):
                grads_of[k], outs_of[k] = grad, out
        return held

    blocks = [None] * blks
    moving, part_down = phase.take(
        jnp.concatenate([normed_mlp.astype(LOW), own_cot], axis=1), down_out.by_rank()
    )
    ahead = turn(moving, "blk", 1)
    near_x, near_y = swap(part_down, "slot", 1), swap(part_down, "slot", 2)
    blocks[0] = seq_gather(moving)
    phase.end(ahead, far_a, far_b, blocks[0])

    moving = phase.take(ahead)
    ahead = turn(moving, "blk", 1)
    cut = hidden // 2
    full_down = [part_down, near_x, near_y, swap(near_x[:, :cut], "slot", 2), swap(near_y[:, cut:], "slot", 1)]
    blocks[1] = seq_gather(moving)
    phase.end(ahead, blocks[1], full_down)

    moving, blocks[0], blocks[1] = phase.take(ahead, blocks[0], blocks[1])
    ahead = turn(moving, "blk", 1)
    blocks[2] = seq_gather(moving)
    held = feed(in_order[0], None)
    grads_of[1], outs_of[1] = seq_reduce(grads_of[1]), seq_reduce(outs_of[1])
    phase.end(ahead, blocks[2], held, grads_of[1], outs_of[1])

    moving, blocks[2], grads_of[:2], outs_of[:2] = phase.take(ahead, blocks[2], grads_of[:2], outs_of[:2])
    blocks[3] = seq_gather(moving)
    grad = turn(add_up(grads_of[1]).astype(LOW), "blk", 1)
    out = turn(add_up(outs_of[1]).astype(LOW), "blk", 1)
    held = feed(in_order[1], held)
    grads_of[2], outs_of[2] = seq_reduce(grads_of[2]), seq_reduce(outs_of[2])
    phase.end(grad, out, held, grads_of[2], outs_of[2])
    hidden_mlp, all_cot, activation, *grad_pair = held

    grad, grads_of[2], outs_of[2], out, activation, grad_pair[1] = phase.take(
        grad, grads_of[2], outs_of[2], out, activation, grad_pair[1]
    )
    grad = turn(add_up([grad, *grads_of[2]]).astype(LOW), "blk", 1)
    out = turn(add_up([out, *outs_of[2]]).astype(LOW), "blk", 1)
    down_terms = weight_terms((all_cot, [activation]))
    pair_b = weight_terms((hidden_mlp, [grad_pair[1]]))
    phase.end(grad, out, down_terms, pair_b)

    grad, grads_of[3], grads_of[0], far_down, far_b = phase.take(
        grad, grads_of[3], grads_of[0], down_terms[3], pair_b[3]
    )
    grads_of[3] = seq_reduce(grads_of[3])
    grad = turn(add_up([grad, *grads_of[3]]).astype(LOW), "blk", 1)
    far_down, far_b = swap(far_down, "slot", 1), swap(far_b, "slot", 2)
    grads_of[0] = seq_reduce(grads_of[0])
    phase.end(grad, grads_of[0])
    grad_part = add_up([grad, *grads_of[0]])
    grad_resid_part, gain_mlp_term = norm_back(normed_mlp, inverse_mlp, grad_part)
    grad_resid = own_cot.astype(WIDE) + grad_resid_part

    grad_q = [None] * blks

    def attend_back(ks, held):
        for some in calls(ks):
            held, grads = attend_back_blocks(
                some[0] // len(some), some, place, queries, key_rows, val_rows, attended, lse, cos_wide, sin_wide,
                full_attn, flat([blocks[k] for k in some]), held,
            )
            for k, grad in zip(some, grads):
                grad_q[k] = grad
        return held

    moving, out, outs_of[3], outs_of[0], half = phase.take(
        grad_resid.astype(LOW), out, outs_of[3], outs_of[0], grad_pair[0]
    )
    ahead = turn(moving, "blk", 1)
    pair_a = weight_terms((hidden_mlp, [half]))
    blocks = [seq_gather(moving), None, None, None]
    outs_of[3] = seq_reduce(outs_of[3])
    phase.end(ahead, blocks[0], outs_of[3], far_down, far_b, pair_a)

    moving, blocks[0], far_down, down_terms, out = phase.take(
        ahead, blocks[0], far_down, down_terms, add_up([out, *outs_of[3]]).astype(LOW)
    )
    ahead = turn(moving, "blk", 1)
    one = swap(add_up([down_terms[2], far_down]).astype(LOW), "slot", 2)
    two = swap(down_terms[1], "slot", 1)
    out = turn(out, "blk", 1)
    blocks[1] = seq_gather(moving)
    held = attend_back(in_order[0], None)
    phase.end(ahead, blocks[1], held, one, two)

    moving, far_a, down_terms, one, two = phase.take(ahead, pair_a[3], down_terms, one, two)
    ahead = turn(moving, "blk", 1)
    far_a = swap(far_a, "slot", 1)
    blocks[2] = seq_gather(moving)
    down_back = Exchange(row_pieces([down_terms[0], one, two]))
    relay_b = add_up([pair_b[1], far_b]).astype(LOW)
    phase.end(ahead, blocks[2], down_back.pieces, relay_b, out)

    moving, blocks[2], two_b, one_b, down_back.pieces = phase.take(ahead, blocks[2], pair_b[2], relay_b, down_back.pieces)
    blocks[3] = seq_gather(moving)
    two_b, one_b = swap(two_b, "slot", 2), swap(one_b, "slot", 1)
    down_back.send(1, 2)
    held = attend_back(in_order[1], held)
    all_resid, grad_k, grad_v = held
    phase.end(held, far_a, down_back.got)

    grad_qkv, terms, gain_terms = [None] * blks, [None] * blks, []

    def finish(ks, grad_k):
        for some in calls(ks, 1024):
            outs, gain_term, parts = finish_blocks(
                some, seqs, grad_q, grad_k, grad_v, cos_wide, sin_wide, full_attn, hidden_attn
            )
            gain_terms.append(gain_term)
            for k, out, part in zip(some, outs, parts):
                grad_qkv[k], terms[k] = out, part

    grad_k, down_back.pieces, outs_of[0] = phase.take(grad_k, down_back.pieces, outs_of[0])
    down_back.send(3)
    outs_of[0] = seq_reduce(outs_of[0])
    finish([*in_turn[0], *in_turn[1]], grad_k)
    phase.end(terms, one_b, two_b, gain_terms, down_back.got)

    terms[1] = seq_reduce(phase.take(terms[1]))
    phase.end(terms[1])

    moving, terms[2], terms[3], grad_qkv, gain_terms, far_a, near_a, middle_a, one_b, two_b = phase.take(
        add_up(terms[1]).astype(LOW), terms[2], terms[3], grad_qkv, gain_terms, far_a, pair_a[1], pair_a[2], one_b, two_b
    )
    moving = turn(moving, "blk", 1)
    one_a, two_a = swap(add_up([middle_a, far_a]).astype(LOW), "slot", 2), swap(near_a, "slot", 1)
    terms[2], terms[3] = seq_reduce(terms[2]), seq_reduce(terms[3])
    gain_terms = jnp.concatenate([add_up(gain_terms), jnp.sum(gain_mlp_term, axis=0, keepdims=True)], axis=0)
    bit = 1
    while bit < seqs:
        gain_terms = gain_terms + swap(gain_terms, "seq", bit)
        bit *= 2
    last_terms = weight_terms((hidden_attn, grad_qkv), (all_resid, attended))
    back_b = Exchange(row_pieces([pair_b[0], one_b, two_b]))
    phase.end(moving, terms[2], terms[3], last_terms, back_b.pieces, gain_terms)

    gain_parts = jnp.split(gain_terms, GROUPS, axis=1)
    moving, far, back_b.pieces, gain_far, gain_two = phase.take(
        add_up([moving, *terms[2]]).astype(LOW), last_terms[3], back_b.pieces, gain_parts[3], gain_parts[1]
    )
    moving = turn(moving, "blk", 1)
    far = swap(far, "slot", 2)
    back_b.send(1, 3)
    gain_far, gain_two = swap(gain_far, "slot", 1), swap(gain_two, "slot", 1)
    phase.end(moving, far, back_b.got, gain_far, gain_two, one_a, two_a)

    moving, relay, near_term, back_b.pieces, terms[0], one_a, two_a = phase.take(
        add_up([moving, *terms[3]]).astype(LOW), add_up([last_terms[1], far]).astype(LOW), last_terms[2],
        back_b.pieces, terms[0], one_a, two_a,
    )
    moving = turn(moving, "blk", 1)
    one, two = swap(relay, "slot", 1), swap(near_term, "slot", 2)
    back_b.send(2)
    back_a = Exchange(row_pieces([pair_a[0], one_a, two_a]))
    phase.end(moving, one, two, back_b.got, back_a.pieces)

    last_back = Exchange(row_pieces([last_terms[0], one, two]))
    gain_relay, last_back.pieces, back_a.pieces, terms[0] = phase.take(
        gain_parts[2] + gain_far, last_back.pieces, back_a.pieces, terms[0]
    )
    back_a.send(1, 2, 3)
    terms[0] = seq_reduce(terms[0])
    last_back.send(1, 2, 3)
    gain_one = swap(gain_relay, "slot", 2)
    gain_sum = after(gain_parts[0] + gain_two + gain_one, back_a.got[1])
    gain_sums = [gain_sum] + [turn(gain_sum, "blk", k) for k in range(1, blks)]

    layer_out = jnp.where(live_rows, resid + add_up([out, *outs_of[0]]), 0.0)
    grad_hidden_attn = add_up([moving, *terms[0]])
    normed_attn, inverse_attn = norm_rows(rows_f)
    grad_in_part, _ = norm_back(normed_attn, inverse_attn, grad_hidden_attn)
    shard = attn_gain.shape[0]
    gain_grads = lax.dynamic_slice(add_up(gain_sums), (0, blk_rank * shard), (2, shard))
    half = hidden // 2
    return (
        slot_order(layer_out).astype(LOW)[None],
        slot_order(grad_resid + grad_in_part)[None],
        gain_grads[0] / gain_attn[:, 0],
        join_owners([last_back], [(0, width)], gain_attn),
        join_owners([last_back], [(width, width)], gain_attn),
        join_owners([last_back], [(2 * width, width)], gain_attn),
        join_owners([last_back], [(3 * width, width)], 1.0),
        gain_grads[1] / gain_mlp[:, 0],
        join_owners([back_a, back_b], [(0, half)], gain_mlp),
        join_owners([back_a, back_b], [(half, half)], gain_mlp),
        join_owners([down_back], [(0, hidden)], 1.0),
    )


def solution(mesh):
    rows = P("slot", ("blk", "seq"), None)
    gain = P(("slot", "blk"))
    weight = P(("slot", "blk"), "seq")
    return jax.shard_map(
        shards,
        mesh=mesh,
        in_specs=(rows, rows, P("slot"), gain, weight, weight, weight, weight, gain, weight, weight, weight),
        out_specs=(rows, rows, gain, weight, weight, weight, weight, gain, weight, weight, weight),
        check_vma=False,
    )
```

```python
import math
from functools import partial

import jax
import jax.numpy as jnp
from jax import lax
from jax.experimental import pallas as pl
from jax.experimental.pallas import tpu as pltpu
from jax.sharding import PartitionSpec as P

HEADS = 32
HEAD_DIM = 64
HALF = HEAD_DIM // 2
EPSILON = 1e-05
ROPE_BASE = 130000.0
LOW = jnp.bfloat16
WIDE = jnp.float32
GROUPS = 4
ANY = pl.BlockSpec(memory_space=pl.ANY)


def turn(value, axis, by):
    count = lax.axis_size(axis)
    return lax.ppermute(value, axis, [(i, (i + by) % count) for i in range(count)])


def swap(value, axis, mask):
    count = lax.axis_size(axis)
    return lax.ppermute(value, axis, [(i, i ^ mask) for i in range(count)])


def after(value, *others):
    return lax.optimization_barrier((value, *others))[0]


def matmul(left, right):
    return jnp.dot(left, right, preferred_element_type=WIDE)


def over_rows(left, right):
    return lax.dot_general(left, right, (((0,), (0,)), ((), ())), preferred_element_type=WIDE)


def over_cols(left, right):
    return lax.dot_general(left, right, (((1,), (1,)), ((), ())), preferred_element_type=WIDE)


def slot_order(array):
    rank = lax.axis_index("slot")
    parts = jnp.split(array, GROUPS, axis=-1)
    for bit in (1, 2):
        flip = (rank & bit) != 0
        parts = [jnp.where(flip, parts[i ^ bit], parts[i]) for i in range(GROUPS)]
    return jnp.concatenate(parts, axis=-1)


def seq_gather(rows):
    count = lax.axis_size("seq")
    held = [rows]
    bit = 1
    while bit < count:
        held = held + [swap(part, "seq", bit) for part in held]
        bit *= 2
    return held


def seq_reduce(parts):
    bit = lax.axis_size("seq") // 2
    parts = [[part] for part in parts]
    while bit >= 1:
        kept = parts[:bit]
        for mine, other in zip(kept, parts[bit:]):
            mine.append(swap(add_up(other).astype(LOW), "seq", bit))
        parts = kept
        bit //= 2
    return parts[0]


def add_up(summands):
    total = summands[0]
    for summand in summands[1:]:
        total = total.astype(WIDE) + summand.astype(WIDE)
    return total


class Phases:
    def __init__(self):
        self.ended = ()

    def take(self, *values):
        values = tuple(values)
        if self.ended:
            values = lax.optimization_barrier((values, self.ended))[0]
        return values[0] if len(values) == 1 else values

    def end(self, *values):
        self.ended = values


class Exchange:
    def __init__(self, pieces):
        self.pieces = pieces
        self.got = {0: pieces[0]}

    def send(self, *steps):
        for k in steps:
            self.got[k] = turn(self.pieces[k], "blk", k)
        return [self.got[k] for k in steps]

    def by_rank(self, columns=slice(None)):
        blks, rank = lax.axis_size("blk"), lax.axis_index("blk")
        parts = [self.got[k][:, columns] for k in range(blks)]
        rows, cols = parts[0].shape
        full = jnp.zeros((blks * rows, cols), parts[0].dtype)
        for k in range(blks):
            full = lax.dynamic_update_slice(full, parts[k], ((rank - k) % blks * rows, 0))
        return full


def column_pieces(arrays, parts=1):
    blks, rank = lax.axis_size("blk"), lax.axis_index("blk")

    def cut(array, owner, part):
        width = array.shape[1] // (blks * parts)
        return lax.dynamic_slice(array, (0, (owner * parts + part) * width), (array.shape[0], width))

    return [
        jnp.concatenate([cut(a, (rank + k) % blks, part) for part in range(parts) for a in arrays], axis=1)
        for k in range(blks)
    ]


def row_pieces(summands):
    blks, rank = lax.axis_size("blk"), lax.axis_index("blk")
    rows = summands[0].shape[0] // blks

    def cut(owner):
        parts = [lax.dynamic_slice(s, (owner * rows, 0), (rows, s.shape[1])) for s in summands]
        return add_up(parts).astype(LOW)

    return [cut((rank + k) % blks) for k in range(blks)]


def join_owners(exchanges, cuts, scale):
    blks, rank = lax.axis_size("blk"), lax.axis_index("blk")
    wide = sum(width for _, width in cuts)
    out = jnp.zeros((exchanges[0].got[0].shape[0], blks * wide * len(exchanges)), WIDE)
    for n, exchanged in enumerate(exchanges):
        for k in range(blks):
            first = ((rank - k) % blks * len(exchanges) + n) * wide
            for at, width in cuts:
                part = exchanged.got[k][:, at : at + width].astype(WIDE) * scale
                out = lax.dynamic_update_slice(out, part, (0, first))
                first = first + width
    return out


def norm_rows(rows):
    inverse = lax.rsqrt(jnp.mean(rows * rows, axis=-1, keepdims=True) + EPSILON)
    return rows * inverse, inverse


def norm_back(normed, inverse, upstream):
    product = upstream * normed
    return inverse * (upstream - normed * jnp.mean(product, axis=-1, keepdims=True)), product


def vmem(shape):
    return pl.BlockSpec(shape, lambda *_: (0,) * len(shape))


def params(mebibytes):
    return pltpu.CompilerParams(vmem_limit_bytes=mebibytes << 20)


def cost():
    return pl.CostEstimate(flops=1, bytes_accessed=1, transcendentals=0)


def partner(vectors):
    width = vectors.shape[1]
    if width % 128 == 0:
        lanes = lax.broadcasted_iota(jnp.int32, (1, width), 1)
        ahead = pltpu.roll(vectors, width - HALF, 1)
        behind = pltpu.roll(vectors, HALF, 1)
        return jnp.where(lanes % HEAD_DIM < HALF, ahead, behind)
    parts = []
    for first in range(0, width, HEAD_DIM):
        parts += [vectors[:, first + HALF : first + HEAD_DIM], vectors[:, first : first + HALF]]
    return jnp.concatenate(parts, axis=1)


def table_kernel(dims, place_ref, cos_ref, sin_ref):
    total, blks, seqs, size = dims
    wide = cos_ref.shape[1]
    index = lax.broadcasted_iota(jnp.int32, (total, 1), 0)
    position = row_positions(index, place_ref[0], place_ref[1], blks, seqs, size).astype(WIDE)
    lane = lax.broadcasted_iota(jnp.int32, (1, wide), 1)
    power = (lane % HALF).astype(WIDE) * (-2.0 / HEAD_DIM)
    angle = position * jnp.exp(power * math.log(ROPE_BASE))
    cos_ref[...] = jnp.cos(angle)
    sin_ref[...] = jnp.where(lane % HEAD_DIM < HALF, -jnp.sin(angle), jnp.sin(angle))


def rotary_tables(place, total, size, wide):
    dims = (total, lax.axis_size("blk"), lax.axis_size("seq"), size)
    return pl.pallas_call(
        partial(table_kernel, dims),
        grid_spec=pltpu.PrefetchScalarGridSpec(
            num_scalar_prefetch=1, grid=(1,), in_specs=[], out_specs=[vmem((total, wide))] * 2
        ),
        out_shape=[jax.ShapeDtypeStruct((total, wide), WIDE)] * 2,
        compiler_params=params(32),
        cost_estimate=cost(),
        name="rotary_tables",
    )(place)


def widen(table, width):
    return table if table.shape[1] == width else jnp.concatenate([table] * (width // table.shape[1]), axis=1)


def qkv_kernel(width, *refs):
    parts, weights, (cos_ref, sin_ref) = refs[:-10], refs[-10:-6], refs[-6:-4]
    h_ref, q_ref, k_ref, v_ref = refs[-4:]
    size, model = parts[0].shape
    step = model // GROUPS
    for n, part in enumerate(parts):
        normed, _ = norm_rows(part[...].astype(WIDE))
        h_ref[n * size : (n + 1) * size, :] = normed.astype(LOW)
    total = h_ref.shape[0]
    rows = min(512, total)

    def some(first):
        here = slice(first, first + rows)
        pre = matmul(h_ref[here, :step], weights[0][:, : 3 * width])
        for i in range(1, GROUPS):
            pre += matmul(h_ref[here, i * step : (i + 1) * step], weights[i][:, : 3 * width])
        cos, sin = widen(cos_ref[here, :], width), widen(sin_ref[here, :], width)
        for at, out_ref in ((0, q_ref), (1, k_ref)):
            half = pre[:, at * width : (at + 1) * width]
            out_ref[here, :] = (half * cos + partner(half) * sin).astype(LOW)
        v_ref[here, :] = pre[:, 2 * width :].astype(LOW)

    for first in range(0, total, rows):
        some(first)


def project_qkv(parts, weights, cos, sin, width):
    size, model = parts[0].shape
    total = size * len(parts)
    return pl.pallas_call(
        partial(qkv_kernel, width),
        grid=(1,),
        in_specs=[vmem((size, model))] * len(parts) + [vmem(w.shape) for w in weights] + [vmem(cos.shape)] * 2,
        out_specs=[vmem((total, model))] + [vmem((total, width))] * 3,
        out_shape=[jax.ShapeDtypeStruct((total, model), LOW)] + [jax.ShapeDtypeStruct((total, width), LOW)] * 3,
        compiler_params=params(60),
        cost_estimate=cost(),
        name="project_qkv",
    )(*parts, *weights, cos, sin)


def row_positions(index, blk_rank, seq_rank, blks, seqs, size):
    sub = index // size
    k, m = sub // seqs, sub % seqs
    return ((blk_rank - k + blks) % blks * seqs + (seq_rank ^ m)) * size + index % size


def allowed_pairs(dims, place_ref, firsts, rows):
    total, blks, seqs, size = dims
    blk_rank, seq_rank, length = place_ref[0], place_ref[1], place_ref[2]
    k_index = lax.broadcasted_iota(jnp.int32, (1, total), 1)
    k_pos = row_positions(k_index, blk_rank, seq_rank, blks, seqs, size)
    k_pos = jnp.where(k_pos < length, k_pos, jnp.int32(1 << 30))
    index = lax.broadcasted_iota(jnp.int32, (rows, 1), 0)
    q_pos = [row_positions(first + index, blk_rank, seq_rank, blks, seqs, size) for first in firsts]
    return k_pos <= jnp.concatenate(q_pos, axis=0)


def tiles_of(count, block):
    if count * block <= 512:
        return [[(g, 0, block) for g in range(count)]]
    rows = min(256, block)
    return [[(g, first, rows)] for g in range(count) for first in range(0, block, rows)]


def rows_of(refs, tile):
    return jnp.concatenate([refs[g][first : first + rows, :] for g, first, rows in tile], axis=0)


def put_rows(refs, tile, value):
    at = 0
    for g, first, rows in tile:
        refs[g][first : first + rows, :] = value[at : at + rows]
        at += rows


def put_parts(terms, size, column, value):
    for n, term in enumerate(terms):
        term[:, column : column + value.shape[1]] = value[n * size : (n + 1) * size]


def by_block(terms, count):
    some = len(terms) // count
    return [terms[g * some : (g + 1) * some] for g in range(count)]


def attend_kernel(dims, ks, width, place_ref, *refs):
    count, seqs = len(ks), dims[2]
    q_refs, (k_ref, v_ref), weights = refs[:count], refs[count : count + 2], refs[count + 2 : count + 6]
    out_refs, lse_refs, terms = refs[count + 6 : 2 * count + 6], refs[2 * count + 6 : 3 * count + 6], refs[3 * count + 6 :]
    block = q_refs[0].shape[0]
    lanes = lax.broadcasted_iota(jnp.int32, (1, width), 1)
    lse_lanes = lax.broadcasted_iota(jnp.int32, (1, 128), 1)
    for tile in tiles_of(count, block):
        rows = tile[0][2]
        allowed = allowed_pairs(dims, place_ref, [ks[g] * block + first for g, first, _ in tile], rows)
        queries = rows_of(q_refs, tile).astype(WIDE) * HEAD_DIM**-0.5
        wide = rows * len(tile)

        def one_head(head, carried):
            out, lse = carried
            mine = lanes // HEAD_DIM == head
            picked = jnp.where(mine, queries, 0.0).astype(LOW)
            scores = jnp.where(allowed, over_cols(picked, k_ref[...]), -1e30)
            top = jnp.max(scores, axis=1, keepdims=True)
            probs = jnp.exp(scores - top)
            weight = jnp.sum(probs, axis=1, keepdims=True)
            mixed = matmul(probs.astype(LOW), v_ref[...]) / weight
            return jnp.where(mine, mixed, out), jnp.where(lse_lanes == head, top + jnp.log(weight), lse)

        out, lse = lax.fori_loop(
            0, width // HEAD_DIM, one_head, (jnp.zeros((wide, width), WIDE), jnp.zeros((wide, 128), WIDE))
        )
        put_rows(out_refs, tile, out.astype(LOW))
        put_rows(lse_refs, tile, lse)
    attended = jnp.concatenate([ref[...] for ref in out_refs], axis=0)
    for i, weight in enumerate(weights):
        step = weight.shape[0]
        put_parts(terms, block // seqs, i * step, over_cols(attended, weight[:, 3 * width :]).astype(LOW))


def attend_blocks(ks, place, queries, key_rows, val_rows, weights, size, model):
    total, width = queries.shape
    blks, seqs, count = lax.axis_size("blk"), lax.axis_size("seq"), len(ks)
    block = total // blks
    rows_at = lambda k, wide: pl.BlockSpec((block, wide), lambda *_: (k, 0))
    got = pl.pallas_call(
        partial(attend_kernel, (total, blks, seqs, size), ks, width),
        grid_spec=pltpu.PrefetchScalarGridSpec(
            num_scalar_prefetch=1,
            grid=(1,),
            in_specs=[rows_at(k, width) for k in ks] + [vmem((total, width))] * 2 + [vmem(w.shape) for w in weights],
            out_specs=[vmem((block, width))] * count + [vmem((block, 128))] * count + [vmem((size, model))] * (count * seqs),
        ),
        out_shape=[jax.ShapeDtypeStruct((block, width), LOW)] * count
        + [jax.ShapeDtypeStruct((block, 128), WIDE)] * count
        + [jax.ShapeDtypeStruct((size, model), LOW)] * (count * seqs),
        compiler_params=params(56),
        cost_estimate=cost(),
        name="attend_blocks",
    )(place, *[queries] * count, key_rows, val_rows, *weights)
    return got[:count], got[count : 2 * count], by_block(got[2 * count :], count)


def mlp_kernel(count, *refs):
    parts, pairs, down = refs[:count], (refs[count : count + 4], refs[count + 4 : count + 8]), refs[count + 8 : count + 13]
    outs = refs[-5 - 2 * count :]
    h_ref, c_ref, act_ref, pair_refs = outs[0], outs[1], outs[2], outs[3:5]
    grad_terms, out_terms = outs[5 : 5 + count], outs[5 + count :]
    size, model = parts[0].shape[0], h_ref.shape[1]
    step, hidden = model // GROUPS, down[0].shape[1] // 2
    groups = [slice(i * step, (i + 1) * step) for i in range(GROUPS)]
    for m in range(count):
        rows = slice(m * size, (m + 1) * size)
        h_ref[rows, :] = parts[m][:, :model]
        c_ref[rows, :] = parts[m][:, model:]
    down_half = lambda i, j: down[i][:, j * hidden : (j + 1) * hidden] if i < 3 else down[3 + j][...]
    for j, pair_ref in enumerate(pair_refs):
        half = slice(j * hidden, (j + 1) * hidden)
        both = matmul(h_ref[:, groups[0]], pairs[j][0][...])
        grad_act = matmul(c_ref[:, groups[0]], down_half(0, j))
        for i in range(1, GROUPS):
            both += matmul(h_ref[:, groups[i]], pairs[j][i][...])
            grad_act += matmul(c_ref[:, groups[i]], down_half(i, j))
        gate, up = both[:, :hidden], both[:, hidden:]
        sig = jax.nn.sigmoid(gate)
        act_ref[:, half] = (gate * sig * up).astype(LOW)
        pair_ref[:, :hidden] = (grad_act * up * sig * (1.0 + gate * (1.0 - sig))).astype(LOW)
        pair_ref[:, hidden:] = (grad_act * gate * sig).astype(LOW)
    for i in range(GROUPS):
        grad = over_cols(pair_refs[0][...], pairs[0][i][...]) + over_cols(pair_refs[1][...], pairs[1][i][...])
        put_parts(grad_terms, size, i * step, grad.astype(LOW))
        if i < 3:
            out = over_cols(act_ref[...], down[i][...])
        else:
            out = over_cols(act_ref[:, :hidden], down[3][...]) + over_cols(act_ref[:, hidden:], down[4][...])
        put_parts(out_terms, size, i * step, out.astype(LOW))


def mlp_blocks(at, seqs, parts, pairs, down, held, total):
    count, (size, model) = len(parts), (parts[0].shape[0], parts[0].shape[1] // 2)
    hidden = down[0].shape[1]
    rows = count * size
    old = [] if held is None else list(held)
    widths = [model, model, hidden, hidden, hidden]
    got = pl.pallas_call(
        partial(mlp_kernel, count),
        grid=(1,),
        in_specs=[vmem((size, 2 * model))] * count
        + [vmem(w.shape) for w in (*pairs[0], *pairs[1], *down)]
        + [ANY] * len(old),
        out_specs=[pl.BlockSpec((rows, wide), lambda _: (at, 0)) for wide in widths] + [vmem((size, model))] * (2 * count),
        out_shape=[jax.ShapeDtypeStruct((total, wide), LOW) for wide in widths]
        + [jax.ShapeDtypeStruct((size, model), LOW)] * (2 * count),
        input_output_aliases={count + 13 + i: i for i in range(5)} if old else {},
        compiler_params=params(60),
        cost_estimate=cost(),
        name="mlp_blocks",
    )(*parts, *pairs[0], *pairs[1], *down, *old)
    return got[:5], by_block(got[5 : 5 + count], count // seqs), by_block(got[5 + count :], count // seqs)


def attend_back_kernel(dims, ks, width, fresh, place_ref, *refs):
    count, seqs = len(ks), dims[2]

    def some(number):
        nonlocal refs
        taken, refs = refs[:number], refs[number:]
        return taken

    q_refs, (k_ref, v_ref), out_refs, lse_refs = some(count), some(2), some(count), some(count)
    cos_refs, sin_refs, weights, parts = some(count), some(count), some(4), some(count * seqs)
    old = [] if fresh else some(3)
    (r_ref, gk_ref, gv_ref), gq_refs, (cot_ref,) = some(3), some(count), some(1)
    block = q_refs[0].shape[0]
    size = block // seqs
    lanes = lax.broadcasted_iota(jnp.int32, (1, width), 1)
    lse_lanes = lax.broadcasted_iota(jnp.int32, (1, 128), 1)
    gk_ref[...] = jnp.zeros_like(gk_ref) if fresh else old[1][...]
    gv_ref[...] = jnp.zeros_like(gv_ref) if fresh else old[2][...]
    for n, part in enumerate(parts):
        r_ref[n * size : (n + 1) * size, :] = part[...]
    step = weights[0].shape[0]
    cot = matmul(r_ref[:, :step], weights[0][:, 3 * width :])
    for i in range(1, GROUPS):
        cot += matmul(r_ref[:, i * step : (i + 1) * step], weights[i][:, 3 * width :])
    cot_ref[...] = cot.astype(LOW).astype(WIDE)
    for tile in tiles_of(count, block):
        rows = tile[0][2]
        allowed = allowed_pairs(dims, place_ref, [ks[g] * block + first for g, first, _ in tile], rows)
        queries = rows_of(q_refs, tile).astype(WIDE) * HEAD_DIM**-0.5
        tile_cot = jnp.concatenate([cot_ref[g * block + first : g * block + first + n, :] for g, first, n in tile], axis=0)
        dots = tile_cot * rows_of(out_refs, tile).astype(WIDE)
        tile_lse = rows_of(lse_refs, tile)
        wide = rows * len(tile)

        def one_head(head, grad_q):
            mine = lanes // HEAD_DIM == head
            picked = jnp.where(mine, queries, 0.0).astype(LOW)
            cot_head = jnp.where(mine, tile_cot, 0.0).astype(LOW)
            row_dot = jnp.sum(jnp.where(mine, dots, 0.0), axis=1, keepdims=True)
            lse = jnp.sum(jnp.where(lse_lanes == head, tile_lse, 0.0), axis=1, keepdims=True)
            scores = jnp.where(allowed, over_cols(picked, k_ref[...]), -1e30)
            probs = jnp.exp(scores - lse)
            gv_ref[...] += over_rows(probs.astype(LOW), cot_head)
            grad_probs = over_cols(cot_head, v_ref[...])
            grad_scores = (probs * (grad_probs - row_dot)).astype(LOW)
            gk_ref[...] += over_rows(grad_scores, picked)
            return jnp.where(mine, matmul(grad_scores, k_ref[...]) * HEAD_DIM**-0.5, grad_q)

        grad_q = lax.fori_loop(0, width // HEAD_DIM, one_head, jnp.zeros((wide, width), WIDE))
        low = grad_q.astype(LOW).astype(WIDE)
        cos, sin = widen(rows_of(cos_refs, tile), width), widen(rows_of(sin_refs, tile), width)
        put_rows(gq_refs, tile, (low * cos - partner(low) * sin).astype(LOW))


def attend_back_blocks(at, ks, place, queries, key_rows, val_rows, attended, lse, cos, sin, weights, parts, held):
    total, width = queries.shape
    blks, seqs, count = lax.axis_size("blk"), lax.axis_size("seq"), len(ks)
    size, model = parts[0].shape
    block = total // blks
    rows_at = lambda k, wide: pl.BlockSpec((block, wide), lambda *_: (k, 0))
    whole = vmem((total, width))
    old = [] if held is None else list(held)
    first_old = 1 + count + 2 + 2 * count + 2 * count + 4 + count * seqs
    tables = [rows_at(k, cos.shape[1]) for k in ks]
    got = pl.pallas_call(
        partial(attend_back_kernel, (total, blks, seqs, size), ks, width, held is None),
        grid_spec=pltpu.PrefetchScalarGridSpec(
            num_scalar_prefetch=1,
            grid=(1,),
            in_specs=[rows_at(k, width) for k in ks]
            + [whole] * 2
            + [vmem((block, width))] * count
            + [vmem((block, 128))] * count
            + tables * 2
            + [vmem(w.shape) for w in weights]
            + [vmem((size, model))] * (count * seqs)
            + ([ANY, whole, whole] if old else []),
            out_specs=[pl.BlockSpec((count * block, model), lambda *_: (at, 0)), whole, whole] + [vmem((block, width))] * count,
            scratch_shapes=[pltpu.VMEM((count * block, width), WIDE)],
        ),
        out_shape=[jax.ShapeDtypeStruct((total, model), LOW)]
        + [jax.ShapeDtypeStruct((total, width), WIDE)] * 2
        + [jax.ShapeDtypeStruct((block, width), LOW)] * count,
        input_output_aliases={first_old + i: i for i in range(3)} if old else {},
        compiler_params=params(60),
        cost_estimate=cost(),
        name="attend_back_blocks",
    )(
        place, *[queries] * count, key_rows, val_rows, *[attended[k] for k in ks], *[lse[k] for k in ks],
        *[cos] * count, *[sin] * count, *weights, *parts, *old,
    )
    return got[:3], got[3:]


def finish_kernel(width, count, seqs, *refs):
    def some(number):
        nonlocal refs
        taken, refs = refs[:number], refs[number:]
        return taken

    gq_refs, gk_refs, gv_refs, cos_refs, sin_refs = (some(count) for _ in range(5))
    weights, normed = some(4), some(count)
    outs, (gain_ref,), terms = some(count), some(1), some(count * seqs)
    size = terms[0].shape[0]
    step = weights[0].shape[0]
    for g, out_ref in enumerate(outs):
        low_k = gk_refs[g][...].astype(LOW).astype(WIDE)
        cos, sin = widen(cos_refs[g][...], width), widen(sin_refs[g][...], width)
        out_ref[:, :width] = gq_refs[g][...]
        out_ref[:, width : 2 * width] = (low_k * cos - partner(low_k) * sin).astype(LOW)
        out_ref[:, 2 * width :] = gv_refs[g][...].astype(LOW)
    grads = jnp.concatenate([ref[...] for ref in outs], axis=0)
    for i in range(GROUPS):
        here = slice(i * step, (i + 1) * step)
        grad = over_cols(grads, weights[i][:, : 3 * width])
        put_parts(terms, size, i * step, grad.astype(LOW))
        rows = jnp.concatenate([ref[:, here] for ref in normed], axis=0).astype(WIDE)
        gain_ref[:, here] = jnp.sum(grad * rows, axis=0, keepdims=True)


def finish_blocks(ks, seqs, grad_q, grad_k, grad_v, cos, sin, weights, normed):
    count = len(ks)
    total, width = grad_k.shape
    model = normed.shape[1]
    block = total // lax.axis_size("blk")
    size = block // seqs
    rows_at = lambda k, wide: pl.BlockSpec((block, wide), lambda _: (k, 0))
    tables = [rows_at(k, cos.shape[1]) for k in ks]
    got = pl.pallas_call(
        partial(finish_kernel, width, count, seqs),
        grid=(1,),
        in_specs=[vmem((block, width))] * count
        + [rows_at(k, width) for k in ks] * 2
        + tables * 2
        + [vmem(w.shape) for w in weights]
        + [rows_at(k, model) for k in ks],
        out_specs=[vmem((block, 3 * width))] * count + [vmem((1, model))] + [vmem((size, model))] * (count * seqs),
        out_shape=[jax.ShapeDtypeStruct((block, 3 * width), LOW)] * count
        + [jax.ShapeDtypeStruct((1, model), WIDE)]
        + [jax.ShapeDtypeStruct((size, model), LOW)] * (count * seqs),
        compiler_params=params(56),
        cost_estimate=cost(),
        name="finish_blocks",
    )(*[grad_q[k] for k in ks], *[grad_k] * count, *[grad_v] * count, *[cos] * count, *[sin] * count, *weights, *[normed] * count)
    return got[:count], got[count], by_block(got[count + 1 :], count)


def weight_kernel(counts, *refs):
    outs = refs[-GROUPS:]
    step = outs[0].shape[0]
    for i, out_ref in enumerate(outs):
        at, column = 0, 0
        for count in counts:
            left_ref, rights = refs[at], refs[at + 1 : at + 1 + count]
            rows, wide = rights[0].shape
            here = slice(i * step, (i + 1) * step)
            total = over_rows(left_ref[:rows, here], rights[0][...])
            for g in range(1, count):
                total += over_rows(left_ref[g * rows : (g + 1) * rows, here], rights[g][...])
            out_ref[:, column : column + wide] = total.astype(LOW)
            at, column = at + 1 + count, column + wide


def weight_terms(*pairs):
    step = pairs[0][0].shape[1] // GROUPS
    cols = sum(rights[0].shape[1] for _, rights in pairs)
    arrays = [a for left, rights in pairs for a in (left, *rights)]
    return pl.pallas_call(
        partial(weight_kernel, [len(rights) for _, rights in pairs]),
        grid=(1,),
        in_specs=[vmem(a.shape) for a in arrays],
        out_specs=[vmem((step, cols))] * GROUPS,
        out_shape=[jax.ShapeDtypeStruct((step, cols), LOW)] * GROUPS,
        compiler_params=params(60),
        cost_estimate=cost(),
        name="weight_terms",
    )(*arrays)


def shards(
    tokens, out_grad, lengths, attn_gain, w_query, w_key, w_value, output_weight, mlp_gain, gate_weight, up_weight, down_weight
):
    seqs, blks = lax.axis_size("seq"), lax.axis_size("blk")
    seq_rank, blk_rank = lax.axis_index("seq"), lax.axis_index("blk")
    size, model = tokens.shape[1], tokens.shape[2]
    block = size * seqs
    total = block * blks
    length = lengths[0]
    width = w_query.shape[1] // blks
    hidden = gate_weight.shape[1] // blks
    positions = (blk_rank * seqs + seq_rank) * size + jnp.arange(size, dtype=jnp.int32)
    live_rows = (positions < length)[:, None]
    place = jnp.stack([blk_rank, seq_rank, length, lax.axis_index("slot")]).astype(jnp.int32)

    cos_wide, sin_wide = rotary_tables(place, total, size, min(width, 128))
    own_tokens = slot_order(tokens[0])
    own_cot = jnp.where(live_rows, slot_order(out_grad[0]), 0)
    gain_attn, gain_mlp = attn_gain.astype(WIDE)[:, None], mlp_gain.astype(WIDE)[:, None]
    rows_f = own_tokens.astype(WIDE)

    def scaled(weight, gain):
        return (weight.astype(WIDE) * gain).astype(LOW)

    attn_out = Exchange(
        column_pieces([scaled(w, gain_attn) for w in (w_query, w_key, w_value)] + [output_weight])
    )
    pair_out = Exchange(column_pieces([scaled(gate_weight, gain_mlp), scaled(up_weight, gain_mlp)], 2))
    down_out = Exchange(column_pieces([down_weight]))
    phase = Phases()
    flat = lambda lists: [item for items in lists for item in items]
    in_order, in_turn = [[0, 1], [2, 3]], [[1, 2], [3, 0]]

    def calls(ks, most=512):
        return [ks] if block * len(ks) <= most else [[k] for k in ks]

    token_blocks = [None] * blks
    attn_out.send(1, 2, 3)
    token_blocks[0] = seq_gather(own_tokens)
    phase.end(attn_out.got, token_blocks[0])

    part_attn, moving = phase.take(attn_out.by_rank(), own_tokens)
    second = turn(moving, "blk", 1)
    ahead = turn(second, "blk", 1)
    near_x, near_y = swap(part_attn, "slot", 1), swap(part_attn, "slot", 2)
    phase.end(second, ahead, near_x, near_y, pair_out.pieces, down_out.pieces, cos_wide, sin_wide)

    second, moving, near_x, pair_out.pieces = phase.take(second, ahead, near_x, pair_out.pieces)
    ahead = turn(moving, "blk", 1)
    far = swap(near_x, "slot", 2)
    pair_out.send(1)
    token_blocks[1], token_blocks[2] = seq_gather(second), seq_gather(moving)
    full_attn = [part_attn, near_x, near_y, far]
    phase.end(ahead, far, token_blocks[1:3], pair_out.got)

    moving, pair_out.pieces = phase.take(ahead, pair_out.pieces)
    token_blocks[3] = seq_gather(moving)
    pair_out.send(2, 3)
    got = []
    for ks in [list(range(blks))] if total <= 1024 else [[k] for k in range(blks)]:
        here = slice(ks[0] * block, (ks[-1] + 1) * block)
        got.append(project_qkv(flat([token_blocks[k] for k in ks]), full_attn, cos_wide[here], sin_wide[here], width))
    hidden_attn, queries, key_rows, val_rows = (
        parts[0] if len(parts) == 1 else jnp.concatenate(parts, axis=0) for parts in zip(*got)
    )
    attended, lse, terms = [None] * blks, [None] * blks, [None] * blks

    def attend(ks, queries):
        for some in calls(ks):
            for k, *got in zip(some, *attend_blocks(some, place, queries, key_rows, val_rows, full_attn, size, model)):
                attended[k], lse[k], terms[k] = got

    attend(in_turn[0], queries)
    phase.end(pair_out.got, terms[1], terms[2])

    queries, pair_out.got, down_out.pieces, terms[1], terms[2] = phase.take(
        queries, pair_out.got, down_out.pieces, terms[1], terms[2]
    )
    half_a = pair_out.by_rank(slice(0, hidden))
    near_x, near_y = [swap(half_a, "slot", 1)], [swap(half_a, "slot", 2)]
    terms[1] = seq_reduce(terms[1])
    moving = turn(add_up(terms[1]).astype(LOW), "blk", 1)
    down_out.send(1)
    terms[2] = seq_reduce(terms[2])
    attend(in_turn[1], queries)
    phase.end(moving, terms, near_x, near_y, down_out.got)

    half_b = pair_out.by_rank(slice(hidden, None))
    moving, half_b, down_out.pieces, terms[3], terms[0] = phase.take(
        add_up([moving, *terms[2]]).astype(LOW), half_b, down_out.pieces, terms[3], terms[0]
    )
    near_x, near_y = near_x + [swap(half_b, "slot", 1)], near_y + [swap(half_b, "slot", 2)]
    moving = turn(moving, "blk", 1)
    down_out.send(2)
    terms[3] = seq_reduce(terms[3])
    phase.end(moving, terms[3], near_x, near_y, down_out.got)

    moving, far_x, far_y, down_out.pieces, terms[0] = phase.take(
        add_up([moving, *terms[3]]).astype(LOW), near_x[0], near_y[1], down_out.pieces, terms[0]
    )
    moving = turn(moving, "blk", 1)
    down_out.send(3)
    far_a, far_b = swap(far_x, "slot", 2), swap(far_y, "slot", 1)
    terms[0] = seq_reduce(terms[0])
    full_pair = [[half_a, near_x[0], near_y[0], far_a], [half_b, near_x[1], near_y[1], far_b]]
    phase.end(moving, terms[0], down_out.got)
    resid = rows_f + add_up([moving, *terms[0]])
    normed_mlp, inverse_mlp = norm_rows(resid)

    grads_of, outs_of = [None] * blks, [None] * blks

    def feed(ks, held):
        for some in calls(ks):
            held, grads, outs = mlp_blocks(
                some[0] // len(some), seqs, flat([blocks[k] for k in some]), full_pair, full_down, held, total
            )
            for k, grad, out in zip(some, grads, outs):
                grads_of[k], outs_of[k] = grad, out
        return held

    blocks = [None] * blks
    moving, part_down = phase.take(
        jnp.concatenate([normed_mlp.astype(LOW), own_cot], axis=1), down_out.by_rank()
    )
    ahead = turn(moving, "blk", 1)
    near_x, near_y = swap(part_down, "slot", 1), swap(part_down, "slot", 2)
    blocks[0] = seq_gather(moving)
    phase.end(ahead, far_a, far_b, blocks[0])

    moving = phase.take(ahead)
    ahead = turn(moving, "blk", 1)
    cut = hidden // 2
    full_down = [part_down, near_x, near_y, swap(near_x[:, :cut], "slot", 2), swap(near_y[:, cut:], "slot", 1)]
    blocks[1] = seq_gather(moving)
    phase.end(ahead, blocks[1], full_down)

    moving, blocks[0], blocks[1] = phase.take(ahead, blocks[0], blocks[1])
    ahead = turn(moving, "blk", 1)
    blocks[2] = seq_gather(moving)
    held = feed(in_order[0], None)
    grads_of[1], outs_of[1] = seq_reduce(grads_of[1]), seq_reduce(outs_of[1])
    phase.end(ahead, blocks[2], held, grads_of[1], outs_of[1])

    moving, blocks[2], grads_of[:2], outs_of[:2] = phase.take(ahead, blocks[2], grads_of[:2], outs_of[:2])
    blocks[3] = seq_gather(moving)
    grad = turn(add_up(grads_of[1]).astype(LOW), "blk", 1)
    out = turn(add_up(outs_of[1]).astype(LOW), "blk", 1)
    held = feed(in_order[1], held)
    grads_of[2], outs_of[2] = seq_reduce(grads_of[2]), seq_reduce(outs_of[2])
    phase.end(grad, out, held, grads_of[2], outs_of[2])
    hidden_mlp, all_cot, activation, *grad_pair = held

    grad, grads_of[2], outs_of[2], out, activation, grad_pair[1] = phase.take(
        grad, grads_of[2], outs_of[2], out, activation, grad_pair[1]
    )
    grad = turn(add_up([grad, *grads_of[2]]).astype(LOW), "blk", 1)
    out = turn(add_up([out, *outs_of[2]]).astype(LOW), "blk", 1)
    down_terms = weight_terms((all_cot, [activation]))
    pair_b = weight_terms((hidden_mlp, [grad_pair[1]]))
    phase.end(grad, out, down_terms, pair_b)

    grad, grads_of[3], grads_of[0], far_down, far_b = phase.take(
        grad, grads_of[3], grads_of[0], down_terms[3], pair_b[3]
    )
    grads_of[3] = seq_reduce(grads_of[3])
    grad = turn(add_up([grad, *grads_of[3]]).astype(LOW), "blk", 1)
    far_down, far_b = swap(far_down, "slot", 1), swap(far_b, "slot", 2)
    grads_of[0] = seq_reduce(grads_of[0])
    phase.end(grad, grads_of[0])
    grad_part = add_up([grad, *grads_of[0]])
    grad_resid_part, gain_mlp_term = norm_back(normed_mlp, inverse_mlp, grad_part)
    grad_resid = own_cot.astype(WIDE) + grad_resid_part

    grad_q = [None] * blks

    def attend_back(ks, held):
        for some in calls(ks):
            held, grads = attend_back_blocks(
                some[0] // len(some), some, place, queries, key_rows, val_rows, attended, lse, cos_wide, sin_wide,
                full_attn, flat([blocks[k] for k in some]), held,
            )
            for k, grad in zip(some, grads):
                grad_q[k] = grad
        return held

    moving, out, outs_of[3], outs_of[0], half = phase.take(
        grad_resid.astype(LOW), out, outs_of[3], outs_of[0], grad_pair[0]
    )
    ahead = turn(moving, "blk", 1)
    pair_a = weight_terms((hidden_mlp, [half]))
    blocks = [seq_gather(moving), None, None, None]
    outs_of[3] = seq_reduce(outs_of[3])
    phase.end(ahead, blocks[0], outs_of[3], far_down, far_b, pair_a)

    moving, blocks[0], far_down, down_terms, out = phase.take(
        ahead, blocks[0], far_down, down_terms, add_up([out, *outs_of[3]]).astype(LOW)
    )
    ahead = turn(moving, "blk", 1)
    one = swap(add_up([down_terms[2], far_down]).astype(LOW), "slot", 2)
    two = swap(down_terms[1], "slot", 1)
    out = turn(out, "blk", 1)
    blocks[1] = seq_gather(moving)
    held = attend_back(in_order[0], None)
    phase.end(ahead, blocks[1], held, one, two)

    moving, far_a, down_terms, one, two = phase.take(ahead, pair_a[3], down_terms, one, two)
    ahead = turn(moving, "blk", 1)
    far_a = swap(far_a, "slot", 1)
    blocks[2] = seq_gather(moving)
    down_back = Exchange(row_pieces([down_terms[0], one, two]))
    relay_b = add_up([pair_b[1], far_b]).astype(LOW)
    phase.end(ahead, blocks[2], down_back.pieces, relay_b, out)

    moving, blocks[2], two_b, one_b, down_back.pieces = phase.take(ahead, blocks[2], pair_b[2], relay_b, down_back.pieces)
    blocks[3] = seq_gather(moving)
    two_b, one_b = swap(two_b, "slot", 2), swap(one_b, "slot", 1)
    down_back.send(1, 2)
    held = attend_back(in_order[1], held)
    all_resid, grad_k, grad_v = held
    phase.end(held, far_a, down_back.got)

    grad_qkv, terms, gain_terms = [None] * blks, [None] * blks, []

    def finish(ks, grad_k):
        for some in calls(ks, 1024):
            outs, gain_term, parts = finish_blocks(
                some, seqs, grad_q, grad_k, grad_v, cos_wide, sin_wide, full_attn, hidden_attn
            )
            gain_terms.append(gain_term)
            for k, out, part in zip(some, outs, parts):
                grad_qkv[k], terms[k] = out, part

    grad_k, down_back.pieces, outs_of[0] = phase.take(grad_k, down_back.pieces, outs_of[0])
    down_back.send(3)
    outs_of[0] = seq_reduce(outs_of[0])
    finish([*in_turn[0], *in_turn[1]], grad_k)
    phase.end(terms, one_b, two_b, gain_terms, down_back.got)

    terms[1] = seq_reduce(phase.take(terms[1]))
    phase.end(terms[1])

    moving, terms[2], terms[3], grad_qkv, gain_terms, far_a, near_a, middle_a, one_b, two_b = phase.take(
        add_up(terms[1]).astype(LOW), terms[2], terms[3], grad_qkv, gain_terms, far_a, pair_a[1], pair_a[2], one_b, two_b
    )
    moving = turn(moving, "blk", 1)
    one_a, two_a = swap(add_up([middle_a, far_a]).astype(LOW), "slot", 2), swap(near_a, "slot", 1)
    terms[2], terms[3] = seq_reduce(terms[2]), seq_reduce(terms[3])
    gain_terms = jnp.concatenate([add_up(gain_terms), jnp.sum(gain_mlp_term, axis=0, keepdims=True)], axis=0)
    bit = 1
    while bit < seqs:
        gain_terms = gain_terms + swap(gain_terms, "seq", bit)
        bit *= 2
    last_terms = weight_terms((hidden_attn, grad_qkv), (all_resid, attended))
    back_b = Exchange(row_pieces([pair_b[0], one_b, two_b]))
    phase.end(moving, terms[2], terms[3], last_terms, back_b.pieces, gain_terms)

    gain_parts = jnp.split(gain_terms, GROUPS, axis=1)
    moving, far, back_b.pieces, gain_far, gain_two = phase.take(
        add_up([moving, *terms[2]]).astype(LOW), last_terms[3], back_b.pieces, gain_parts[3], gain_parts[1]
    )
    moving = turn(moving, "blk", 1)
    far = swap(far, "slot", 2)
    back_b.send(1, 3)
    gain_far, gain_two = swap(gain_far, "slot", 1), swap(gain_two, "slot", 1)
    phase.end(moving, far, back_b.got, gain_far, gain_two, one_a, two_a)

    moving, relay, near_term, back_b.pieces, terms[0], one_a, two_a = phase.take(
        add_up([moving, *terms[3]]).astype(LOW), add_up([last_terms[1], far]).astype(LOW), last_terms[2],
        back_b.pieces, terms[0], one_a, two_a,
    )
    moving = turn(moving, "blk", 1)
    one, two = swap(relay, "slot", 1), swap(near_term, "slot", 2)
    back_b.send(2)
    back_a = Exchange(row_pieces([pair_a[0], one_a, two_a]))
    phase.end(moving, one, two, back_b.got, back_a.pieces)

    last_back = Exchange(row_pieces([last_terms[0], one, two]))
    gain_relay, last_back.pieces, back_a.pieces, terms[0] = phase.take(
        gain_parts[2] + gain_far, last_back.pieces, back_a.pieces, terms[0]
    )
    back_a.send(1, 2, 3)
    terms[0] = seq_reduce(terms[0])
    last_back.send(1, 2, 3)
    gain_one = swap(gain_relay, "slot", 2)
    gain_sum = after(gain_parts[0] + gain_two + gain_one, back_a.got[1])
    gain_sums = [gain_sum] + [turn(gain_sum, "blk", k) for k in range(1, blks)]

    layer_out = jnp.where(live_rows, resid + add_up([out, *outs_of[0]]), 0.0)
    grad_hidden_attn = add_up([moving, *terms[0]])
    normed_attn, inverse_attn = norm_rows(rows_f)
    grad_in_part, _ = norm_back(normed_attn, inverse_attn, grad_hidden_attn)
    shard = attn_gain.shape[0]
    gain_grads = lax.dynamic_slice(add_up(gain_sums), (0, blk_rank * shard), (2, shard))
    half = hidden // 2
    return (
        slot_order(layer_out).astype(LOW)[None],
        slot_order(grad_resid + grad_in_part)[None],
        gain_grads[0] / gain_attn[:, 0],
        join_owners([last_back], [(0, width)], gain_attn),
        join_owners([last_back], [(width, width)], gain_attn),
        join_owners([last_back], [(2 * width, width)], gain_attn),
        join_owners([last_back], [(3 * width, width)], 1.0),
        gain_grads[1] / gain_mlp[:, 0],
        join_owners([back_a, back_b], [(0, half)], gain_mlp),
        join_owners([back_a, back_b], [(half, half)], gain_mlp),
        join_owners([down_back], [(0, hidden)], 1.0),
    )


def solution(mesh):
    rows = P("slot", ("blk", "seq"), None)
    gain = P(("slot", "blk"))
    weight = P(("slot", "blk"), "seq")
    return jax.shard_map(
        shards,
        mesh=mesh,
        in_specs=(rows, rows, P("slot"), gain, weight, weight, weight, weight, gain, weight, weight, weight),
        out_specs=(rows, rows, gain, weight, weight, weight, weight, gain, weight, weight, weight),
        check_vma=False,
    )
```
